32 devices in a mesh: seq: 2 (over core), node: 4 (over y, x), group: 4 (over z).
Axes of the slice: x: 2, y: 2, z: 4, core: 2. Of those that a mesh axis runs over, the one named last changes fastest.
Arguments:
- patch_tokens: bfloat16 [64, 196, 384], P(('node', 'group'), 'seq'), may hold values from -6 to 6
- special_tokens: bfloat16 [64, 2, 384], P(('node', 'group')), may hold values from -6 to 6
- patch_upstream: bfloat16 [64, 196, 384], P(('node', 'group'), 'seq'), may hold values from -6 to 6
- special_upstream: bfloat16 [64, 2, 384], P(('node', 'group')), may hold values from -6 to 6
- patch_rank: int32 [64, 196], P(('node', 'group'), 'seq'), may hold values from 0 to 195, each once within a row
- keep_count: int32 [64], P(('node', 'group')), may hold values from 40 to 196
- project_in: float32 [384, 1152], replicated, may hold values from -0.3125 to 0.3125
- project_out: float32 [384, 384], replicated, may hold values from -1.25 to 1.25
- expand_weight: float32 [384, 1536], replicated, may hold values from -0.3125 to 0.3125
- reduce_weight: float32 [1536, 384], replicated, may hold values from -0.15625 to 0.15625
- small_params: float32 [12, 384], replicated
- project_in_momentum: float32 [384, 1152], replicated, may hold values from -0.75 to 0.75
- project_out_momentum: float32 [384, 384], replicated, may hold values from -0.75 to 0.75
- expand_momentum: float32 [384, 1536], replicated, may hold values from -0.75 to 0.75
- reduce_momentum: float32 [1536, 384], replicated, may hold values from -0.75 to 0.75
- small_momentum: float32 [12, 384], replicated, may hold values from -4 to 4
- project_in_error: float32 [32, 384, 1152], P(('seq', 'node', 'group')), may hold values from -96 to 96
- project_out_error: float32 [32, 384, 384], P(('seq', 'node', 'group')), may hold values from -96 to 96
- expand_error: float32 [32, 384, 1536], P(('seq', 'node', 'group')), may hold values from -96 to 96
- reduce_error: float32 [32, 1536, 384], P(('seq', 'node', 'group')), may hold values from -96 to 96
- project_in_factor: float32 [1152, 8], replicated, may hold values from -6 to 6
- project_out_factor: float32 [384, 8], replicated, may hold values from -6 to 6
- expand_factor: float32 [1536, 8], replicated, may hold values from -6 to 6
- reduce_factor: float32 [384, 8], replicated, may hold values from -6 to 6
Outputs:
- patch_output: bfloat16 [64, 196, 384], P(('node', 'group'), 'seq')
- special_output: bfloat16 [64, 2, 384], P(('node', 'group'))
- patch_grad: bfloat16 [64, 196, 384], P(('node', 'group'), 'seq')
- special_grad: bfloat16 [64, 2, 384], P(('node', 'group'))
- new_project_in: float32 [384, 1152], replicated
- new_project_out: float32 [384, 384], replicated
- new_expand: float32 [384, 1536], replicated
- new_reduce: float32 [1536, 384], replicated
- new_small: float32 [12, 384], replicated
- new_project_in_momentum: float32 [384, 1152], replicated
- new_project_out_momentum: float32 [384, 384], replicated
- new_expand_momentum: float32 [384, 1536], replicated
- new_reduce_momentum: float32 [1536, 384], replicated
- new_small_momentum: float32 [12, 384], replicated
- new_project_in_error: float32 [32, 384, 1152], P(('seq', 'node', 'group'))
- new_project_out_error: float32 [32, 384, 384], P(('seq', 'node', 'group'))
- new_expand_error: float32 [32, 384, 1536], P(('seq', 'node', 'group'))
- new_reduce_error: float32 [32, 1536, 384], P(('seq', 'node', 'group'))
- new_project_in_factor: float32 [1152, 8], replicated
- new_project_out_factor: float32 [384, 8], replicated
- new_expand_factor: float32 [1536, 8], replicated
- new_reduce_factor: float32 [384, 8], replicated
The draws below stay inside these ranges and needn't reach their ends.
Inputs may be any that keep to these rules, and one draw needn't show every extreme that they name: `patch_rank`: the ranks of an image's patches are each of 0 to 195 once.
All inputs are finite; a program needn't handle non-finite values.
Results may differ from the reference program's by a relative error of at most 0.018.
Values may be sent and summed in bfloat16 or wider, within the bound.
A program may use at most 128 MiB of HBM per device.

```python
import math
import jax
import jax.numpy as jnp
from jax import lax

D = 384
HEADS = 6
HEAD_DIM = 64
FF = 1536
PATCHES = 196
RANK = 8
LEAST_KEEP = 40
IMG_DEV = 4
IMAGES = 64
REPLICAS = 16
WORKERS = 32
N_SEQ = 2


def draw_keep_count(key, part):
    drop_range = PATCHES - LEAST_KEEP
    first_key, second_key = jax.random.split(key)
    left_draw = jax.random.randint(first_key, (IMAGES,), 0, drop_range + 1)
    right_draw = jax.random.randint(second_key, (IMAGES,), 0, drop_range + 1)
    dropped = left_draw * right_draw // max(drop_range, 1)
    counts = PATCHES - dropped
    image_ids = jnp.arange(IMAGES)
    counts = jnp.where(image_ids == 0, PATCHES, counts)
    counts = jnp.where(image_ids == 1, LEAST_KEEP, counts)
    return counts.astype(jnp.int32)


def draw_small_params(key, part):
    first_key, second_key = jax.random.split(key)
    row_total = 8 + FF // D
    noise = jax.random.normal(first_key, (row_total, D), jnp.float32)
    gains = jax.random.uniform(second_key, (row_total, D), jnp.float32, 0.6, 1.4)
    row_ids = jnp.arange(row_total)[:, None]
    is_gain = (row_ids == 0) | (row_ids == 5)
    return jnp.where(is_gain, gains, 0.3 * noise).astype(jnp.float32)


def level_of(key, extent, shards, low, top_value):
    loudness = 1.0
    for axis_at, blocks in shards:
        heights = jax.random.uniform(jax.random.fold_in(jax.random.fold_in(key, 6), axis_at), (blocks,), jnp.float32, low / len(shards), top_value / len(shards))
        loudness = loudness * jnp.repeat(jnp.exp(heights), extent[axis_at] // blocks).reshape((-1,) + (1,) * (len(extent) - 1 - axis_at))
    return loudness


def centred(stream_key, shape, scale, most, cuts=(), kind=jnp.bfloat16):
    loudness = level_of(stream_key, shape, cuts, -0.22, 0.18) if cuts else 1.0
    entries = jax.random.normal(stream_key, shape, jnp.float32) * scale * loudness
    return jnp.minimum(jnp.maximum(entries, -most), most).astype(kind)


def setup_inputs(seed: int = 0) -> dict:
    key_of = jax.random.split(jax.random.key(seed), 25)
    return {
        "patch_tokens": centred(key_of[0], (IMAGES, PATCHES, D), 1.0, 6.0, ((0, 16), (1, 2))),
        "special_tokens": centred(key_of[1], (IMAGES, 2, D), 1.0, 6.0, ((0, 16),)),
        "patch_upstream": centred(key_of[2], (IMAGES, PATCHES, D), 1.0, 6.0, ((0, 16), (1, 2))),
        "special_upstream": centred(key_of[3], (IMAGES, 2, D), 1.0, 6.0, ((0, 16),)),
        "patch_rank": jax.vmap(lambda own: jax.random.permutation(own, PATCHES))(jax.random.split(key_of[4], IMAGES)).reshape((IMAGES, PATCHES)).astype(jnp.int32),
        "keep_count": draw_keep_count(jax.random.fold_in(key_of[24], 71), 0),
        "project_in": centred(key_of[6], (D, 3 * D), D ** -0.5, 0.3125, (), jnp.float32),
        "project_out": centred(key_of[7], (D, D), (D // 16) ** -0.5, 1.25, (), jnp.float32),
        "expand_weight": centred(key_of[8], (D, FF), D ** -0.5, 0.3125, (), jnp.float32),
        "reduce_weight": centred(key_of[9], (FF, D), FF ** -0.5, 0.15625, (), jnp.float32),
        "small_params": draw_small_params(jax.random.fold_in(key_of[24], 71), 0),
        "project_in_momentum": centred(key_of[11], (D, 3 * D), 0.05, 0.75, (), jnp.float32),
        "project_out_momentum": centred(key_of[12], (D, D), 0.05, 0.75, (), jnp.float32),
        "expand_momentum": centred(key_of[13], (D, FF), 0.05, 0.75, (), jnp.float32),
        "reduce_momentum": centred(key_of[14], (FF, D), 0.05, 0.75, (), jnp.float32),
        "small_momentum": centred(key_of[15], (8 + FF // D, D), 0.3, 4.0, (), jnp.float32),
        "project_in_error": centred(key_of[16], (WORKERS, D, 3 * D), (2 * IMG_DEV + 8), 96.0, ((0, 32),), jnp.float32),
        "project_out_error": centred(key_of[17], (WORKERS, D, D), (2 * IMG_DEV + 8), 96.0, ((0, 32),), jnp.float32),
        "expand_error": centred(key_of[18], (WORKERS, D, FF), (2 * IMG_DEV + 8), 96.0, ((0, 32),), jnp.float32),
        "reduce_error": centred(key_of[19], (WORKERS, FF, D), (2 * IMG_DEV + 8), 96.0, ((0, 32),), jnp.float32),
        "project_in_factor": centred(key_of[20], (3 * D, RANK), 1.0, 6.0, (), jnp.float32),
        "project_out_factor": centred(key_of[21], (D, RANK), 1.0, 6.0, (), jnp.float32),
        "expand_factor": centred(key_of[22], (FF, RANK), 1.0, 6.0, (), jnp.float32),
        "reduce_factor": centred(key_of[23], (D, RANK), 1.0, 6.0, (), jnp.float32),
    }


EPSILON = 1e-06
RATE = 0.1
DECAY = 0.9
HIGH = lax.Precision.HIGHEST

@jax.custom_vjp
def low(v):
    return lax.optimization_barrier(v.astype(jnp.bfloat16)).astype(jnp.float32)

@jax.custom_vjp
def low_back(v):
    return v

def low_keep(v):
    return (low(v), None)

def low_pass(kept, grad):
    return (grad,)

def back_keep(v):
    return (v, None)

def back_low(kept, grad):
    return (low(grad),)
low.defvjp(low_keep, low_pass)
low_back.defvjp(back_keep, back_low)

def layer_norm(values, gain_row, bias_row):
    center = values - lax.optimization_barrier(jnp.mean(values, axis=-1, keepdims=True))
    spread = lax.optimization_barrier(jnp.mean(center * center, axis=-1, keepdims=True))
    return center * lax.rsqrt(spread + EPSILON) * gain_row + bias_row

def gelu_exact(values):
    return 0.5 * values * (1.0 + lax.erf(values * (1.0 / math.sqrt(2.0))))

def orthonormal(factor):
    columns = []
    for column_id in range(factor.shape[1]):
        column = factor[:, column_id]
        for earlier in columns:
            column = column - jnp.sum(earlier * column) * earlier
        columns.append(column * lax.rsqrt(jnp.sum(column * column) + EPSILON))
    return jnp.stack(columns, axis=1)

def mixed_product(hidden, weight_zero, weight_one, coef_zero, coef_one):
    part_zero = jnp.einsum('ntd,de->nte', hidden, low(weight_zero), precision=HIGH)
    part_one = jnp.einsum('ntd,de->nte', hidden, low(weight_one), precision=HIGH)
    return part_zero * coef_zero[None, :, None] + part_one * coef_one[None, :, None]

def layer_block(tokens_in, key_mask, coef_zero, coef_one, params, weights_zero, weights_one):
    image_count, length, model_width = tokens_in.shape
    expand_bias = params[8:].reshape(-1)
    hidden_one = low(layer_norm(tokens_in, params[0], params[1]))
    bias_qkv = jnp.concatenate([params[2], jnp.zeros((model_width,), jnp.float32), params[3]])
    qkv_rows = mixed_product(hidden_one, weights_zero[0], weights_one[0], coef_zero, coef_one) + bias_qkv
    qkv_rows = low_back(low(qkv_rows)).reshape(image_count, length, 3, HEADS, HEAD_DIM)
    query_rows = qkv_rows[:, :, 0]
    key_rows = qkv_rows[:, :, 1]
    value_rows = qkv_rows[:, :, 2]
    scores = low_back(jnp.einsum('iqhd,ikhd->ihqk', query_rows, key_rows, precision=HIGH) * (1.0 / math.sqrt(HEAD_DIM)))
    scores = jnp.where(key_mask[:, None, None, :], scores, -1e+30)
    row_top = lax.optimization_barrier(jnp.max(scores, axis=-1, keepdims=True))
    exp_scores = jnp.exp(scores - row_top)
    probs_low = low(exp_scores / lax.optimization_barrier(jnp.sum(exp_scores, axis=-1, keepdims=True)))
    attended = jnp.einsum('ihqk,ikhd->iqhd', probs_low, value_rows, precision=HIGH)
    attended = low_back(low(attended)).reshape(image_count, length, model_width)
    branch = low_back(mixed_product(attended, weights_zero[1], weights_one[1], coef_zero, coef_one) + params[4])
    middle = tokens_in + branch
    hidden_two = low(layer_norm(middle, params[5], params[6]))
    pre_act = low_back(mixed_product(hidden_two, weights_zero[2], weights_one[2], coef_zero, coef_one) + expand_bias)
    activated = low_back(low(gelu_exact(pre_act)))
    return middle + mixed_product(activated, weights_zero[3], weights_one[3], coef_zero, coef_one) + params[7]

def reference(patch_tokens, special_tokens, patch_upstream, special_upstream, patch_rank, keep_count, project_in, project_out, expand_weight, reduce_weight, small_params, project_in_momentum, project_out_momentum, expand_momentum, reduce_momentum, small_momentum, project_in_error, project_out_error, expand_error, reduce_error, project_in_factor, project_out_factor, expand_factor, reduce_factor):
    half_rows = PATCHES // N_SEQ
    length = PATCHES + 2
    model_width = patch_tokens.shape[2]
    positions = jnp.arange(length)
    coef_zero = jnp.where(positions < 2, 0.5, jnp.where(positions < 2 + half_rows, 1.0, 0.0)).astype(jnp.float32)
    coef_one = jnp.where(positions < 2, 0.5, jnp.where(positions < 2 + half_rows, 0.0, 1.0)).astype(jnp.float32)
    weights = (project_in, project_out, expand_weight, reduce_weight)
    kept_patches = patch_rank < keep_count[:, None]
    key_mask = jnp.concatenate([jnp.ones((IMAGES, 2), jnp.bool_), kept_patches], axis=1)
    tokens_all = jnp.concatenate([special_tokens, patch_tokens], axis=1).astype(jnp.float32) * key_mask[..., None]
    upstream_all = jnp.concatenate([special_upstream, patch_upstream], axis=1).astype(jnp.float32)
    tokens_all = tokens_all.reshape(REPLICAS, IMG_DEV, length, model_width)
    upstream_all = upstream_all.reshape(REPLICAS, IMG_DEV, length, model_width)
    mask_all = key_mask.reshape(REPLICAS, IMG_DEV, length)

    def replica_step(total_small, inputs):
        tokens_in, mask_rows, upstream = inputs

        def forward(tokens_value, params, weights_zero, weights_one):
            return layer_block(tokens_value, mask_rows, coef_zero, coef_one, params, weights_zero, weights_one)
        output, pullback = jax.vjp(forward, tokens_in, small_params, weights, weights)
        grad_in, grad_small, grad_zero, grad_one = pullback(upstream)
        return (total_small + grad_small, (output, grad_in * mask_rows[..., None], grad_zero, grad_one))
    total_small, (outputs, grads_in, grads_zero, grads_one) = lax.scan(replica_step, jnp.zeros_like(small_params), (tokens_all, mask_all, upstream_all))
    outputs = outputs.reshape(IMAGES, length, model_width)
    grads_in = grads_in.reshape(IMAGES, length, model_width)
    workers = N_SEQ * REPLICAS
    momenta = (project_in_momentum, project_out_momentum, expand_momentum, reduce_momentum)
    errors = (project_in_error, project_out_error, expand_error, reduce_error)
    factors = (project_in_factor, project_out_factor, expand_factor, reduce_factor)
    new_weights = []
    new_momenta = []
    new_errors = []
    new_factors = []
    for which in range(4):
        merged = jnp.concatenate([grads_zero[which], grads_one[which]], axis=0) + errors[which]
        left_sum = lax.optimization_barrier(jnp.sum(jnp.einsum('wnm,mr->wnr', merged, factors[which], precision=HIGH), axis=0)) / workers
        basis = orthonormal(left_sum)
        right_sum = lax.optimization_barrier(jnp.sum(jnp.einsum('wnm,nr->wmr', merged, basis, precision=HIGH), axis=0)) / workers
        approx = jnp.dot(basis, right_sum.T, precision=HIGH)
        new_errors.append(merged - approx)
        momentum_next = DECAY * momenta[which] + approx
        new_momenta.append(momentum_next)
        new_weights.append(weights[which] - RATE * momentum_next)
        new_factors.append(right_sum)
    small_grad = total_small / workers
    small_next = DECAY * small_momentum + small_grad
    small_new = small_params - RATE * small_next
    return (outputs[:, 2:].astype(jnp.bfloat16), outputs[:, :2].astype(jnp.bfloat16), grads_in[:, 2:].astype(jnp.bfloat16), grads_in[:, :2].astype(jnp.bfloat16), new_weights[0], new_weights[1], new_weights[2], new_weights[3], small_new, new_momenta[0], new_momenta[1], new_momenta[2], new_momenta[3], small_next, new_errors[0], new_errors[1], new_errors[2], new_errors[3], new_factors[0], new_factors[1], new_factors[2], new_factors[3])
```

```python
import functools
import math

import jax
import jax.numpy as jnp
from jax import lax
from jax.experimental import pallas as pl
from jax.experimental.pallas import tpu as pltpu
from jax.sharding import PartitionSpec as P

HEADS = 6
HEAD_DIM = 64
EPSILON = 1e-06
RATE = 0.1
DECAY = 0.9
RANK = 8
MESH = pl.DeviceIdType.MESH
F32 = jnp.float32
BF16 = jnp.bfloat16
INPUTS = (
    "patch_tokens",
    "special_tokens",
    "patch_upstream",
    "special_upstream",
    "patch_rank",
    "keep_count",
    "project_in",
    "project_out",
    "expand_weight",
    "reduce_weight",
    "small_params",
    "project_in_momentum",
    "project_out_momentum",
    "expand_momentum",
    "reduce_momentum",
    "small_momentum",
    "project_in_error",
    "project_out_error",
    "expand_error",
    "reduce_error",
    "project_in_factor",
    "project_out_factor",
    "expand_factor",
    "reduce_factor",
)
OUTPUTS = (
    "out_patch",
    "out_special",
    "grad_patch",
    "grad_special",
    "new_in",
    "new_out",
    "new_exp",
    "new_red",
    "new_small",
    "mom_in",
    "mom_out",
    "mom_exp",
    "mom_red",
    "mom_small",
    "err_in",
    "err_out",
    "err_exp",
    "err_red",
    "new_f_in",
    "new_f_out",
    "new_f_exp",
    "new_f_red",
)
KEYS = 128


def round_up(value, unit):
    return -(-value // unit) * unit


def mm(left_side, right_side):
    return jnp.dot(left_side, right_side, preferred_element_type=F32)


def mm_nt(left_side, right_side):
    return lax.dot_general(
        left_side, right_side, (((1,), (1,)), ((), ())), preferred_element_type=F32
    )


def mm_tn(left_side, right_side):
    return lax.dot_general(
        left_side, right_side, (((0,), (0,)), ((), ())), preferred_element_type=F32
    )


def split(value):
    high = value.astype(BF16)
    return high, (value - high.astype(F32)).astype(BF16)


def orthonormal(rows):
    row_ids = lax.broadcasted_iota(jnp.int32, (RANK, 1), 0)
    for step in range(RANK):
        own = rows[step : step + 1, :]
        dots = jnp.sum(rows * own, axis=1, keepdims=True)
        scale = lax.rsqrt(dots[step : step + 1, :] + EPSILON)
        unit = own * scale
        later = jnp.where(row_ids > step, dots * scale, 0.0)
        rows = jnp.where(row_ids == step, unit, rows - later * unit)
    return rows


def outer_product(basis, right):
    basis_high, basis_low = split(basis)
    right_high, right_low = split(right)
    left_stack = jnp.concatenate(
        [basis_high.astype(F32), basis_low.astype(F32)] * 2, axis=0
    ).astype(BF16)
    right_stack = jnp.concatenate(
        [right_high.astype(F32)] * 2 + [right_low.astype(F32)] * 2, axis=0
    ).astype(BF16)
    return left_stack, right_stack


class Names:
    pass


def layer_kernel(chips, groups, images, half, names, *all_refs):
    refs = Names()
    for name, ref in zip(names, all_refs):
        setattr(refs, name, ref)
    r = refs
    width = HEADS * HEAD_DIM
    special = round_up(half, 8)
    block = round_up(special + 2, 16)
    rows_all = images * block
    workers = 2 * chips
    seq = lax.axis_index("seq")
    node = lax.axis_index("node")
    group = lax.axis_index("group")
    chip = node * groups + group
    partner = 1 - seq

    loads = {}

    def load(name, source, target):
        loads[name] = pltpu.make_async_copy(source, target, r.load_sem.at[len(loads)])
        loads[name].start()

    load("tokens", r.patch_tokens, r.raw_patch)
    load("special", r.special_tokens, r.raw_special)
    load("rank", r.patch_rank, r.rank)
    load("small", r.small_params, r.new_small)
    load("w_in", r.project_in, r.new_in)
    load("f_in", r.project_in_factor, r.new_f_in)
    load("f_out", r.project_out_factor, r.new_f_out)
    load("f_exp", r.expand_factor, r.new_f_exp)
    load("f_red", r.reduce_factor, r.new_f_red)
    load("upstream", r.patch_upstream, r.raw_up)
    load("special_up", r.special_upstream, r.raw_special_up)
    load("e_in", r.project_in_error.at[0], r.err_in)
    load("e_exp", r.expand_error.at[0], r.err_exp)
    load("e_red", r.reduce_error.at[0], r.err_red)
    load("e_out", r.project_out_error.at[0], r.err_out)
    load("w_out", r.project_out, r.new_out)
    load("w_exp", r.expand_weight, r.new_exp)
    load("w_red", r.reduce_weight, r.new_red)
    load("m_small", r.small_momentum, r.mom_small)
    load("m_out", r.project_out_momentum, r.mom_out)
    load("m_exp", r.expand_momentum, r.mom_exp)
    load("m_red", r.reduce_momentum, r.mom_red)
    load("m_in", r.project_in_momentum, r.mom_in)

    barrier = pltpu.get_barrier_semaphore()
    pl.semaphore_signal(barrier, inc=1, device_id={"seq": partner}, device_id_type=MESH)

    def peer_of(step):
        other = lax.rem(chip + step, chips)
        return other // groups, lax.rem(other, groups)

    def greet(step, carry):
        other_node, other_group = peer_of(step)
        pl.semaphore_signal(
            barrier,
            inc=1,
            device_id={"node": other_node, "group": other_group},
            device_id_type=MESH,
        )
        return carry

    lax.fori_loop(1, chips, greet, 0)

    def to_partner(source, target, sem_id):
        return pltpu.make_async_remote_copy(
            src_ref=source,
            dst_ref=target,
            send_sem=r.pair_send.at[sem_id],
            recv_sem=r.pair_recv.at[sem_id],
            device_id={"seq": partner},
            device_id_type=MESH,
        )

    def to_chip(step, source, target, sems, sem_id):
        other_node, other_group = peer_of(step)
        return pltpu.make_async_remote_copy(
            src_ref=source,
            dst_ref=target,
            send_sem=sems[0].at[sem_id, step],
            recv_sem=sems[1].at[sem_id, step],
            device_id={"node": other_node, "group": other_group},
            device_id_type=MESH,
        )

    chip_sems = (r.chip_send, r.chip_recv)

    def chips_start(source, slots, sem_id):
        slots[chip] = source[...]

        def go(step, carry):
            to_chip(step, source, slots.at[chip], chip_sems, sem_id).start()
            return carry

        lax.fori_loop(1, chips, go, 0)

    def chips_finish(source, slots, sem_id):
        def done(step, carry):
            to_chip(step, source, slots.at[chip], chip_sems, sem_id).wait()
            return carry

        lax.fori_loop(1, chips, done, 0)

        def add(index, total):
            return total + slots[index].astype(F32)

        return lax.fori_loop(1, chips, add, slots[0].astype(F32), unroll=min(chips - 1, 15))

    def along(axis, step):
        size = lax.axis_size(axis)
        return {axis: lax.rem(lax.axis_index(axis) + step, size)}

    def axis_copy(axis, step, source, slots, sem_id):
        return pltpu.make_async_remote_copy(
            src_ref=source,
            dst_ref=slots.at[lax.axis_index(axis)],
            send_sem=r.chip_send.at[sem_id, step],
            recv_sem=r.chip_recv.at[sem_id, step],
            device_id=along(axis, step),
            device_id_type=MESH,
        )

    def axis_start(axis, source, slots, sem_id):
        slots[lax.axis_index(axis)] = source[...]

        def go(step, carry):
            axis_copy(axis, step, source, slots, sem_id).start()
            return carry

        lax.fori_loop(1, lax.axis_size(axis), go, 0)

    def axis_finish(axis, source, slots, sem_id):
        def done(step, carry):
            axis_copy(axis, step, source, slots, sem_id).wait()
            return carry

        lax.fori_loop(1, lax.axis_size(axis), done, 0)
        total = slots[0].astype(F32)
        for index in range(1, lax.axis_size(axis)):
            total = total + slots[index].astype(F32)
        return total

    loads["rank"].wait()
    r.flags[...] = jnp.zeros_like(r.flags)
    for i in range(images):
        r.flags[i : i + 1, 0:half] = jnp.where(
            r.rank[i : i + 1, :] < r.keep_count[i], 1.0, 0.0
        ).astype(F32)
    lane_ids = lax.broadcasted_iota(jnp.int32, (1, KEYS), 1)
    special_lanes = jnp.where((lane_ids >= special) & (lane_ids < special + 2), 1.0, 0.0)
    own_columns = jnp.transpose(r.flags[...] + special_lanes)
    for i in range(images):
        r.mask_columns[i, 0:KEYS, :] = own_columns[:, i : i + 1]

    small = r.new_small
    loads["small"].wait()

    def small_row(index):
        return small[index : index + 1, :]

    loads["tokens"].wait()
    loads["special"].wait()
    r.mixed[...] = r.raw_patch[...].astype(F32)
    for i in range(images):
        base = i * block
        r.tokens[base + special - 8 : base + block, :] = jnp.zeros(
            (block - special + 8, width), F32
        )
        r.tokens[base : base + half, :] = (
            r.mixed[:, i, :] * r.mask_columns[i, 0:half, :]
        )
        r.tokens[base + special : base + special + 2, :] = r.raw_special[i].astype(F32)

    def normalise(source, i, gain, shift, xhat_ref, scale_ref, hidden_ref):
        at = pl.ds(pl.multiple_of(i * block, 16), block)
        values = source[at, :]
        center = values - jnp.mean(values, axis=1, keepdims=True)
        spread = jnp.mean(center * center, axis=1, keepdims=True)
        scale = lax.rsqrt(spread + EPSILON)
        xhat = center * scale
        xhat_ref[at, :] = xhat
        scale_ref[at, :] = scale
        hidden_ref[at, :] = (xhat * gain + shift).astype(BF16)

    @pl.loop(0, images)
    def _(i):
        normalise(r.tokens, i, small_row(0), small_row(1), r.xhat_one, r.scale_one, r.hidden_one)

    loads["w_in"].wait()
    r.low_in[...] = r.new_in[...].astype(BF16)
    for i in range(images):
        r.keys[0, i, block:KEYS, :] = jnp.zeros((KEYS - block, 2 * width), BF16)
    for part in (1, 2, 0):
        product = mm(r.hidden_one[...], r.low_in[:, part * width : (part + 1) * width])
        if part == 0:
            query = (product + small_row(2)).astype(BF16).astype(F32) * (
                1.0 / math.sqrt(HEAD_DIM)
            )
            r.query[...] = query.astype(BF16)
        else:
            if part == 2:
                product = product + small_row(3)
            for i in range(images):
                r.keys[0, i, 0:block, (part - 1) * width : part * width] = product[
                    i * block : (i + 1) * block
                ].astype(BF16)
        if part == 2:
            pl.semaphore_wait(barrier, chips)
            key_copy = to_partner(r.keys.at[0], r.keys.at[1], 0)
            flag_copy = to_partner(r.flags, r.other_flags, 1)
            key_copy.start()
            flag_copy.start()

    def error_left(error_ref, factor_ref, row_start, row_count):
        return mm_nt(
            factor_ref[...].astype(BF16), error_ref[row_start : row_start + row_count, :].astype(BF16)
        )

    loads["upstream"].wait()
    loads["special_up"].wait()
    r.mixed[...] = r.raw_up[...].astype(F32)
    for i in range(images):
        base = i * block
        r.middle[base + special - 8 : base + block, :] = jnp.zeros(
            (block - special + 8, width), F32
        )
        r.middle[base : base + half, :] = r.mixed[:, i, :]
        r.middle[base + special : base + special + 2, :] = 0.5 * r.raw_special_up[i].astype(F32)
    r.upstream[...] = r.middle[...].astype(BF16)
    loads["f_in"].wait()
    loads["f_out"].wait()
    loads["f_exp"].wait()
    loads["f_red"].wait()
    loads["e_in"].wait()
    r.left_in[...] = error_left(r.err_in, r.new_f_in, 0, width)
    loads["e_exp"].wait()
    r.lefts[4] = error_left(r.err_exp, r.new_f_exp, 0, width)
    loads["e_red"].wait()
    for part in range(4):
        r.lefts[part] = error_left(r.err_red, r.new_f_red, part * width, width)
    loads["e_out"].wait()
    r.lefts[5] = error_left(r.err_out, r.new_f_out, 0, width)

    key_copy.wait()
    flag_copy.wait()
    other_columns = jnp.transpose(r.other_flags[...])
    for i in range(images):
        r.mask_columns[i, KEYS : 2 * KEYS, :] = other_columns[:, i : i + 1]

    pair_width = 2 * HEAD_DIM
    pairs = HEADS // 2
    low_lanes = lax.broadcasted_iota(jnp.int32, (1, pair_width), 1) < HEAD_DIM

    def stacked(value):
        zero = jnp.zeros_like(value)
        return jnp.concatenate(
            [jnp.where(low_lanes, value, zero), jnp.where(low_lanes, zero, value)], axis=0
        )

    def unstacked(value):
        return jnp.where(low_lanes, value[0:block], value[block : 2 * block])

    def of_both(i, lanes):
        return jnp.concatenate([r.keys[0, i, :, lanes], r.keys[1, i, :, lanes]], axis=0)

    @pl.loop(0, images)
    def _(i):
        at = pl.ds(pl.multiple_of(i * block, 16), block)
        valid = r.mask_columns[i] > 0.5
        for pair in range(pairs):
            lanes = slice(pair * pair_width, (pair + 1) * pair_width)
            value_lanes = slice(width + pair * pair_width, width + (pair + 1) * pair_width)
            scores = mm_nt(of_both(i, lanes), stacked(r.query[at, lanes]))
            scores = jnp.where(valid, scores, -1e30)
            top = jnp.max(scores, axis=0, keepdims=True)
            weights = jnp.exp(scores - top)
            probs = weights * (1.0 / jnp.sum(weights, axis=0, keepdims=True))
            r.probs[i * pairs + pair] = probs
            mixed = mm_tn(probs.astype(BF16), of_both(i, value_lanes))
            r.attended[at, lanes] = unstacked(mixed).astype(BF16)

    loads["w_out"].wait()
    r.low_out[...] = r.new_out[...].astype(BF16)
    r.middle[...] = r.tokens[...] + mm(r.attended[...], r.low_out[...]) + small_row(4)

    @pl.loop(0, images)
    def _(i):
        normalise(r.middle, i, small_row(5), small_row(6), r.xhat_two, r.scale_two, r.hidden_two)

    strip = 16
    chunk = 2 * width
    hidden_lanes = r.low_exp.shape[1]
    loads["w_exp"].wait()
    r.low_exp[...] = r.new_exp[...].astype(BF16)
    loads["w_red"].wait()
    r.low_red[...] = r.new_red[...].astype(BF16)
    bias_rows = chunk // width
    r.total[...] = r.middle[...] + small_row(7)
    for part in range(hidden_lanes // chunk):
        lanes = slice(part * chunk, (part + 1) * chunk)
        bias = jnp.concatenate(
            [small_row(8 + part * bias_rows + index) for index in range(bias_rows)], axis=1
        )
        r.wide[...] = mm(r.hidden_two[...], r.low_exp[:, lanes])

        @pl.loop(0, rows_all // strip)
        def _(index):
            at = pl.ds(pl.multiple_of(index * strip, strip), strip)
            pre = r.wide[at, :] + bias
            normal = 0.5 + 0.5 * lax.erf(pre * (1.0 / math.sqrt(2.0)))
            density = jnp.exp(-0.5 * pre * pre) * (1.0 / math.sqrt(2.0 * math.pi))
            r.activated[at, lanes] = (pre * normal).astype(BF16)
            r.slope[at, lanes] = normal + pre * density

        r.total[...] += mm(r.activated[:, lanes], r.low_red[lanes, :])
    for i in range(images):
        base = i * block
        r.mixed[:, i, :] = r.total[base : base + half, :]
        r.out_special[i] = r.total[base + special : base + special + 2, :].astype(BF16)

    r.out_patch[...] = r.mixed[...].astype(BF16)

    folded = mm_nt(r.new_f_red[...].astype(BF16), r.upstream[...]).astype(BF16)
    for part in range(4):
        lanes = slice(part * width, (part + 1) * width)
        r.lefts[part] += mm(folded, r.activated[:, lanes])
    ones = jnp.ones((8, rows_all), BF16)
    for part in range(hidden_lanes // chunk):
        lanes = slice(part * chunk, (part + 1) * chunk)
        grad_act = mm_nt(r.upstream[...], r.low_red[lanes, :]).astype(BF16).astype(F32)
        grad_pre = grad_act * r.slope[:, lanes]
        r.grad_pre[:, lanes] = grad_pre.astype(BF16)
        row = jnp.sum(grad_pre, axis=0, keepdims=True)
        for index in range(bias_rows):
            first = 4 + part * bias_rows + index
            r.lefts[6, first : first + 1, :] = row[:, index * width : (index + 1) * width]
        back = mm_nt(r.grad_pre[:, lanes], r.low_exp[:, lanes])
        if part == 0:
            r.total[...] = back
        else:
            r.total[...] += back
    folded = mm_nt(r.new_f_exp[...].astype(BF16), r.grad_pre[...]).astype(BF16)
    r.lefts[4] += mm(folded, r.hidden_two[...])

    def normalise_back(i, gain, xhat_ref, scale_ref, gain_ref, shift_ref):
        at = pl.ds(pl.multiple_of(i * block, 16), block)
        grad = r.total[at, :]
        xhat = xhat_ref[at, :]
        gained = grad * gain
        first = jnp.mean(gained, axis=1, keepdims=True)
        second = jnp.mean(gained * xhat, axis=1, keepdims=True)
        gain_ref[...] += jnp.sum(grad * xhat, axis=0, keepdims=True)
        shift_ref[...] += jnp.sum(grad, axis=0, keepdims=True)
        return scale_ref[at, :] * (gained - first - xhat * second)

    r.gain_sum[...] = jnp.zeros_like(r.gain_sum)
    r.shift_sum[...] = jnp.zeros_like(r.shift_sum)

    @pl.loop(0, images)
    def _(i):
        at = pl.ds(pl.multiple_of(i * block, 16), block)
        back = normalise_back(i, small_row(5), r.xhat_two, r.scale_two, r.gain_sum, r.shift_sum)
        grad = r.upstream[at, :].astype(F32) + back
        r.grad_middle[at, :] = grad
        r.grad_branch[at, :] = grad.astype(BF16)

    r.lefts[6, 1:2, :] = r.gain_sum[...]
    r.lefts[6, 2:3, :] = r.shift_sum[...]
    r.lefts[6, 3:4, :] = mm(ones, r.upstream[...])[0:1]
    r.lefts[6, 0:1, :] = mm(ones, r.grad_branch[...])[0:1]
    r.lefts[7] = jnp.zeros((RANK, width), F32)
    folded = mm_nt(r.new_f_out[...].astype(BF16), r.grad_branch[...]).astype(BF16)
    r.lefts[5] += mm(folded, r.attended[...])

    def units_pair_start(units, arrived, sem_id):
        copy = to_partner(units, arrived, sem_id)
        copy.start()
        return copy

    def units_group_start(copy, units, arrived, outgoing, slots, sem_id):
        copy.wait()
        for index in range(2):
            first = seq * 4 + 2 * index
            outgoing[0, index] = jnp.concatenate(
                [units[first] + arrived[first], units[first + 1] + arrived[first + 1]], axis=0
            ).astype(BF16)
        axis_start("group", outgoing.at[0], slots, sem_id)

    def units_node_start(outgoing, group_slots, node_slots, sem_id):
        total = axis_finish("group", outgoing.at[0], group_slots, sem_id)
        outgoing[1] = total.astype(BF16)
        axis_start("node", outgoing.at[1], node_slots, sem_id + 1)

    def units_share(outgoing, node_slots, result, sem_id, pair_id):
        total = axis_finish("node", outgoing.at[1], node_slots, sem_id)
        for index in range(2):
            first = seq * 4 + 2 * index
            result[first] = total[index, 0:RANK]
            result[first + 1] = total[index, RANK : 2 * RANK]
        half_units = result.at[pl.ds(seq * 4, 4)]
        copy = to_partner(half_units, half_units, pair_id)
        copy.start()
        return copy

    left_copy = units_pair_start(r.lefts, r.lefts_arrived, 2)

    r.grad_attended[...] = mm_nt(r.grad_branch[...], r.low_out[...]).astype(BF16)
    r.err_out[...] += mm_tn(r.attended[...], r.grad_branch[...])
    for part in range(hidden_lanes // chunk):
        lanes = slice(part * chunk, (part + 1) * chunk)
        r.err_red[lanes, :] += mm_tn(r.activated[:, lanes], r.upstream[...])
        r.err_exp[:, lanes] += mm_tn(r.hidden_two[...], r.grad_pre[:, lanes])
    units_group_start(left_copy, r.lefts, r.lefts_arrived, r.lefts_out, r.lefts_group, 0)

    def grad_copy(i):
        return to_partner(r.grad_sent.at[i], r.grad_arrived.at[i], 8 + i)

    @pl.loop(0, images)
    def _(i):
        base = pl.multiple_of(i * block, 16)
        at = pl.ds(base, block)
        specials = pl.ds(pl.multiple_of(base + special, 8), 2)
        for pair in range(pairs):
            lanes = slice(pair * pair_width, (pair + 1) * pair_width)
            value_lanes = slice(width + pair * pair_width, width + (pair + 1) * pair_width)
            grad_mixed = stacked(r.grad_attended[at, lanes])
            query = stacked(r.query[at, lanes])
            probs = r.probs[i * pairs + pair]
            grad_probs = mm_nt(of_both(i, value_lanes), grad_mixed)
            delta = jnp.sum(probs * grad_probs, axis=0, keepdims=True)
            grad_scores = (probs * (grad_probs - delta)).astype(BF16)
            r.grad_query[at, lanes] = unstacked(mm_tn(grad_scores, of_both(i, lanes))) * (
                1.0 / math.sqrt(HEAD_DIM)
            )
            grad_keys = mm(grad_scores, query)
            grad_values = mm(probs.astype(BF16), grad_mixed)
            r.grad_own[i, :, lanes] = grad_keys[0:KEYS]
            r.grad_own[i, :, value_lanes] = grad_values[0:KEYS]
            r.grad_sent[i, :, lanes] = grad_keys[KEYS : 2 * KEYS]
            r.grad_sent[i, :, value_lanes] = grad_values[KEYS : 2 * KEYS]
        r.grad_sent[i, special : special + 2, :] = r.grad_own[i, special : special + 2, :]
        r.grad_sent[i, block : block + 2, 0:width] = r.grad_query[specials, :]
        grad_copy(i).start()

    units_node_start(r.lefts_out, r.lefts_group, r.lefts_node, 0)

    row_ids = lax.broadcasted_iota(jnp.int32, (block, 1), 0)
    halved = jnp.where((row_ids >= special) & (row_ids < special + 2), 0.5, 1.0)

    @pl.loop(0, images)
    def _(i):
        grad_copy(i).wait()
        base = pl.multiple_of(i * block, 16)
        at = pl.ds(base, block)
        specials = pl.ds(pl.multiple_of(base + special, 8), 2)
        r.grad_query[specials, :] += r.grad_arrived[i, block : block + 2, 0:width]
        query_part = r.grad_query[at, :].astype(BF16).astype(F32) * halved
        r.grad_qkv[at, 0:width] = query_part.astype(BF16)
        rest = (r.grad_own[i, 0:block, :] + r.grad_arrived[i, 0:block, :]).astype(BF16)
        r.grad_qkv[at, width : 3 * width] = (rest.astype(F32) * halved).astype(BF16)

    folded = mm_nt(r.new_f_in[...].astype(BF16), r.grad_qkv[...]).astype(BF16)
    r.left_in[...] += mm(folded, r.hidden_one[...])
    left_in_copy = to_partner(r.left_in, r.left_in_arrived, 4)
    left_in_copy.start()

    r.total[...] = mm_nt(r.grad_qkv[...], r.low_in[...])

    left_in_copy.wait()
    pair_sum = r.left_in[...] + r.left_in_arrived[...]
    r.left_in_out[...] = jnp.concatenate(
        [pair_sum[:, 0:256], jnp.concatenate([pair_sum[:, 256:384], jnp.zeros((RANK, 128), F32)], axis=1)],
        axis=0,
    ).astype(BF16)
    chips_start(r.left_in_out, r.left_in_slots, 5)

    left_share = units_share(r.lefts_out, r.lefts_node, r.lefts_total, 1, 3)
    r.gain_sum[...] = jnp.zeros_like(r.gain_sum)
    r.shift_sum[...] = jnp.zeros_like(r.shift_sum)

    @pl.loop(0, images)
    def _(i):
        at = pl.ds(pl.multiple_of(i * block, 16), block)
        back = normalise_back(i, small_row(0), r.xhat_one, r.scale_one, r.gain_sum, r.shift_sum)
        r.total[at, :] = (back + r.grad_middle[at, :]) * (2.0 - jnp.where(halved < 1.0, 0.0, 1.0))

    r.late_rows[...] = jnp.zeros_like(r.late_rows)
    r.late_rows[0:1, :] = r.gain_sum[...]
    r.late_rows[1:2, :] = r.shift_sum[...]
    r.late_rows[2:3, :] = mm(ones, r.grad_qkv[:, 0:width])[0:1]
    r.late_rows[3:4, :] = mm(ones, r.grad_qkv[:, 2 * width : 3 * width])[0:1]
    left_share.wait()
    inverse = 1.0 / workers
    basis_red = orthonormal(
        jnp.concatenate([r.lefts_total[part] for part in range(4)], axis=1) * inverse
    )
    basis_exp = orthonormal(r.lefts_total[4] * inverse)
    basis_out = orthonormal(r.lefts_total[5] * inverse)
    r.basis_red[...] = basis_red
    r.basis_exp[...] = basis_exp
    r.basis_out[...] = basis_out

    def right_of(basis, merged):
        both = jnp.concatenate([basis, basis - basis.astype(BF16).astype(F32)], axis=0).astype(BF16)
        product = mm(both, merged.astype(BF16))
        return product[0:RANK] + product[RANK : 2 * RANK]

    for part in range(4):
        lanes = slice(part * width, (part + 1) * width)
        r.rights[part] = right_of(basis_exp, r.err_exp[:, lanes])
    r.rights[4] = right_of(basis_red, r.err_red[...])
    r.rights[5] = right_of(basis_out, r.err_out[...])
    r.rights[6] = jnp.zeros((RANK, width), F32)
    r.rights[7] = jnp.zeros((RANK, width), F32)
    right_copy = units_pair_start(r.rights, r.rights_arrived, 5)

    for part in range(3):
        lanes = slice(part * width, (part + 1) * width)
        r.err_in[:, lanes] += mm_tn(r.hidden_one[...], r.grad_qkv[:, lanes])
    units_group_start(right_copy, r.rights, r.rights_arrived, r.rights_out, r.rights_group, 2)

    total = chips_finish(r.left_in_out, r.left_in_slots, 5)
    basis_in = orthonormal(
        jnp.concatenate([total[0:RANK], total[RANK : 2 * RANK, 0:128]], axis=1) * inverse
    )
    for part in range(3):
        lanes = slice(part * width, (part + 1) * width)
        r.right_in[part] = right_of(basis_in, r.err_in[:, lanes])
    r.right_in[3] = r.late_rows[...]
    right_in_copy = to_partner(r.right_in, r.right_in_arrived, 6)
    right_in_copy.start()
    for i in range(images):
        base = i * block
        r.mixed[:, i, :] = r.total[base : base + half, :] * r.mask_columns[i, 0:half, :]
        r.grad_special[i] = r.total[base + special : base + special + 2, :].astype(BF16)
    right_in_copy.wait()
    first = seq * 2
    r.right_in_out[...] = jnp.concatenate(
        [
            r.right_in[first] + r.right_in_arrived[first],
            r.right_in[first + 1] + r.right_in_arrived[first + 1],
        ],
        axis=0,
    ).astype(BF16)
    chips_start(r.right_in_out, r.right_in_slots, 4)
    units_node_start(r.rights_out, r.rights_group, r.rights_node, 2)
    r.grad_patch[...] = r.mixed[...].astype(BF16)

    def update(basis, right, error_ref, weight_ref, momentum_ref, lanes, row_start, row_count):
        left_stack, right_stack = outer_product(basis, right)
        at = slice(row_start, row_start + row_count)
        approx = mm_tn(left_stack, right_stack)
        error_ref[at, lanes] = error_ref[at, lanes] - approx
        momentum = DECAY * momentum_ref[at, lanes] + approx
        momentum_ref[at, lanes] = momentum
        weight_ref[at, lanes] = weight_ref[at, lanes] - RATE * momentum

    right_share = units_share(r.rights_out, r.rights_node, r.rights_total, 3, 7)
    loads["m_small"].wait()
    loads["m_in"].wait()
    loads["m_out"].wait()
    loads["m_exp"].wait()
    loads["m_red"].wait()
    right_share.wait()
    for part in range(4):
        lanes = slice(part * width, (part + 1) * width)
        right = r.rights_total[part] * inverse
        update(r.basis_exp[...], right, r.err_exp, r.new_exp, r.mom_exp, lanes, 0, width)
        r.new_f_exp[:, lanes] = right
        right = r.rights_total[4] * inverse
        update(
            r.basis_red[:, lanes],
            right,
            r.err_red,
            r.new_red,
            r.mom_red,
            slice(0, width),
            part * width,
            width,
        )
    r.new_f_red[...] = r.rights_total[4] * inverse
    right = r.rights_total[5] * inverse
    update(r.basis_out[...], right, r.err_out, r.new_out, r.mom_out, slice(0, width), 0, width)
    r.new_f_out[...] = right

    total = chips_finish(r.right_in_out, r.right_in_slots, 4)
    r.right_in_total[first] = total[0:RANK]
    r.right_in_total[first + 1] = total[RANK : 2 * RANK]
    half_units = r.right_in_total.at[pl.ds(first, 2)]
    share = to_partner(half_units, half_units, 12)
    share.start()
    share.wait()
    for part in range(3):
        lanes = slice(part * width, (part + 1) * width)
        right = r.right_in_total[part] * inverse
        update(basis_in, right, r.err_in, r.new_in, r.mom_in, lanes, 0, width)
        r.new_f_in[:, lanes] = right

    def small_update(at, grad):
        momentum = DECAY * r.mom_small[at, :] + grad * inverse
        r.mom_small[at, :] = momentum
        r.new_small[at, :] = r.new_small[at, :] - RATE * momentum

    small_update(slice(0, 4), r.right_in_total[3][0:4])
    small_update(slice(4, 12), r.lefts_total[6])


def store_kernel(count, *refs):
    sources, targets, sem = refs[:count], refs[count : 2 * count], refs[2 * count]
    copies = []
    for index in range(count):
        source, target = sources[index], targets[index]
        if len(source.shape) != len(target.shape):
            target = target.at[0]
        copies.append(pltpu.make_async_copy(source, target, sem.at[index]))
    for copy in copies:
        copy.start()
    for copy in copies:
        copy.wait()


def body(chips, groups, *args):
    args = list(args)
    for index in (0, 2):
        args[index] = jnp.transpose(args[index], (1, 0, 2))
    half, images, width = args[0].shape
    wide = args[8].shape[1]
    special = round_up(half, 8)
    block = round_up(special + 2, 16)
    rows = images * block
    out_shapes = [((half, images, width), BF16), ((images, 2, width), BF16)] * 2
    weight_shapes = [(width, 3 * width), (width, width), (width, wide), (wide, width)]
    small_shape = (args[10].shape, F32)
    out_shapes += [(shape, F32) for shape in weight_shapes] + [small_shape]
    out_shapes += [(shape, F32) for shape in weight_shapes] + [small_shape]
    out_shapes += [(shape, F32) for shape in weight_shapes]
    out_shapes += [((RANK, size), F32) for size in (3 * width, width, wide, width)]
    unit = (RANK, width)
    scratch = dict(
        raw_patch=pltpu.VMEM((half, images, width), BF16),
        raw_special=pltpu.VMEM((images, 2, width), BF16),
        raw_up=pltpu.VMEM((half, images, width), BF16),
        raw_special_up=pltpu.VMEM((images, 2, width), BF16),
        mixed=pltpu.VMEM((half, images, width), F32),
        rank=pltpu.VMEM((images, half), jnp.int32),
        flags=pltpu.VMEM((8, KEYS), F32),
        other_flags=pltpu.VMEM((8, KEYS), F32),
        mask_columns=pltpu.VMEM((images, 2 * KEYS, 1), F32),
        tokens=pltpu.VMEM((rows, width), F32),
        xhat_one=pltpu.VMEM((rows, width), F32),
        xhat_two=pltpu.VMEM((rows, width), F32),
        scale_one=pltpu.VMEM((rows, 1), F32),
        scale_two=pltpu.VMEM((rows, 1), F32),
        hidden_one=pltpu.VMEM((rows, width), BF16),
        hidden_two=pltpu.VMEM((rows, width), BF16),
        low_in=pltpu.VMEM((width, 3 * width), BF16),
        low_out=pltpu.VMEM((width, width), BF16),
        low_exp=pltpu.VMEM((width, wide), BF16),
        low_red=pltpu.VMEM((wide, width), BF16),
        query=pltpu.VMEM((rows, width), BF16),
        keys=pltpu.VMEM((2, images, KEYS, 2 * width), BF16),
        upstream=pltpu.VMEM((rows, width), BF16),
        probs=pltpu.VMEM((images * HEADS // 2, 2 * KEYS, 2 * block), F32),
        attended=pltpu.VMEM((rows, width), BF16),
        middle=pltpu.VMEM((rows, width), F32),
        wide=pltpu.VMEM((rows, 2 * width), F32),
        activated=pltpu.VMEM((rows, wide), BF16),
        slope=pltpu.VMEM((rows, wide), F32),
        grad_pre=pltpu.VMEM((rows, wide), BF16),
        total=pltpu.VMEM((rows, width), F32),
        gain_sum=pltpu.VMEM((1, width), F32),
        shift_sum=pltpu.VMEM((1, width), F32),
        grad_middle=pltpu.VMEM((rows, width), F32),
        grad_branch=pltpu.VMEM((rows, width), BF16),
        grad_attended=pltpu.VMEM((rows, width), BF16),
        grad_query=pltpu.VMEM((rows, width), F32),
        grad_own=pltpu.VMEM((images, KEYS, 2 * width), F32),
        grad_sent=pltpu.VMEM((images, KEYS, 2 * width), F32),
        grad_arrived=pltpu.VMEM((images, KEYS, 2 * width), F32),
        grad_qkv=pltpu.VMEM((rows, 3 * width), BF16),
        lefts=pltpu.VMEM((8,) + unit, F32),
        lefts_arrived=pltpu.VMEM((8,) + unit, F32),
        lefts_out=pltpu.VMEM((2, 2, 2 * RANK, width), BF16),
        lefts_group=pltpu.VMEM((groups, 2, 2 * RANK, width), BF16),
        lefts_node=pltpu.VMEM((chips // groups, 2, 2 * RANK, width), BF16),
        lefts_total=pltpu.VMEM((8,) + unit, F32),
        rights=pltpu.VMEM((8,) + unit, F32),
        rights_arrived=pltpu.VMEM((8,) + unit, F32),
        rights_out=pltpu.VMEM((2, 2, 2 * RANK, width), BF16),
        rights_group=pltpu.VMEM((groups, 2, 2 * RANK, width), BF16),
        rights_node=pltpu.VMEM((chips // groups, 2, 2 * RANK, width), BF16),
        rights_total=pltpu.VMEM((8,) + unit, F32),
        left_in=pltpu.VMEM(unit, F32),
        left_in_arrived=pltpu.VMEM(unit, F32),
        left_in_out=pltpu.VMEM((2 * RANK, 256), BF16),
        left_in_slots=pltpu.VMEM((chips, 2 * RANK, 256), BF16),
        right_in=pltpu.VMEM((4,) + unit, F32),
        right_in_arrived=pltpu.VMEM((4,) + unit, F32),
        right_in_out=pltpu.VMEM((2 * RANK, width), BF16),
        right_in_slots=pltpu.VMEM((chips, 2 * RANK, width), BF16),
        right_in_total=pltpu.VMEM((4,) + unit, F32),
        basis_red=pltpu.VMEM((RANK, wide), F32),
        basis_exp=pltpu.VMEM(unit, F32),
        basis_out=pltpu.VMEM(unit, F32),
        late_rows=pltpu.VMEM(unit, F32),
        load_sem=pltpu.SemaphoreType.DMA((23,)),
        pair_send=pltpu.SemaphoreType.DMA((13,)),
        pair_recv=pltpu.SemaphoreType.DMA((13,)),
        chip_send=pltpu.SemaphoreType.DMA((6, chips)),
        chip_recv=pltpu.SemaphoreType.DMA((6, chips)),
    )
    names = INPUTS + OUTPUTS + tuple(scratch)
    in_specs = [
        pl.BlockSpec(memory_space=pltpu.SMEM if name == "keep_count" else pl.ANY)
        for name in INPUTS
    ]
    in_vmem = pl.BlockSpec(memory_space=pltpu.VMEM)
    results = pl.pallas_call(
        functools.partial(layer_kernel, chips, groups, images, half, names),
        out_shape=[pltpu.VMEM(shape, dtype) for shape, dtype in out_shapes],
        in_specs=in_specs,
        out_specs=[in_vmem] * len(OUTPUTS),
        scratch_shapes=list(scratch.values()),
        compiler_params=pltpu.CompilerParams(
            collective_id=0, has_side_effects=True, vmem_limit_bytes=40 << 20
        ),
        name="layer",
    )(*args[:20], *[jnp.transpose(factor) for factor in args[20:]])
    final_shapes = [
        jax.ShapeDtypeStruct((1,) + shape if 14 <= index < 18 else shape, dtype)
        for index, (shape, dtype) in enumerate(out_shapes)
    ]
    count = len(OUTPUTS)
    stored = list(
        pl.pallas_call(
            functools.partial(store_kernel, count),
            out_shape=final_shapes,
            in_specs=[in_vmem] * count,
            out_specs=[pl.BlockSpec(memory_space=pl.ANY)] * count,
            scratch_shapes=[pltpu.SemaphoreType.DMA((count,))],
            compiler_params=pltpu.CompilerParams(vmem_limit_bytes=1 << 20),
            name="store",
        )(*results)
    )
    for index in (0, 2):
        stored[index] = jnp.transpose(stored[index], (1, 0, 2))
    return (*stored[:18], *[jnp.transpose(factor) for factor in stored[18:]])


def solution(mesh):
    images_over = ("node", "group")
    rows_spec = P(images_over, "seq", None)
    special_spec = P(images_over, None, None)
    worker_spec = P(("seq", "node", "group"), None, None)
    whole = P()
    placed = (
        (rows_spec, special_spec) * 2
        + (P(images_over, "seq"), P(images_over))
        + (whole,) * 10
        + (worker_spec,) * 4
        + (whole,) * 4
    )
    groups = mesh.shape["group"]
    chips = mesh.shape["node"] * groups
    return jax.shard_map(
        functools.partial(body, chips, groups),
        mesh=mesh,
        in_specs=placed,
        out_specs=(rows_spec, special_spec) * 2
        + (whole,) * 10
        + (worker_spec,) * 4
        + (whole,) * 4,
        check_vma=False,
    )
```

```python
import functools
import math

import jax
import jax.numpy as jnp
from jax import lax
from jax.experimental import pallas as pl
from jax.experimental.pallas import tpu as pltpu
from jax.sharding import PartitionSpec as P

HEADS = 6
HEAD_DIM = 64
EPSILON = 1e-06
RATE = 0.1
DECAY = 0.9
RANK = 8
MESH = pl.DeviceIdType.MESH
F32 = jnp.float32
BF16 = jnp.bfloat16
INPUTS = (
    "patch_tokens",
    "special_tokens",
    "patch_upstream",
    "special_upstream",
    "patch_rank",
    "keep_count",
    "project_in",
    "project_out",
    "expand_weight",
    "reduce_weight",
    "small_params",
    "project_in_momentum",
    "project_out_momentum",
    "expand_momentum",
    "reduce_momentum",
    "small_momentum",
    "project_in_error",
    "project_out_error",
    "expand_error",
    "reduce_error",
    "project_in_factor",
    "project_out_factor",
    "expand_factor",
    "reduce_factor",
)
OUTPUTS = (
    "out_patch",
    "out_special",
    "grad_patch",
    "grad_special",
    "new_in",
    "new_out",
    "new_exp",
    "new_red",
    "new_small",
    "mom_in",
    "mom_out",
    "mom_exp",
    "mom_red",
    "mom_small",
    "err_in",
    "err_out",
    "err_exp",
    "err_red",
    "new_f_in",
    "new_f_out",
    "new_f_exp",
    "new_f_red",
)
BASES = ("basis_in", "basis_out", "basis_exp", "basis_red")
KINDS = ("new_", "mom_", "err_")
MATRICES = ("in", "out", "exp", "red")
KEYS = 128


def round_up(value, unit):
    return -(-value // unit) * unit


def mm(left_side, right_side):
    return jnp.dot(left_side, right_side, preferred_element_type=F32)


def mm_nt(left_side, right_side):
    return lax.dot_general(
        left_side, right_side, (((1,), (1,)), ((), ())), preferred_element_type=F32
    )


def mm_tn(left_side, right_side):
    return lax.dot_general(
        left_side, right_side, (((0,), (0,)), ((), ())), preferred_element_type=F32
    )


def split(value):
    high = value.astype(BF16)
    return high, (value - high.astype(F32)).astype(BF16)


def orthonormal(rows):
    row_ids = lax.broadcasted_iota(jnp.int32, (RANK, 1), 0)
    for step in range(RANK):
        own = rows[step : step + 1, :]
        dots = jnp.sum(rows * own, axis=1, keepdims=True)
        scale = lax.rsqrt(dots[step : step + 1, :] + EPSILON)
        unit = own * scale
        later = jnp.where(row_ids > step, dots * scale, 0.0)
        rows = jnp.where(row_ids == step, unit, rows - later * unit)
    return rows


def outer_product(basis, right):
    basis_high, basis_low = split(basis)
    right_high, right_low = split(right)
    left_stack = jnp.concatenate(
        [basis_high.astype(F32), basis_low.astype(F32)] * 2, axis=0
    ).astype(BF16)
    right_stack = jnp.concatenate(
        [right_high.astype(F32)] * 2 + [right_low.astype(F32)] * 2, axis=0
    ).astype(BF16)
    return left_stack, right_stack


class Names:
    pass


def layer_kernel(chips, groups, images, half, names, *all_refs):
    refs = Names()
    for name, ref in zip(names, all_refs):
        setattr(refs, name, ref)
    r = refs
    width = HEADS * HEAD_DIM
    special = round_up(half, 8)
    block = round_up(special + 2, 16)
    rows_all = images * block
    workers = 2 * chips
    seq = lax.axis_index("seq")
    node = lax.axis_index("node")
    group = lax.axis_index("group")
    chip = node * groups + group
    partner = 1 - seq

    loads = {}

    def load(name, source, target):
        loads[name] = pltpu.make_async_copy(source, target, r.load_sem.at[len(loads)])
        loads[name].start()

    load("tokens", r.patch_tokens, r.raw_patch)
    load("special", r.special_tokens, r.raw_special)
    load("rank", r.patch_rank, r.rank)
    load("count", r.keep_count, r.count)
    load("small", r.small_params, r.new_small)
    load("w_in", r.project_in, r.new_in)

    def load_second():
        load("upstream", r.patch_upstream, r.raw_up)
        load("special_up", r.special_upstream, r.raw_special_up)
        load("f_in", r.project_in_factor, r.new_f_in)
        load("f_out", r.project_out_factor, r.new_f_out)
        load("f_exp", r.expand_factor, r.new_f_exp)
        load("f_red", r.reduce_factor, r.new_f_red)
        load("e_in", r.project_in_error.at[0], r.err_in)
        load("e_exp", r.expand_error.at[0], r.err_exp)
        load("e_red", r.reduce_error.at[0], r.err_red)
        load("e_out", r.project_out_error.at[0], r.err_out)

    def load_third():
        load("w_out", r.project_out, r.new_out)
        load("w_exp", r.expand_weight, r.new_exp)
        load("w_red", r.reduce_weight, r.new_red)

    def load_last():
        load("m_small", r.small_momentum, r.mom_small)
        load("m_out", r.project_out_momentum, r.mom_out)
        load("m_exp", r.expand_momentum, r.mom_exp)
        load("m_red", r.reduce_momentum, r.mom_red)
        load("m_in", r.project_in_momentum, r.mom_in)

    barrier = pltpu.get_barrier_semaphore()
    pl.semaphore_signal(barrier, inc=1, device_id={"seq": partner}, device_id_type=MESH)

    def peer_of(step):
        other = lax.rem(chip + step, chips)
        return other // groups, lax.rem(other, groups)

    def greet(step, carry):
        other_node, other_group = peer_of(step)
        pl.semaphore_signal(
            barrier,
            inc=1,
            device_id={"node": other_node, "group": other_group},
            device_id_type=MESH,
        )
        return carry

    lax.fori_loop(1, chips, greet, 0)

    def to_partner(source, target, sem_id):
        return pltpu.make_async_remote_copy(
            src_ref=source,
            dst_ref=target,
            send_sem=r.pair_send.at[sem_id],
            recv_sem=r.pair_recv.at[sem_id],
            device_id={"seq": partner},
            device_id_type=MESH,
        )

    def to_chip(step, source, target, sems, sem_id):
        other_node, other_group = peer_of(step)
        return pltpu.make_async_remote_copy(
            src_ref=source,
            dst_ref=target,
            send_sem=sems[0].at[sem_id, step],
            recv_sem=sems[1].at[sem_id, step],
            device_id={"node": other_node, "group": other_group},
            device_id_type=MESH,
        )

    chip_sems = (r.chip_send, r.chip_recv)

    def chips_start(source, slots, sem_id):
        slots[chip] = source[...]

        def go(step, carry):
            to_chip(step, source, slots.at[chip], chip_sems, sem_id).start()
            return carry

        lax.fori_loop(1, chips, go, 0)

    def chips_finish(source, slots, sem_id):
        def done(step, carry):
            to_chip(step, source, slots.at[chip], chip_sems, sem_id).wait()
            return carry

        lax.fori_loop(1, chips, done, 0)

        def add(index, total):
            return total + slots[index].astype(F32)

        return lax.fori_loop(1, chips, add, slots[0].astype(F32), unroll=min(chips - 1, 15))

    def along(axis, step):
        size = lax.axis_size(axis)
        return {axis: lax.rem(lax.axis_index(axis) + step, size)}

    def axis_copy(axis, step, source, slots, sem_id):
        return pltpu.make_async_remote_copy(
            src_ref=source,
            dst_ref=slots.at[lax.axis_index(axis)],
            send_sem=r.chip_send.at[sem_id, step],
            recv_sem=r.chip_recv.at[sem_id, step],
            device_id=along(axis, step),
            device_id_type=MESH,
        )

    def axis_start(axis, source, slots, sem_id):
        slots[lax.axis_index(axis)] = source[...]

        def go(step, carry):
            axis_copy(axis, step, source, slots, sem_id).start()
            return carry

        lax.fori_loop(1, lax.axis_size(axis), go, 0)

    def axis_finish(axis, source, slots, sem_id):
        def done(step, carry):
            axis_copy(axis, step, source, slots, sem_id).wait()
            return carry

        lax.fori_loop(1, lax.axis_size(axis), done, 0)
        total = slots[0].astype(F32)
        for index in range(1, lax.axis_size(axis)):
            total = total + slots[index].astype(F32)
        return total

    loads["rank"].wait()
    loads["count"].wait()
    r.flags[...] = jnp.zeros_like(r.flags)
    for i in range(images):
        r.flags[i : i + 1, 0:half] = jnp.where(
            r.rank[i : i + 1, :] < r.count[i], 1.0, 0.0
        ).astype(F32)
    lane_ids = lax.broadcasted_iota(jnp.int32, (1, KEYS), 1)
    special_lanes = jnp.where((lane_ids >= special) & (lane_ids < special + 2), 1.0, 0.0)
    own_columns = jnp.transpose(r.flags[...] + special_lanes)
    for i in range(images):
        r.mask_columns[i, 0:KEYS, :] = own_columns[:, i : i + 1]

    small = r.new_small
    loads["small"].wait()

    def small_row(index):
        return small[index : index + 1, :]

    loads["tokens"].wait()
    loads["special"].wait()
    r.mixed[...] = r.raw_patch[...].astype(F32)
    for i in range(images):
        base = i * block
        r.tokens[base + special - 8 : base + block, :] = jnp.zeros(
            (block - special + 8, width), F32
        )
        r.tokens[base : base + half, :] = (
            r.mixed[:, i, :] * r.mask_columns[i, 0:half, :]
        )
        r.tokens[base + special : base + special + 2, :] = r.raw_special[i].astype(F32)

    def normalise(source, i, gain, shift, xhat_ref, scale_ref, hidden_ref):
        at = pl.ds(pl.multiple_of(i * block, 16), block)
        values = source[at, :]
        center = values - jnp.mean(values, axis=1, keepdims=True)
        spread = jnp.mean(center * center, axis=1, keepdims=True)
        scale = lax.rsqrt(spread + EPSILON)
        xhat = center * scale
        xhat_ref[at, :] = xhat
        scale_ref[at, :] = scale
        hidden_ref[at, :] = (xhat * gain + shift).astype(BF16)

    @pl.loop(0, images)
    def _(i):
        normalise(r.tokens, i, small_row(0), small_row(1), r.xhat_one, r.scale_one, r.hidden_one)

    loads["w_in"].wait()
    load_second()
    r.low_in[0:width, :] = r.new_in[...].astype(BF16)
    for i in range(images):
        r.keys[0, i, block:KEYS, :] = jnp.zeros((KEYS - block, 2 * width), BF16)
    for part in (1, 2, 0):
        product = mm(r.hidden_one[...], r.low_in[0:width, part * width : (part + 1) * width])
        if part == 0:
            query = (product + small_row(2)).astype(BF16).astype(F32) * (
                1.0 / math.sqrt(HEAD_DIM)
            )
            r.query[...] = query.astype(BF16)
        else:
            if part == 2:
                product = product + small_row(3)
            for i in range(images):
                r.keys[0, i, 0:block, (part - 1) * width : part * width] = product[
                    i * block : (i + 1) * block
                ].astype(BF16)
        if part == 2:
            pl.semaphore_wait(barrier, chips)
            key_copy = to_partner(r.keys.at[0], r.keys.at[1], 0)
            flag_copy = to_partner(r.flags, r.other_flags, 1)
            key_copy.start()
            flag_copy.start()

    def error_left(error_ref, factor_ref, row_start, row_count):
        return mm_nt(
            factor_ref[...].astype(BF16), error_ref[row_start : row_start + row_count, :].astype(BF16)
        )

    loads["upstream"].wait()
    loads["special_up"].wait()
    r.mixed[...] = r.raw_up[...].astype(F32)
    for i in range(images):
        base = i * block
        r.middle[base + special - 8 : base + block, :] = jnp.zeros(
            (block - special + 8, width), F32
        )
        r.middle[base : base + half, :] = r.mixed[:, i, :]
        r.middle[base + special : base + special + 2, :] = 0.5 * r.raw_special_up[i].astype(F32)
    r.lefts[6, 3:4, :] = jnp.sum(r.middle[...], axis=0, keepdims=True)
    r.upstream[...] = r.middle[...].astype(BF16)
    loads["f_in"].wait()
    loads["f_out"].wait()
    loads["f_exp"].wait()
    loads["f_red"].wait()

    def with_factor(low_ref, factor_ref):
        factor = factor_ref[...]
        low_ref[width : width + 2 * RANK, :] = jnp.concatenate(
            [factor, jnp.zeros_like(factor)], axis=0
        ).astype(BF16)

    with_factor(r.low_in, r.new_f_in)
    with_factor(r.low_out, r.new_f_out)
    with_factor(r.low_exp, r.new_f_exp)
    folded_red = mm_nt(r.new_f_red[...].astype(BF16), r.upstream[...])
    r.folded_red[...] = folded_red.astype(BF16)
    loads["e_in"].wait()
    r.left_in[...] = error_left(r.err_in, r.new_f_in, 0, width)
    loads["e_exp"].wait()
    r.lefts[4] = error_left(r.err_exp, r.new_f_exp, 0, width)
    load_third()
    loads["e_red"].wait()
    for part in range(4):
        r.lefts[part] = error_left(r.err_red, r.new_f_red, part * width, width)
    loads["e_out"].wait()
    r.lefts[5] = error_left(r.err_out, r.new_f_out, 0, width)

    key_copy.wait()
    flag_copy.wait()
    other_columns = jnp.transpose(r.other_flags[...])
    for i in range(images):
        r.mask_columns[i, KEYS : 2 * KEYS, :] = other_columns[:, i : i + 1]

    pair_width = 2 * HEAD_DIM
    pairs = HEADS // 2
    low_lanes = lax.broadcasted_iota(jnp.int32, (1, pair_width), 1) < HEAD_DIM

    def stacked(value):
        zero = jnp.zeros_like(value)
        return jnp.concatenate(
            [jnp.where(low_lanes, value, zero), jnp.where(low_lanes, zero, value)], axis=0
        )

    def unstacked(value):
        return jnp.where(low_lanes, value[0:block], value[block : 2 * block])

    def of_both(i, lanes):
        return jnp.concatenate([r.keys[0, i, :, lanes], r.keys[1, i, :, lanes]], axis=0)

    @pl.loop(0, images)
    def _(i):
        at = pl.ds(pl.multiple_of(i * block, 16), block)
        valid = r.mask_columns[i] > 0.5

        def lanes_of(pair, first=0):
            return slice(first + pair * pair_width, first + (pair + 1) * pair_width)

        for pair in range(pairs):
            scores = mm_nt(of_both(i, lanes_of(pair)), stacked(r.query[at, lanes_of(pair)]))
            r.probs[i * pairs + pair] = jnp.where(valid, scores, -1e30)
        for pair in range(pairs):
            scores = r.probs[i * pairs + pair]
            top = jnp.max(scores, axis=0, keepdims=True)
            weights = jnp.exp(scores - top)
            probs = weights * (1.0 / jnp.sum(weights, axis=0, keepdims=True))
            r.probs[i * pairs + pair] = probs
            r.low_probs[pair] = probs.astype(BF16)
        for pair in range(pairs):
            mixed = mm_tn(r.low_probs[pair], of_both(i, lanes_of(pair, width)))
            r.attended[at, lanes_of(pair)] = unstacked(mixed).astype(BF16)

    loads["w_out"].wait()
    load_last()
    r.low_out[0:width, :] = r.new_out[...].astype(BF16)
    r.middle[...] = r.tokens[...] + mm(r.attended[...], r.low_out[0:width, :]) + small_row(4)

    @pl.loop(0, images)
    def _(i):
        normalise(r.middle, i, small_row(5), small_row(6), r.xhat_two, r.scale_two, r.hidden_two)

    strip = 16
    chunk = 2 * width
    hidden_lanes = r.low_exp.shape[1]
    loads["w_exp"].wait()
    r.low_exp[0:width, :] = r.new_exp[...].astype(BF16)
    loads["w_red"].wait()
    r.low_red[...] = r.new_red[...].astype(BF16)
    bias_rows = chunk // width
    r.total[...] = r.middle[...] + small_row(7)
    for part in range(hidden_lanes // chunk):
        lanes = slice(part * chunk, (part + 1) * chunk)
        bias = jnp.concatenate(
            [small_row(8 + part * bias_rows + index) for index in range(bias_rows)], axis=1
        )
        r.wide[...] = mm(r.hidden_two[...], r.low_exp[0:width, lanes])

        @pl.loop(0, rows_all // strip)
        def _(index):
            at = pl.ds(pl.multiple_of(index * strip, strip), strip)
            pre = r.wide[at, :] + bias
            normal = 0.5 + 0.5 * lax.erf(pre * (1.0 / math.sqrt(2.0)))
            density = jnp.exp(-0.5 * pre * pre) * (1.0 / math.sqrt(2.0 * math.pi))
            r.activated[at, lanes] = (pre * normal).astype(BF16)
            r.slope[at, lanes] = normal + pre * density

        r.total[...] += mm(r.activated[:, lanes], r.low_red[lanes, :])
    for i in range(images):
        base = i * block
        r.mixed[:, i, :] = r.total[base : base + half, :]
        r.out_special[i] = r.total[base + special : base + special + 2, :].astype(BF16)

    r.out_patch[...] = r.mixed[...].astype(BF16)

    for part in range(4):
        lanes = slice(part * width, (part + 1) * width)
        r.lefts[part] += mm(r.folded_red[...], r.activated[:, lanes])
    for part in range(hidden_lanes // chunk):
        lanes = slice(part * chunk, (part + 1) * chunk)
        grad_act = mm_nt(r.upstream[...], r.low_red[lanes, :]).astype(BF16).astype(F32)
        grad_pre = grad_act * r.slope[:, lanes]
        r.grad_pre[:, lanes] = grad_pre.astype(BF16)
        row = jnp.sum(grad_pre, axis=0, keepdims=True)
        for index in range(bias_rows):
            first = 4 + part * bias_rows + index
            r.lefts[6, first : first + 1, :] = row[:, index * width : (index + 1) * width]
        back = mm_nt(r.grad_pre[:, lanes], r.low_exp[:, lanes])
        if part == 0:
            r.total[...] = back[:, 0:width]
            r.folded[...] = back[:, width : width + 2 * RANK]
        else:
            r.total[...] += back[:, 0:width]
            r.folded[...] += back[:, width : width + 2 * RANK]

    def left_of(hidden_ref):
        return mm_tn(r.folded[...].astype(BF16), hidden_ref[...])[0:RANK]

    r.lefts[4] += left_of(r.hidden_two)

    def normalise_back(i, gain, xhat_ref, scale_ref, gain_ref, shift_ref):
        at = pl.ds(pl.multiple_of(i * block, 16), block)
        grad = r.total[at, :]
        xhat = xhat_ref[at, :]
        gained = grad * gain
        first = jnp.mean(gained, axis=1, keepdims=True)
        second = jnp.mean(gained * xhat, axis=1, keepdims=True)
        gain_ref[...] += jnp.sum(grad * xhat, axis=0, keepdims=True)
        shift_ref[...] += jnp.sum(grad, axis=0, keepdims=True)
        return scale_ref[at, :] * (gained - first - xhat * second)

    r.gain_sum[...] = jnp.zeros_like(r.gain_sum)
    r.shift_sum[...] = jnp.zeros_like(r.shift_sum)
    r.branch_sum[...] = jnp.zeros_like(r.branch_sum)

    @pl.loop(0, images)
    def _(i):
        at = pl.ds(pl.multiple_of(i * block, 16), block)
        back = normalise_back(i, small_row(5), r.xhat_two, r.scale_two, r.gain_sum, r.shift_sum)
        grad = r.upstream[at, :].astype(F32) + back
        r.grad_middle[at, :] = grad
        low = grad.astype(BF16)
        r.grad_branch[at, :] = low
        r.branch_sum[...] += jnp.sum(low.astype(F32), axis=0, keepdims=True)

    r.lefts[6, 1:2, :] = r.gain_sum[...]
    r.lefts[6, 2:3, :] = r.shift_sum[...]
    r.lefts[6, 0:1, :] = r.branch_sum[...]
    r.lefts[7] = jnp.zeros((RANK, width), F32)
    back = mm_nt(r.grad_branch[...], r.low_out[...])
    r.grad_attended[...] = back[:, 0:width].astype(BF16)
    r.folded[...] = back[:, width : width + 2 * RANK]
    r.lefts[5] += left_of(r.attended)

    def units_pair_start(units, arrived, sem_id):
        copy = to_partner(units, arrived, sem_id)
        copy.start()
        return copy

    def units_group_start(copy, units, arrived, outgoing, slots, sem_id):
        copy.wait()
        for index in range(2):
            first = seq * 4 + 2 * index
            outgoing[0, index] = jnp.concatenate(
                [units[first] + arrived[first], units[first + 1] + arrived[first + 1]], axis=0
            ).astype(BF16)
        axis_start("group", outgoing.at[0], slots, sem_id)

    def units_node_start(outgoing, group_slots, node_slots, sem_id):
        total = axis_finish("group", outgoing.at[0], group_slots, sem_id)
        outgoing[1] = total.astype(BF16)
        axis_start("node", outgoing.at[1], node_slots, sem_id + 1)

    def units_share(outgoing, node_slots, result, sem_id, pair_id):
        total = axis_finish("node", outgoing.at[1], node_slots, sem_id)
        for index in range(2):
            first = seq * 4 + 2 * index
            result[first] = total[index, 0:RANK]
            result[first + 1] = total[index, RANK : 2 * RANK]
        half_units = result.at[pl.ds(seq * 4, 4)]
        copy = to_partner(half_units, half_units, pair_id)
        copy.start()
        return copy

    left_copy = units_pair_start(r.lefts, r.lefts_arrived, 2)

    def grad_copy(i):
        return to_partner(r.grad_sent.at[i], r.grad_arrived.at[i], 8 + i)

    @pl.loop(0, images)
    def _(i):
        base = pl.multiple_of(i * block, 16)
        at = pl.ds(base, block)
        specials = pl.ds(pl.multiple_of(base + special, 8), 2)

        def lanes_of(pair, first=0):
            return slice(first + pair * pair_width, first + (pair + 1) * pair_width)

        for pair in range(pairs):
            grad_mixed = stacked(r.grad_attended[at, lanes_of(pair)])
            r.grad_probs[pair] = mm_nt(of_both(i, lanes_of(pair, width)), grad_mixed)
        for pair in range(pairs):
            probs = r.probs[i * pairs + pair]
            weighted = probs * r.grad_probs[pair]
            delta = jnp.sum(weighted, axis=0, keepdims=True)
            r.low_probs[pair] = (weighted - probs * delta).astype(BF16)
        for pair in range(pairs):
            grad_scores = r.low_probs[pair]
            r.grad_query[at, lanes_of(pair)] = unstacked(
                mm_tn(grad_scores, of_both(i, lanes_of(pair)))
            ) * (1.0 / math.sqrt(HEAD_DIM))
            grad_keys = mm(grad_scores, stacked(r.query[at, lanes_of(pair)]))
            r.grad_own[i, :, lanes_of(pair)] = grad_keys[0:KEYS]
            r.grad_sent[i, :, lanes_of(pair)] = grad_keys[KEYS : 2 * KEYS]
        for pair in range(pairs):
            grad_mixed = stacked(r.grad_attended[at, lanes_of(pair)])
            grad_values = mm(r.probs[i * pairs + pair].astype(BF16), grad_mixed)
            r.grad_own[i, :, lanes_of(pair, width)] = grad_values[0:KEYS]
            r.grad_sent[i, :, lanes_of(pair, width)] = grad_values[KEYS : 2 * KEYS]
        r.grad_sent[i, special : special + 2, :] = r.grad_own[i, special : special + 2, :]
        r.grad_sent[i, block : block + 2, 0:width] = r.grad_query[specials, :]
        grad_copy(i).start()

        @pl.when(i == 0)
        def _():
            units_group_start(left_copy, r.lefts, r.lefts_arrived, r.lefts_out, r.lefts_group, 0)

    units_node_start(r.lefts_out, r.lefts_group, r.lefts_node, 0)

    row_ids = lax.broadcasted_iota(jnp.int32, (block, 1), 0)
    halved = jnp.where((row_ids >= special) & (row_ids < special + 2), 0.5, 1.0)
    r.late_rows[...] = jnp.zeros_like(r.late_rows)

    @pl.loop(0, images)
    def _(i):
        grad_copy(i).wait()
        base = pl.multiple_of(i * block, 16)
        at = pl.ds(base, block)
        specials = pl.ds(pl.multiple_of(base + special, 8), 2)
        r.grad_query[specials, :] += r.grad_arrived[i, block : block + 2, 0:width]
        query_part = r.grad_query[at, :].astype(BF16).astype(F32) * halved
        r.grad_qkv[at, 0:width] = query_part.astype(BF16)
        r.late_rows[2:3, :] += jnp.sum(query_part, axis=0, keepdims=True)
        rest = (r.grad_own[i, 0:block, :] + r.grad_arrived[i, 0:block, :]).astype(BF16)
        rest = rest.astype(F32) * halved
        r.late_rows[3:4, :] += jnp.sum(rest[:, width : 2 * width], axis=0, keepdims=True)
        r.grad_qkv[at, width : 3 * width] = rest.astype(BF16)

    back = mm_nt(r.grad_qkv[...], r.low_in[...])
    r.total[...] = back[:, 0:width]
    r.folded[...] = back[:, width : width + 2 * RANK]
    r.left_in[...] += left_of(r.hidden_one)
    left_in_copy = to_partner(r.left_in, r.left_in_arrived, 4)
    left_in_copy.start()

    left_in_copy.wait()
    pair_sum = r.left_in[...] + r.left_in_arrived[...]
    r.left_in_out[...] = jnp.concatenate(
        [pair_sum[:, 0:256], jnp.concatenate([pair_sum[:, 256:384], jnp.zeros((RANK, 128), F32)], axis=1)],
        axis=0,
    ).astype(BF16)
    chips_start(r.left_in_out, r.left_in_slots, 5)

    r.err_out[...] += mm_tn(r.attended[...], r.grad_branch[...])
    for part in range(hidden_lanes // chunk):
        lanes = slice(part * chunk, (part + 1) * chunk)
        r.err_red[lanes, :] += mm_tn(r.activated[:, lanes], r.upstream[...])
        r.err_exp[:, lanes] += mm_tn(r.hidden_two[...], r.grad_pre[:, lanes])
    left_share = units_share(r.lefts_out, r.lefts_node, r.lefts_total, 1, 3)
    r.gain_sum[...] = jnp.zeros_like(r.gain_sum)
    r.shift_sum[...] = jnp.zeros_like(r.shift_sum)

    @pl.loop(0, images)
    def _(i):
        at = pl.ds(pl.multiple_of(i * block, 16), block)
        back = normalise_back(i, small_row(0), r.xhat_one, r.scale_one, r.gain_sum, r.shift_sum)
        r.total[at, :] = (back + r.grad_middle[at, :]) * jnp.where(halved < 1.0, 2.0, 1.0)

    r.late_rows[0:1, :] = r.gain_sum[...]
    r.late_rows[1:2, :] = r.shift_sum[...]
    left_share.wait()
    inverse = 1.0 / workers
    basis_red = orthonormal(
        jnp.concatenate([r.lefts_total[part] for part in range(4)], axis=1) * inverse
    )
    basis_exp = orthonormal(r.lefts_total[4] * inverse)
    basis_out = orthonormal(r.lefts_total[5] * inverse)
    r.basis_red[...] = basis_red
    r.basis_exp[...] = basis_exp
    r.basis_out[...] = basis_out

    def right_of(basis, merged):
        both = jnp.concatenate([basis, basis - basis.astype(BF16).astype(F32)], axis=0).astype(BF16)
        product = mm(both, merged.astype(BF16))
        return product[0:RANK] + product[RANK : 2 * RANK]

    for part in range(4):
        lanes = slice(part * width, (part + 1) * width)
        r.rights[part] = right_of(basis_exp, r.err_exp[:, lanes])
    r.rights[4] = right_of(basis_red, r.err_red[...])
    r.rights[5] = right_of(basis_out, r.err_out[...])
    r.rights[6] = jnp.zeros((RANK, width), F32)
    r.rights[7] = jnp.zeros((RANK, width), F32)
    right_copy = units_pair_start(r.rights, r.rights_arrived, 5)
    for part in range(3):
        lanes = slice(part * width, (part + 1) * width)
        r.err_in[:, lanes] += mm_tn(r.hidden_one[...], r.grad_qkv[:, lanes])
    units_group_start(right_copy, r.rights, r.rights_arrived, r.rights_out, r.rights_group, 2)

    total = chips_finish(r.left_in_out, r.left_in_slots, 5)
    basis_in = orthonormal(
        jnp.concatenate([total[0:RANK], total[RANK : 2 * RANK, 0:128]], axis=1) * inverse
    )
    r.basis_in[...] = basis_in
    for part in range(3):
        lanes = slice(part * width, (part + 1) * width)
        r.right_in[part] = right_of(basis_in, r.err_in[:, lanes])
    r.right_in[3] = r.late_rows[...]
    right_in_copy = to_partner(r.right_in, r.right_in_arrived, 6)
    right_in_copy.start()
    for i in range(images):
        base = i * block
        r.mixed[:, i, :] = r.total[base : base + half, :] * r.mask_columns[i, 0:half, :]
        r.grad_special[i] = r.total[base + special : base + special + 2, :].astype(BF16)
    right_in_copy.wait()
    first = seq * 2
    r.right_in_out[...] = jnp.concatenate(
        [
            r.right_in[first] + r.right_in_arrived[first],
            r.right_in[first + 1] + r.right_in_arrived[first + 1],
        ],
        axis=0,
    ).astype(BF16)
    chips_start(r.right_in_out, r.right_in_slots, 4)
    units_node_start(r.rights_out, r.rights_group, r.rights_node, 2)
    r.grad_patch[...] = r.mixed[...].astype(BF16)

    for name in ("m_small", "m_in", "m_out", "m_exp", "m_red"):
        loads[name].wait()
    right_share = units_share(r.rights_out, r.rights_node, r.rights_total, 3, 7)
    right_share.wait()
    for part in range(4):
        r.new_f_exp[:, part * width : (part + 1) * width] = r.rights_total[part] * inverse
    r.new_f_red[...] = r.rights_total[4] * inverse
    r.new_f_out[...] = r.rights_total[5] * inverse

    def small_update(at, grad):
        momentum = DECAY * r.mom_small[at, :] + grad * inverse
        r.mom_small[at, :] = momentum
        r.new_small[at, :] = r.new_small[at, :] - RATE * momentum

    small_update(slice(4, 12), r.lefts_total[6])

    total = chips_finish(r.right_in_out, r.right_in_slots, 4)
    r.right_in_total[first] = total[0:RANK]
    r.right_in_total[first + 1] = total[RANK : 2 * RANK]
    half_units = r.right_in_total.at[pl.ds(first, 2)]
    share = to_partner(half_units, half_units, 12)
    share.start()
    share.wait()
    for part in range(3):
        r.new_f_in[:, part * width : (part + 1) * width] = r.right_in_total[part] * inverse
    small_update(slice(0, 4), r.right_in_total[3][0:4])


def store_kernel(names, targets, *all_refs):
    refs = Names()
    for name, ref in zip(names, all_refs):
        setattr(refs, name, ref)
    copies = []

    def send(source, target):
        copies.append(pltpu.make_async_copy(source, target, refs.sem.at[len(copies)]))
        copies[-1].start()

    updated = {kind + which for kind in KINDS for which in MATRICES}
    for name in targets:
        if name not in updated:
            send(getattr(refs, name), getattr(refs, "hbm_" + name))
    rows = 128
    for which in ("exp", "red", "out", "in"):
        weight, momentum, error = (getattr(refs, kind + which) for kind in KINDS)
        new_weight, new_momentum, new_error = (getattr(refs, "next_" + kind + which) for kind in KINDS)
        left_stack, right_stack = outer_product(
            getattr(refs, "basis_" + which)[...], getattr(refs, "new_f_" + which)[...]
        )
        for strip in range(weight.shape[0] // rows):
            at = slice(strip * rows, (strip + 1) * rows)
            approx = mm_tn(left_stack[:, at], right_stack)
            new_error[at, :] = error[at, :] - approx
            send(new_error.at[pl.ds(strip * rows, rows)], getattr(refs, "hbm_err_" + which).at[0, pl.ds(strip * rows, rows)])
            next_momentum = DECAY * momentum[at, :] + approx
            new_momentum[at, :] = next_momentum
            send(new_momentum.at[pl.ds(strip * rows, rows)], getattr(refs, "hbm_mom_" + which).at[pl.ds(strip * rows, rows)])
            new_weight[at, :] = weight[at, :] - RATE * next_momentum
            send(new_weight.at[pl.ds(strip * rows, rows)], getattr(refs, "hbm_new_" + which).at[pl.ds(strip * rows, rows)])
    for copy in copies:
        copy.wait()


def body(chips, groups, *args):
    args = list(args)
    for index in (0, 2):
        args[index] = jnp.transpose(args[index], (1, 0, 2))
    half, images, width = args[0].shape
    wide = args[8].shape[1]
    special = round_up(half, 8)
    block = round_up(special + 2, 16)
    rows = images * block
    out_shapes = [((half, images, width), BF16), ((images, 2, width), BF16)] * 2
    weight_shapes = [(width, 3 * width), (width, width), (width, wide), (wide, width)]
    small_shape = (args[10].shape, F32)
    out_shapes += [(shape, F32) for shape in weight_shapes] + [small_shape]
    out_shapes += [(shape, F32) for shape in weight_shapes] + [small_shape]
    out_shapes += [(shape, F32) for shape in weight_shapes]
    out_shapes += [((RANK, size), F32) for size in (3 * width, width, wide, width)]
    unit = (RANK, width)
    scratch = dict(
        raw_patch=pltpu.VMEM((half, images, width), BF16),
        raw_special=pltpu.VMEM((images, 2, width), BF16),
        raw_up=pltpu.VMEM((half, images, width), BF16),
        raw_special_up=pltpu.VMEM((images, 2, width), BF16),
        mixed=pltpu.VMEM((half, images, width), F32),
        rank=pltpu.VMEM((images, half), jnp.int32),
        count=pltpu.SMEM((images,), jnp.int32),
        folded=pltpu.VMEM((rows, 2 * RANK), F32),
        folded_red=pltpu.VMEM((RANK, rows), BF16),
        low_probs=pltpu.VMEM((HEADS // 2, 2 * KEYS, 2 * block), BF16),
        grad_probs=pltpu.VMEM((HEADS // 2, 2 * KEYS, 2 * block), F32),
        branch_sum=pltpu.VMEM((1, width), F32),
        flags=pltpu.VMEM((8, KEYS), F32),
        other_flags=pltpu.VMEM((8, KEYS), F32),
        mask_columns=pltpu.VMEM((images, 2 * KEYS, 1), F32),
        tokens=pltpu.VMEM((rows, width), F32),
        xhat_one=pltpu.VMEM((rows, width), F32),
        xhat_two=pltpu.VMEM((rows, width), F32),
        scale_one=pltpu.VMEM((rows, 1), F32),
        scale_two=pltpu.VMEM((rows, 1), F32),
        hidden_one=pltpu.VMEM((rows, width), BF16),
        hidden_two=pltpu.VMEM((rows, width), BF16),
        low_in=pltpu.VMEM((width + 2 * RANK, 3 * width), BF16),
        low_out=pltpu.VMEM((width + 2 * RANK, width), BF16),
        low_exp=pltpu.VMEM((width + 2 * RANK, wide), BF16),
        low_red=pltpu.VMEM((wide, width), BF16),
        query=pltpu.VMEM((rows, width), BF16),
        keys=pltpu.VMEM((2, images, KEYS, 2 * width), BF16),
        upstream=pltpu.VMEM((rows, width), BF16),
        probs=pltpu.VMEM((images * HEADS // 2, 2 * KEYS, 2 * block), F32),
        attended=pltpu.VMEM((rows, width), BF16),
        middle=pltpu.VMEM((rows, width), F32),
        wide=pltpu.VMEM((rows, 2 * width), F32),
        activated=pltpu.VMEM((rows, wide), BF16),
        slope=pltpu.VMEM((rows, wide), F32),
        grad_pre=pltpu.VMEM((rows, wide), BF16),
        total=pltpu.VMEM((rows, width), F32),
        gain_sum=pltpu.VMEM((1, width), F32),
        shift_sum=pltpu.VMEM((1, width), F32),
        grad_middle=pltpu.VMEM((rows, width), F32),
        grad_branch=pltpu.VMEM((rows, width), BF16),
        grad_attended=pltpu.VMEM((rows, width), BF16),
        grad_query=pltpu.VMEM((rows, width), F32),
        grad_own=pltpu.VMEM((images, KEYS, 2 * width), F32),
        grad_sent=pltpu.VMEM((images, KEYS, 2 * width), F32),
        grad_arrived=pltpu.VMEM((images, KEYS, 2 * width), F32),
        grad_qkv=pltpu.VMEM((rows, 3 * width), BF16),
        lefts=pltpu.VMEM((8,) + unit, F32),
        lefts_arrived=pltpu.VMEM((8,) + unit, F32),
        lefts_out=pltpu.VMEM((2, 2, 2 * RANK, width), BF16),
        lefts_group=pltpu.VMEM((groups, 2, 2 * RANK, width), BF16),
        lefts_node=pltpu.VMEM((chips // groups, 2, 2 * RANK, width), BF16),
        lefts_total=pltpu.VMEM((8,) + unit, F32),
        rights=pltpu.VMEM((8,) + unit, F32),
        rights_arrived=pltpu.VMEM((8,) + unit, F32),
        rights_out=pltpu.VMEM((2, 2, 2 * RANK, width), BF16),
        rights_group=pltpu.VMEM((groups, 2, 2 * RANK, width), BF16),
        rights_node=pltpu.VMEM((chips // groups, 2, 2 * RANK, width), BF16),
        rights_total=pltpu.VMEM((8,) + unit, F32),
        left_in=pltpu.VMEM(unit, F32),
        left_in_arrived=pltpu.VMEM(unit, F32),
        left_in_out=pltpu.VMEM((2 * RANK, 256), BF16),
        left_in_slots=pltpu.VMEM((chips, 2 * RANK, 256), BF16),
        right_in=pltpu.VMEM((4,) + unit, F32),
        right_in_arrived=pltpu.VMEM((4,) + unit, F32),
        right_in_out=pltpu.VMEM((2 * RANK, width), BF16),
        right_in_slots=pltpu.VMEM((chips, 2 * RANK, width), BF16),
        right_in_total=pltpu.VMEM((4,) + unit, F32),
        late_rows=pltpu.VMEM(unit, F32),
        load_sem=pltpu.SemaphoreType.DMA((len(INPUTS),)),
        pair_send=pltpu.SemaphoreType.DMA((13,)),
        pair_recv=pltpu.SemaphoreType.DMA((13,)),
        chip_send=pltpu.SemaphoreType.DMA((6, chips)),
        chip_recv=pltpu.SemaphoreType.DMA((6, chips)),
    )
    made = OUTPUTS + BASES
    made_shapes = out_shapes + [((RANK, size), F32) for size in (width, width, width, wide)]
    names = INPUTS + made + tuple(scratch)
    in_hbm = pl.BlockSpec(memory_space=pltpu.HBM)
    in_vmem = pl.BlockSpec(memory_space=pltpu.VMEM)
    results = pl.pallas_call(
        functools.partial(layer_kernel, chips, groups, images, half, names),
        out_shape=[pltpu.VMEM(shape, dtype) for shape, dtype in made_shapes],
        in_specs=[in_hbm] * len(INPUTS),
        out_specs=[in_vmem] * len(made),
        scratch_shapes=list(scratch.values()),
        compiler_params=pltpu.CompilerParams(
            collective_id=0, has_side_effects=True, vmem_limit_bytes=40 << 20
        ),
        name="layer",
    )(*args[:20], *[jnp.transpose(factor) for factor in args[20:]])
    final_shapes = [
        jax.ShapeDtypeStruct((1,) + shape if 14 <= index < 18 else shape, dtype)
        for index, (shape, dtype) in enumerate(out_shapes)
    ]
    updated = {
        "next_" + kind + which: shape
        for index, kind in enumerate(KINDS)
        for which, shape in zip(MATRICES, weight_shapes)
    }
    stored = list(
        pl.pallas_call(
            functools.partial(
                store_kernel,
                made + tuple("hbm_" + name for name in OUTPUTS) + tuple(updated) + ("sem",),
                OUTPUTS,
            ),
            out_shape=final_shapes,
            in_specs=[in_vmem] * len(made),
            out_specs=[in_hbm] * len(OUTPUTS),
            scratch_shapes=[pltpu.VMEM(shape, F32) for shape in updated.values()]
            + [pltpu.SemaphoreType.DMA((96,))],
            compiler_params=pltpu.CompilerParams(vmem_limit_bytes=24 << 20),
            name="store",
        )(*results)
    )
    for index in (0, 2):
        stored[index] = jnp.transpose(stored[index], (1, 0, 2))
    return (*stored[:18], *[jnp.transpose(factor) for factor in stored[18:]])


def solution(mesh):
    images_over = ("node", "group")
    rows_spec = P(images_over, "seq", None)
    special_spec = P(images_over, None, None)
    worker_spec = P(("seq", "node", "group"), None, None)
    whole = P()
    placed = (
        (rows_spec, special_spec) * 2
        + (P(images_over, "seq"), P(images_over))
        + (whole,) * 10
        + (worker_spec,) * 4
        + (whole,) * 4
    )
    groups = mesh.shape["group"]
    chips = mesh.shape["node"] * groups
    return jax.shard_map(
        functools.partial(body, chips, groups),
        mesh=mesh,
        in_specs=placed,
        out_specs=(rows_spec, special_spec) * 2
        + (whole,) * 10
        + (worker_spec,) * 4
        + (whole,) * 4,
        check_vma=False,
    )
```

```python
import functools
import math

import jax
import jax.numpy as jnp
from jax import lax
from jax.experimental import pallas as pl
from jax.experimental.pallas import tpu as pltpu
from jax.sharding import PartitionSpec as P

HEADS = 6
HEAD_DIM = 64
EPSILON = 1e-06
RATE = 0.1
DECAY = 0.9
RANK = 8
MESH = pl.DeviceIdType.MESH
F32 = jnp.float32
BF16 = jnp.bfloat16
INPUTS = (
    "patch_tokens",
    "special_tokens",
    "patch_upstream",
    "special_upstream",
    "patch_rank",
    "keep_count",
    "project_in",
    "project_out",
    "expand_weight",
    "reduce_weight",
    "small_params",
    "project_in_momentum",
    "project_out_momentum",
    "expand_momentum",
    "reduce_momentum",
    "small_momentum",
    "project_in_error",
    "project_out_error",
    "expand_error",
    "reduce_error",
    "project_in_factor",
    "project_out_factor",
    "expand_factor",
    "reduce_factor",
)
OUTPUTS = (
    "out_patch",
    "out_special",
    "grad_patch",
    "grad_special",
    "new_in",
    "new_out",
    "new_exp",
    "new_red",
    "new_small",
    "mom_in",
    "mom_out",
    "mom_exp",
    "mom_red",
    "mom_small",
    "err_in",
    "err_out",
    "err_exp",
    "err_red",
    "new_f_in",
    "new_f_out",
    "new_f_exp",
    "new_f_red",
)
BASES = ("basis_in", "basis_out", "basis_exp", "basis_red")
KINDS = ("new_", "mom_", "err_")
MATRICES = ("in", "out", "exp", "red")
KEYS = 128


def round_up(value, unit):
    return -(-value // unit) * unit


def mm(left_side, right_side):
    return jnp.dot(left_side, right_side, preferred_element_type=F32)


def mm_nt(left_side, right_side):
    return lax.dot_general(
        left_side, right_side, (((1,), (1,)), ((), ())), preferred_element_type=F32
    )


def mm_tn(left_side, right_side):
    return lax.dot_general(
        left_side, right_side, (((0,), (0,)), ((), ())), preferred_element_type=F32
    )


def split(value):
    high = value.astype(BF16)
    return high, (value - high.astype(F32)).astype(BF16)


def orthonormal(rows):
    row_ids = lax.broadcasted_iota(jnp.int32, (RANK, 1), 0)
    for step in range(RANK):
        own = rows[step : step + 1, :]
        dots = jnp.sum(rows * own, axis=1, keepdims=True)
        scale = lax.rsqrt(dots[step : step + 1, :] + EPSILON)
        unit = own * scale
        later = jnp.where(row_ids > step, dots * scale, 0.0)
        rows = jnp.where(row_ids == step, unit, rows - later * unit)
    return rows


def outer_product(basis, right):
    basis_high, basis_low = split(basis)
    right_high, right_low = split(right)
    left_stack = jnp.concatenate(
        [basis_high.astype(F32), basis_low.astype(F32)] * 2, axis=0
    ).astype(BF16)
    right_stack = jnp.concatenate(
        [right_high.astype(F32)] * 2 + [right_low.astype(F32)] * 2, axis=0
    ).astype(BF16)
    return left_stack, right_stack


class Names:
    pass


def layer_kernel(chips, groups, images, half, names, *all_refs):
    refs = Names()
    for name, ref in zip(names, all_refs):
        setattr(refs, name, ref)
    r = refs
    width = HEADS * HEAD_DIM
    special = round_up(half, 8)
    block = round_up(special + 2, 16)
    rows_all = images * block
    workers = 2 * chips
    seq = lax.axis_index("seq")
    node = lax.axis_index("node")
    group = lax.axis_index("group")
    chip = node * groups + group
    partner = 1 - seq

    loads = {}
    free_sems = list(range(r.load_sem.shape[0]))

    class Load:
        def __init__(self, source, target):
            self.sem_id = free_sems.pop(0)
            self.copy = pltpu.make_async_copy(source, target, r.load_sem.at[self.sem_id])
            self.copy.start()

        def wait(self):
            self.copy.wait()
            free_sems.append(self.sem_id)

    def load(name, source, target):
        loads[name] = Load(source, target)

    load("tokens", r.patch_tokens, r.raw_patch)
    load("special", r.special_tokens, r.raw_special)
    load("rank", r.patch_rank, r.rank)
    load("count", r.keep_count, r.count)
    load("small", r.small_params, r.new_small)
    load("w_in", r.project_in, r.new_in)

    load("f_in", r.project_in_factor, r.new_f_in)
    load("f_out", r.project_out_factor, r.new_f_out)
    load("f_exp", r.expand_factor, r.new_f_exp)
    load("f_red", r.reduce_factor, r.new_f_red)
    load("upstream", r.patch_upstream, r.raw_up)
    load("special_up", r.special_upstream, r.raw_special_up)
    load("e_in", r.project_in_error.at[0], r.err_in)
    load("e_exp", r.expand_error.at[0], r.err_exp)
    load("e_red", r.reduce_error.at[0], r.err_red)
    load("e_out", r.project_out_error.at[0], r.err_out)

    def load_third():
        load("w_out", r.project_out, r.new_out)
        load("w_exp", r.expand_weight, r.new_exp)
        load("w_red", r.reduce_weight, r.new_red)

    def load_last():
        load("m_small", r.small_momentum, r.mom_small)
        load("m_out", r.project_out_momentum, r.mom_out)
        load("m_exp", r.expand_momentum, r.mom_exp)
        load("m_red", r.reduce_momentum, r.mom_red)
        load("m_in", r.project_in_momentum, r.mom_in)

    barrier = pltpu.get_barrier_semaphore()
    pl.semaphore_signal(barrier, inc=1, device_id={"seq": partner}, device_id_type=MESH)

    nodes = chips // groups

    def each_chip(act):
        def row(step, first):
            for ahead in range(first, groups):
                act({"node": lax.rem(node + step, nodes), "group": lax.rem(group + ahead, groups)})

        def others(step, carry):
            row(step, 0)
            return carry

        lax.fori_loop(1, nodes, others, 0)
        row(0, 1)

    def greet(device):
        pl.semaphore_signal(barrier, inc=1, device_id=device, device_id_type=MESH)

    each_chip(greet)

    def to_partner(source, target, sem_id):
        return pltpu.make_async_remote_copy(
            src_ref=source,
            dst_ref=target,
            send_sem=r.pair_send.at[sem_id],
            recv_sem=r.pair_recv.at[sem_id],
            device_id={"seq": partner},
            device_id_type=MESH,
        )

    def remote(source, target, sem_id, device):
        return pltpu.make_async_remote_copy(
            src_ref=source,
            dst_ref=target,
            send_sem=r.stage_send.at[sem_id],
            recv_sem=r.stage_recv.at[sem_id],
            device_id=device,
            device_id_type=MESH,
        )

    def stage_finish(count, slots, sem_id):
        several = slots.at[pl.ds(0, count - 1)]
        whole = remote(several, several, sem_id, {"seq": partner})
        whole.wait_recv()
        whole.wait_send()
        if count <= 32:
            total = slots[0].astype(F32)
            for index in range(1, count):
                total = total + slots[index].astype(F32)
            return total

        def add(index, total):
            return total + slots[index].astype(F32)

        return lax.fori_loop(1, count, add, slots[0].astype(F32))

    def chips_start(source, slots, sem_id):
        slots[chip] = source[...]
        each_chip(lambda device: remote(source, slots.at[chip], sem_id, device).start())

    def chips_finish(slots, sem_id):
        return stage_finish(chips, slots, sem_id)

    def axis_start(axis, source, slots, sem_id):
        size, place = lax.axis_size(axis), lax.axis_index(axis)
        slots[place] = source[...]
        for step in range(1, size):
            device = {axis: lax.rem(place + step, size)}
            remote(source, slots.at[place], sem_id, device).start()

    def axis_finish(axis, slots, sem_id):
        return stage_finish(lax.axis_size(axis), slots, sem_id)

    loads["rank"].wait()
    loads["count"].wait()
    r.flags[...] = jnp.zeros_like(r.flags)
    for i in range(images):
        r.flags[i : i + 1, 0:half] = jnp.where(
            r.rank[i : i + 1, :] < r.count[i], 1.0, 0.0
        ).astype(F32)
    lane_ids = lax.broadcasted_iota(jnp.int32, (1, KEYS), 1)
    special_lanes = jnp.where((lane_ids >= special) & (lane_ids < special + 2), 1.0, 0.0)
    own_columns = jnp.transpose(r.flags[...] + special_lanes)
    for i in range(images):
        r.mask_columns[i, 0:KEYS, :] = own_columns[:, i : i + 1]

    small = r.new_small
    loads["small"].wait()

    def small_row(index):
        return small[index : index + 1, :]

    loads["tokens"].wait()
    loads["special"].wait()
    r.mixed[...] = r.raw_patch[...].astype(F32)
    for i in range(images):
        base = i * block
        r.tokens[base + special - 8 : base + block, :] = jnp.zeros(
            (block - special + 8, width), F32
        )
        r.tokens[base : base + half, :] = (
            r.mixed[:, i, :] * r.mask_columns[i, 0:half, :]
        )
        r.tokens[base + special : base + special + 2, :] = r.raw_special[i].astype(F32)

    def normalise(source, i, gain, shift, xhat_ref, scale_ref, hidden_ref):
        at = pl.ds(pl.multiple_of(i * block, 16), block)
        values = source[at, :]
        center = values - jnp.mean(values, axis=1, keepdims=True)
        spread = jnp.mean(center * center, axis=1, keepdims=True)
        scale = lax.rsqrt(spread + EPSILON)
        xhat = center * scale
        xhat_ref[at, :] = xhat
        scale_ref[at, :] = scale
        hidden_ref[at, :] = (xhat * gain + shift).astype(BF16)

    @pl.loop(0, images)
    def _(i):
        normalise(r.tokens, i, small_row(0), small_row(1), r.xhat_one, r.scale_one, r.hidden_one)

    loads["w_in"].wait()
    load_third()
    r.low_in[0:width, :] = r.new_in[...].astype(BF16)
    for i in range(images):
        r.keys[0, i, block:KEYS, :] = jnp.zeros((KEYS - block, 2 * width), BF16)
    for part in (1, 2, 0):
        product = mm(r.hidden_one[...], r.low_in[0:width, part * width : (part + 1) * width])
        if part == 0:
            query = (product + small_row(2)).astype(BF16).astype(F32) * (
                1.0 / math.sqrt(HEAD_DIM)
            )
            r.query[...] = query.astype(BF16)
        else:
            if part == 2:
                product = product + small_row(3)
            for i in range(images):
                r.keys[0, i, 0:block, (part - 1) * width : part * width] = product[
                    i * block : (i + 1) * block
                ].astype(BF16)
        if part == 2:
            pl.semaphore_wait(barrier, chips)
            key_copy = to_partner(r.keys.at[0], r.keys.at[1], 0)
            flag_copy = to_partner(r.flags, r.other_flags, 1)
            key_copy.start()
            flag_copy.start()

    def error_left(error_ref, factor_ref, row_start, row_count):
        return mm_nt(
            factor_ref[...].astype(BF16), error_ref[row_start : row_start + row_count, :].astype(BF16)
        )

    loads["upstream"].wait()
    loads["special_up"].wait()
    r.mixed[...] = r.raw_up[...].astype(F32)
    for i in range(images):
        base = i * block
        r.middle[base + special - 8 : base + block, :] = jnp.zeros(
            (block - special + 8, width), F32
        )
        r.middle[base : base + half, :] = r.mixed[:, i, :]
        r.middle[base + special : base + special + 2, :] = 0.5 * r.raw_special_up[i].astype(F32)
    r.lefts[6, 3:4, :] = jnp.sum(r.middle[...], axis=0, keepdims=True)
    r.upstream[...] = r.middle[...].astype(BF16)
    loads["f_in"].wait()
    loads["f_out"].wait()
    loads["f_exp"].wait()
    loads["f_red"].wait()

    def with_factor(low_ref, factor_ref):
        factor = factor_ref[...]
        low_ref[width : width + 2 * RANK, :] = jnp.concatenate(
            [factor, jnp.zeros_like(factor)], axis=0
        ).astype(BF16)

    with_factor(r.low_in, r.new_f_in)
    with_factor(r.low_out, r.new_f_out)
    with_factor(r.low_exp, r.new_f_exp)
    folded_red = mm_nt(r.new_f_red[...].astype(BF16), r.upstream[...])
    r.folded_red[...] = folded_red.astype(BF16)
    loads["e_in"].wait()
    r.left_in[...] = error_left(r.err_in, r.new_f_in, 0, width)
    loads["e_exp"].wait()
    r.lefts[4] = error_left(r.err_exp, r.new_f_exp, 0, width)
    loads["e_red"].wait()
    for part in range(4):
        r.lefts[part] = error_left(r.err_red, r.new_f_red, part * width, width)
    loads["e_out"].wait()
    r.lefts[5] = error_left(r.err_out, r.new_f_out, 0, width)

    key_copy.wait()
    flag_copy.wait()
    other_columns = jnp.transpose(r.other_flags[...])
    for i in range(images):
        r.mask_columns[i, KEYS : 2 * KEYS, :] = other_columns[:, i : i + 1]

    pair_width = 2 * HEAD_DIM
    pairs = HEADS // 2
    low_lanes = lax.broadcasted_iota(jnp.int32, (1, pair_width), 1) < HEAD_DIM

    def stacked(value):
        zero = jnp.zeros_like(value)
        return jnp.concatenate(
            [jnp.where(low_lanes, value, zero), jnp.where(low_lanes, zero, value)], axis=0
        )

    def unstacked(value):
        return jnp.where(low_lanes, value[0:block], value[block : 2 * block])

    def of_both(i, lanes):
        return jnp.concatenate([r.keys[0, i, :, lanes], r.keys[1, i, :, lanes]], axis=0)

    @pl.loop(0, images)
    def _(i):
        at = pl.ds(pl.multiple_of(i * block, 16), block)
        valid = r.mask_columns[i] > 0.5

        def lanes_of(pair, first=0):
            return slice(first + pair * pair_width, first + (pair + 1) * pair_width)

        for pair in range(pairs):
            scores = mm_nt(of_both(i, lanes_of(pair)), stacked(r.query[at, lanes_of(pair)]))
            r.probs[i * pairs + pair] = jnp.where(valid, scores, -1e30)
        for pair in range(pairs):
            scores = r.probs[i * pairs + pair]
            top = jnp.max(scores, axis=0, keepdims=True)
            weights = jnp.exp(scores - top)
            probs = weights * (1.0 / jnp.sum(weights, axis=0, keepdims=True))
            r.probs[i * pairs + pair] = probs
            r.low_probs[pair] = probs.astype(BF16)
        for pair in range(pairs):
            mixed = mm_tn(r.low_probs[pair], of_both(i, lanes_of(pair, width)))
            r.attended[at, lanes_of(pair)] = unstacked(mixed).astype(BF16)

    loads["w_out"].wait()
    load_last()
    r.low_out[0:width, :] = r.new_out[...].astype(BF16)
    r.middle[...] = r.tokens[...] + mm(r.attended[...], r.low_out[0:width, :]) + small_row(4)

    @pl.loop(0, images)
    def _(i):
        normalise(r.middle, i, small_row(5), small_row(6), r.xhat_two, r.scale_two, r.hidden_two)

    strip = 64
    chunk = 2 * width
    hidden_lanes = r.low_exp.shape[1]
    loads["w_exp"].wait()
    r.low_exp[0:width, :] = r.new_exp[...].astype(BF16)
    loads["w_red"].wait()
    r.low_red[...] = r.new_red[...].astype(BF16)
    bias_rows = chunk // width
    part_lanes = r.wide.shape[2]
    parts = hidden_lanes // part_lanes
    bias_one = jnp.concatenate([small_row(8 + index) for index in range(hidden_lanes // width)], axis=1)
    r.total[...] = r.middle[...] + small_row(7)

    def lanes_at(part, count=1):
        return slice(part * part_lanes, (part + count) * part_lanes)

    def expand(part):
        r.wide[part % 2] = mm(r.hidden_two[...], r.low_exp[0:width, lanes_at(part)])

    def activate(part):
        for index in range(rows_all // strip):
            at = slice(index * strip, (index + 1) * strip)
            pre = r.wide[part % 2, at, :] + bias_one[:, lanes_at(part)]
            normal = 0.5 + 0.5 * lax.erf(pre * (1.0 / math.sqrt(2.0)))
            density = jnp.exp(-0.5 * pre * pre) * (1.0 / math.sqrt(2.0 * math.pi))
            r.activated[at, lanes_at(part)] = (pre * normal).astype(BF16)
            r.slope[at, lanes_at(part)] = normal + pre * density

    def contract(part):
        lanes = lanes_at(part, 2)
        r.total[...] += mm(r.activated[:, lanes], r.low_red[lanes, :])

    expand(0)
    for part in range(parts):
        if part + 1 < parts:
            expand(part + 1)
        activate(part)
        if part >= 2 and part % 2 == 0:
            contract(part - 2)
    contract(parts - 2)
    for i in range(images):
        base = i * block
        r.mixed[:, i, :] = r.total[base : base + half, :]
        r.out_special[i] = r.total[base + special : base + special + 2, :].astype(BF16)

    r.out_patch[...] = r.mixed[...].astype(BF16)

    for part in range(4):
        lanes = slice(part * width, (part + 1) * width)
        r.lefts[part] += mm(r.folded_red[...], r.activated[:, lanes])
    for part in range(hidden_lanes // chunk):
        lanes = slice(part * chunk, (part + 1) * chunk)
        grad_act = mm_nt(r.upstream[...], r.low_red[lanes, :]).astype(BF16).astype(F32)
        grad_pre = grad_act * r.slope[:, lanes]
        r.grad_pre[:, lanes] = grad_pre.astype(BF16)
        row = jnp.sum(grad_pre, axis=0, keepdims=True)
        for index in range(bias_rows):
            first = 4 + part * bias_rows + index
            r.lefts[6, first : first + 1, :] = row[:, index * width : (index + 1) * width]
        back = mm_nt(r.grad_pre[:, lanes], r.low_exp[:, lanes])
        if part == 0:
            r.total[...] = back[:, 0:width]
            r.folded[...] = back[:, width : width + 2 * RANK]
        else:
            r.total[...] += back[:, 0:width]
            r.folded[...] += back[:, width : width + 2 * RANK]

    def left_of(hidden_ref):
        return mm_tn(r.folded[...].astype(BF16), hidden_ref[...])[0:RANK]

    r.lefts[4] += left_of(r.hidden_two)

    def normalise_back(i, gain, xhat_ref, scale_ref, gain_ref, shift_ref):
        at = pl.ds(pl.multiple_of(i * block, 16), block)
        grad = r.total[at, :]
        xhat = xhat_ref[at, :]
        gained = grad * gain
        first = jnp.mean(gained, axis=1, keepdims=True)
        second = jnp.mean(gained * xhat, axis=1, keepdims=True)
        gain_ref[...] += jnp.sum(grad * xhat, axis=0, keepdims=True)
        shift_ref[...] += jnp.sum(grad, axis=0, keepdims=True)
        return scale_ref[at, :] * (gained - first - xhat * second)

    r.gain_sum[...] = jnp.zeros_like(r.gain_sum)
    r.shift_sum[...] = jnp.zeros_like(r.shift_sum)
    r.branch_sum[...] = jnp.zeros_like(r.branch_sum)

    @pl.loop(0, images)
    def _(i):
        at = pl.ds(pl.multiple_of(i * block, 16), block)
        back = normalise_back(i, small_row(5), r.xhat_two, r.scale_two, r.gain_sum, r.shift_sum)
        grad = r.upstream[at, :].astype(F32) + back
        r.grad_middle[at, :] = grad
        low = grad.astype(BF16)
        r.grad_branch[at, :] = low
        r.branch_sum[...] += jnp.sum(low.astype(F32), axis=0, keepdims=True)

    r.lefts[6, 1:2, :] = r.gain_sum[...]
    r.lefts[6, 2:3, :] = r.shift_sum[...]
    r.lefts[6, 0:1, :] = r.branch_sum[...]
    r.lefts[7] = jnp.zeros((RANK, width), F32)
    back = mm_nt(r.grad_branch[...], r.low_out[...])
    r.grad_attended[...] = back[:, 0:width].astype(BF16)
    r.folded[...] = back[:, width : width + 2 * RANK]
    r.lefts[5] += left_of(r.attended)

    def units_pair_start(units, arrived, sem_id):
        copy = to_partner(units, arrived, sem_id)
        copy.start()
        return copy

    def units_group_start(copy, units, arrived, outgoing, slots, sem_id):
        copy.wait()
        for index in range(2):
            first = seq * 4 + 2 * index
            outgoing[0, index] = jnp.concatenate(
                [units[first] + arrived[first], units[first + 1] + arrived[first + 1]], axis=0
            ).astype(BF16)
        axis_start("group", outgoing.at[0], slots, sem_id)

    def units_node_start(outgoing, group_slots, node_slots, sem_id):
        total = axis_finish("group", group_slots, sem_id)
        outgoing[1] = total.astype(BF16)
        axis_start("node", outgoing.at[1], node_slots, sem_id + 1)

    def units_share(node_slots, result, sem_id, pair_id):
        total = axis_finish("node", node_slots, sem_id)
        for index in range(2):
            first = seq * 4 + 2 * index
            result[first] = total[index, 0:RANK]
            result[first + 1] = total[index, RANK : 2 * RANK]
        half_units = result.at[pl.ds(seq * 4, 4)]
        copy = to_partner(half_units, half_units, pair_id)
        copy.start()
        return copy

    left_copy = units_pair_start(r.lefts, r.lefts_arrived, 2)

    def grad_copy(i):
        return to_partner(r.grad_sent.at[i], r.grad_arrived.at[i], 8 + i)

    @pl.loop(0, images)
    def _(i):
        base = pl.multiple_of(i * block, 16)
        at = pl.ds(base, block)
        specials = pl.ds(pl.multiple_of(base + special, 8), 2)

        def lanes_of(pair, first=0):
            return slice(first + pair * pair_width, first + (pair + 1) * pair_width)

        for pair in range(pairs):
            grad_mixed = stacked(r.grad_attended[at, lanes_of(pair)])
            r.grad_probs[pair] = mm_nt(of_both(i, lanes_of(pair, width)), grad_mixed)
        for pair in range(pairs):
            probs = r.probs[i * pairs + pair]
            weighted = probs * r.grad_probs[pair]
            delta = jnp.sum(weighted, axis=0, keepdims=True)
            r.low_probs[pair] = (weighted - probs * delta).astype(BF16)
        for pair in range(pairs):
            grad_scores = r.low_probs[pair]
            r.grad_query[at, lanes_of(pair)] = unstacked(
                mm_tn(grad_scores, of_both(i, lanes_of(pair)))
            ) * (1.0 / math.sqrt(HEAD_DIM))
            grad_keys = mm(grad_scores, stacked(r.query[at, lanes_of(pair)]))
            r.grad_own[i, :, lanes_of(pair)] = grad_keys[0:KEYS]
            r.grad_sent[i, :, lanes_of(pair)] = grad_keys[KEYS : 2 * KEYS]
        for pair in range(pairs):
            grad_mixed = stacked(r.grad_attended[at, lanes_of(pair)])
            grad_values = mm(r.probs[i * pairs + pair].astype(BF16), grad_mixed)
            r.grad_own[i, :, lanes_of(pair, width)] = grad_values[0:KEYS]
            r.grad_sent[i, :, lanes_of(pair, width)] = grad_values[KEYS : 2 * KEYS]
        r.grad_sent[i, special : special + 2, :] = r.grad_own[i, special : special + 2, :]
        r.grad_sent[i, block : block + 2, 0:width] = r.grad_query[specials, :]
        grad_copy(i).start()

        @pl.when(i == 0)
        def _():
            units_group_start(left_copy, r.lefts, r.lefts_arrived, r.lefts_out, r.lefts_group, 0)

    units_node_start(r.lefts_out, r.lefts_group, r.lefts_node, 0)

    row_ids = lax.broadcasted_iota(jnp.int32, (block, 1), 0)
    halved = jnp.where((row_ids >= special) & (row_ids < special + 2), 0.5, 1.0)
    r.late_rows[...] = jnp.zeros_like(r.late_rows)
    r.err_out[...] += mm_tn(r.attended[...], r.grad_branch[...])
    for part in range(hidden_lanes // chunk):
        lanes = slice(part * chunk, (part + 1) * chunk)
        r.err_red[lanes, :] += mm_tn(r.activated[:, lanes], r.upstream[...])

    @pl.loop(0, images)
    def _(i):
        grad_copy(i).wait()
        base = pl.multiple_of(i * block, 16)
        at = pl.ds(base, block)
        specials = pl.ds(pl.multiple_of(base + special, 8), 2)
        r.grad_query[specials, :] += r.grad_arrived[i, block : block + 2, 0:width]
        query_part = r.grad_query[at, :].astype(BF16).astype(F32) * halved
        r.grad_qkv[at, 0:width] = query_part.astype(BF16)
        r.late_rows[2:3, :] += jnp.sum(query_part, axis=0, keepdims=True)
        rest = (r.grad_own[i, 0:block, :] + r.grad_arrived[i, 0:block, :]).astype(BF16)
        rest = rest.astype(F32) * halved
        r.late_rows[3:4, :] += jnp.sum(rest[:, width : 2 * width], axis=0, keepdims=True)
        r.grad_qkv[at, width : 3 * width] = rest.astype(BF16)

    back = mm_nt(r.grad_qkv[...], r.low_in[...])
    r.total[...] = back[:, 0:width]
    r.folded[...] = back[:, width : width + 2 * RANK]
    r.left_in[...] += left_of(r.hidden_one)
    left_in_copy = to_partner(r.left_in, r.left_in_arrived, 4)
    left_in_copy.start()
    r.gain_sum[...] = jnp.zeros_like(r.gain_sum)
    r.shift_sum[...] = jnp.zeros_like(r.shift_sum)

    @pl.loop(0, images)
    def _(i):
        at = pl.ds(pl.multiple_of(i * block, 16), block)
        back = normalise_back(i, small_row(0), r.xhat_one, r.scale_one, r.gain_sum, r.shift_sum)
        r.total[at, :] = (back + r.grad_middle[at, :]) * jnp.where(halved < 1.0, 2.0, 1.0)

    r.late_rows[0:1, :] = r.gain_sum[...]
    r.late_rows[1:2, :] = r.shift_sum[...]
    left_in_copy.wait()
    pair_sum = r.left_in[...] + r.left_in_arrived[...]
    r.left_in_out[...] = jnp.concatenate(
        [pair_sum[:, 0:256], jnp.concatenate([pair_sum[:, 256:384], jnp.zeros((RANK, 128), F32)], axis=1)],
        axis=0,
    ).astype(BF16)
    chips_start(r.left_in_out, r.left_in_slots, 5)

    left_share = units_share(r.lefts_node, r.lefts_total, 1, 3)
    for part in range(hidden_lanes // chunk):
        lanes = slice(part * chunk, (part + 1) * chunk)
        r.err_exp[:, lanes] += mm_tn(r.hidden_two[...], r.grad_pre[:, lanes])
    left_share.wait()
    inverse = 1.0 / workers
    basis_red = orthonormal(
        jnp.concatenate([r.lefts_total[part] for part in range(4)], axis=1) * inverse
    )
    basis_exp = orthonormal(r.lefts_total[4] * inverse)
    basis_out = orthonormal(r.lefts_total[5] * inverse)
    r.basis_red[...] = basis_red
    r.basis_exp[...] = basis_exp
    r.basis_out[...] = basis_out

    def right_of(basis, merged):
        both = jnp.concatenate([basis, basis - basis.astype(BF16).astype(F32)], axis=0).astype(BF16)
        product = mm(both, merged.astype(BF16))
        return product[0:RANK] + product[RANK : 2 * RANK]

    for part in range(4):
        lanes = slice(part * width, (part + 1) * width)
        r.rights[part] = right_of(basis_exp, r.err_exp[:, lanes])
    r.rights[4] = right_of(basis_red, r.err_red[...])
    r.rights[5] = right_of(basis_out, r.err_out[...])
    r.rights[6] = jnp.zeros((RANK, width), F32)
    r.rights[7] = jnp.zeros((RANK, width), F32)
    right_copy = units_pair_start(r.rights, r.rights_arrived, 5)
    for part in range(3):
        lanes = slice(part * width, (part + 1) * width)
        r.err_in[:, lanes] += mm_tn(r.hidden_one[...], r.grad_qkv[:, lanes])
    units_group_start(right_copy, r.rights, r.rights_arrived, r.rights_out, r.rights_group, 2)

    total = chips_finish(r.left_in_slots, 5)
    basis_in = orthonormal(
        jnp.concatenate([total[0:RANK], total[RANK : 2 * RANK, 0:128]], axis=1) * inverse
    )
    r.basis_in[...] = basis_in
    for part in range(3):
        lanes = slice(part * width, (part + 1) * width)
        r.right_in[part] = right_of(basis_in, r.err_in[:, lanes])
    r.right_in[3] = r.late_rows[...]
    right_in_copy = to_partner(r.right_in, r.right_in_arrived, 6)
    right_in_copy.start()
    for i in range(images):
        base = i * block
        r.mixed[:, i, :] = r.total[base : base + half, :] * r.mask_columns[i, 0:half, :]
        r.grad_special[i] = r.total[base + special : base + special + 2, :].astype(BF16)
    right_in_copy.wait()
    first = seq * 2
    r.right_in_out[...] = jnp.concatenate(
        [
            r.right_in[first] + r.right_in_arrived[first],
            r.right_in[first + 1] + r.right_in_arrived[first + 1],
        ],
        axis=0,
    ).astype(BF16)
    chips_start(r.right_in_out, r.right_in_slots, 4)
    units_node_start(r.rights_out, r.rights_group, r.rights_node, 2)
    r.grad_patch[...] = r.mixed[...].astype(BF16)

    for name in ("m_small", "m_in", "m_out", "m_exp", "m_red"):
        loads[name].wait()
    right_share = units_share(r.rights_node, r.rights_total, 3, 7)
    right_share.wait()
    for part in range(4):
        r.new_f_exp[:, part * width : (part + 1) * width] = r.rights_total[part] * inverse
    r.new_f_red[...] = r.rights_total[4] * inverse
    r.new_f_out[...] = r.rights_total[5] * inverse

    def small_update(at, grad):
        momentum = DECAY * r.mom_small[at, :] + grad * inverse
        r.mom_small[at, :] = momentum
        r.new_small[at, :] = r.new_small[at, :] - RATE * momentum

    small_update(slice(4, 12), r.lefts_total[6])

    total = chips_finish(r.right_in_slots, 4)
    r.right_in_total[first] = total[0:RANK]
    r.right_in_total[first + 1] = total[RANK : 2 * RANK]
    half_units = r.right_in_total.at[pl.ds(first, 2)]
    share = to_partner(half_units, half_units, 12)
    share.start()
    share.wait()
    for part in range(3):
        r.new_f_in[:, part * width : (part + 1) * width] = r.right_in_total[part] * inverse
    small_update(slice(0, 4), r.right_in_total[3][0:4])


def store_kernel(names, targets, *all_refs):
    refs = Names()
    for name, ref in zip(names, all_refs):
        setattr(refs, name, ref)
    waits = []

    def send(name, at=None):
        source, target = getattr(refs, "next_" + name, None), getattr(refs, "hbm_" + name)
        if source is None:
            source = getattr(refs, name)
        if len(target.shape) > len(source.shape):
            target = target.at[0]
        sem = refs.sem.at[targets.index(name)]
        if at is None or at.start == 0:
            waits.append(pltpu.make_async_copy(source, target, sem))
        if at is not None:
            at = pl.ds(at.start, at.stop - at.start)
            source, target = source.at[at], target.at[at]
        pltpu.make_async_copy(source, target, sem).start()

    updated = {kind + which for kind in KINDS for which in MATRICES}
    for name in targets:
        if name not in updated:
            send(name)
    for which, rows in (("exp", 128), ("red", 384), ("out", 384), ("in", 128)):
        weight, momentum, error = (getattr(refs, kind + which) for kind in KINDS)
        new_weight, new_momentum, new_error = (getattr(refs, "next_" + kind + which) for kind in KINDS)
        left_stack, right_stack = outer_product(
            getattr(refs, "basis_" + which)[...], getattr(refs, "new_f_" + which)[...]
        )
        for strip in range(weight.shape[0] // rows):
            at = slice(strip * rows, (strip + 1) * rows)
            approx = mm_tn(left_stack[:, at], right_stack)
            new_error[at, :] = error[at, :] - approx
            send("err_" + which, at)
            next_momentum = DECAY * momentum[at, :] + approx
            new_momentum[at, :] = next_momentum
            send("mom_" + which, at)
            new_weight[at, :] = weight[at, :] - RATE * next_momentum
            send("new_" + which, at)
    for copy in waits:
        copy.wait()


def body(chips, groups, *args):
    args = list(args)
    for index in (0, 2):
        args[index] = jnp.transpose(args[index], (1, 0, 2))
    half, images, width = args[0].shape
    wide = args[8].shape[1]
    special = round_up(half, 8)
    block = round_up(special + 2, 16)
    rows = images * block
    out_shapes = [((half, images, width), BF16), ((images, 2, width), BF16)] * 2
    weight_shapes = [(width, 3 * width), (width, width), (width, wide), (wide, width)]
    small_shape = (args[10].shape, F32)
    out_shapes += [(shape, F32) for shape in weight_shapes] + [small_shape]
    out_shapes += [(shape, F32) for shape in weight_shapes] + [small_shape]
    out_shapes += [(shape, F32) for shape in weight_shapes]
    out_shapes += [((RANK, size), F32) for size in (3 * width, width, wide, width)]
    unit = (RANK, width)
    scratch = dict(
        raw_patch=pltpu.VMEM((half, images, width), BF16),
        raw_special=pltpu.VMEM((images, 2, width), BF16),
        raw_up=pltpu.VMEM((half, images, width), BF16),
        raw_special_up=pltpu.VMEM((images, 2, width), BF16),
        mixed=pltpu.VMEM((half, images, width), F32),
        rank=pltpu.VMEM((images, half), jnp.int32),
        count=pltpu.SMEM((images,), jnp.int32),
        folded=pltpu.VMEM((rows, 2 * RANK), F32),
        folded_red=pltpu.VMEM((RANK, rows), BF16),
        low_probs=pltpu.VMEM((HEADS // 2, 2 * KEYS, 2 * block), BF16),
        grad_probs=pltpu.VMEM((HEADS // 2, 2 * KEYS, 2 * block), F32),
        branch_sum=pltpu.VMEM((1, width), F32),
        flags=pltpu.VMEM((8, KEYS), F32),
        other_flags=pltpu.VMEM((8, KEYS), F32),
        mask_columns=pltpu.VMEM((images, 2 * KEYS, 1), F32),
        tokens=pltpu.VMEM((rows, width), F32),
        xhat_one=pltpu.VMEM((rows, width), F32),
        xhat_two=pltpu.VMEM((rows, width), F32),
        scale_one=pltpu.VMEM((rows, 1), F32),
        scale_two=pltpu.VMEM((rows, 1), F32),
        hidden_one=pltpu.VMEM((rows, width), BF16),
        hidden_two=pltpu.VMEM((rows, width), BF16),
        low_in=pltpu.VMEM((width + 2 * RANK, 3 * width), BF16),
        low_out=pltpu.VMEM((width + 2 * RANK, width), BF16),
        low_exp=pltpu.VMEM((width + 2 * RANK, wide), BF16),
        low_red=pltpu.VMEM((wide, width), BF16),
        query=pltpu.VMEM((rows, width), BF16),
        keys=pltpu.VMEM((2, images, KEYS, 2 * width), BF16),
        upstream=pltpu.VMEM((rows, width), BF16),
        probs=pltpu.VMEM((images * HEADS // 2, 2 * KEYS, 2 * block), F32),
        attended=pltpu.VMEM((rows, width), BF16),
        middle=pltpu.VMEM((rows, width), F32),
        wide=pltpu.VMEM((2, rows, 256), F32),
        activated=pltpu.VMEM((rows, wide), BF16),
        slope=pltpu.VMEM((rows, wide), F32),
        grad_pre=pltpu.VMEM((rows, wide), BF16),
        total=pltpu.VMEM((rows, width), F32),
        gain_sum=pltpu.VMEM((1, width), F32),
        shift_sum=pltpu.VMEM((1, width), F32),
        grad_middle=pltpu.VMEM((rows, width), F32),
        grad_branch=pltpu.VMEM((rows, width), BF16),
        grad_attended=pltpu.VMEM((rows, width), BF16),
        grad_query=pltpu.VMEM((rows, width), F32),
        grad_own=pltpu.VMEM((images, KEYS, 2 * width), F32),
        grad_sent=pltpu.VMEM((images, KEYS, 2 * width), F32),
        grad_arrived=pltpu.VMEM((images, KEYS, 2 * width), F32),
        grad_qkv=pltpu.VMEM((rows, 3 * width), BF16),
        lefts=pltpu.VMEM((8,) + unit, F32),
        lefts_arrived=pltpu.VMEM((8,) + unit, F32),
        lefts_out=pltpu.VMEM((2, 2, 2 * RANK, width), BF16),
        lefts_group=pltpu.VMEM((groups, 2, 2 * RANK, width), BF16),
        lefts_node=pltpu.VMEM((chips // groups, 2, 2 * RANK, width), BF16),
        lefts_total=pltpu.VMEM((8,) + unit, F32),
        rights=pltpu.VMEM((8,) + unit, F32),
        rights_arrived=pltpu.VMEM((8,) + unit, F32),
        rights_out=pltpu.VMEM((2, 2, 2 * RANK, width), BF16),
        rights_group=pltpu.VMEM((groups, 2, 2 * RANK, width), BF16),
        rights_node=pltpu.VMEM((chips // groups, 2, 2 * RANK, width), BF16),
        rights_total=pltpu.VMEM((8,) + unit, F32),
        left_in=pltpu.VMEM(unit, F32),
        left_in_arrived=pltpu.VMEM(unit, F32),
        left_in_out=pltpu.VMEM((2 * RANK, 256), BF16),
        left_in_slots=pltpu.VMEM((chips, 2 * RANK, 256), BF16),
        right_in=pltpu.VMEM((4,) + unit, F32),
        right_in_arrived=pltpu.VMEM((4,) + unit, F32),
        right_in_out=pltpu.VMEM((2 * RANK, width), BF16),
        right_in_slots=pltpu.VMEM((chips, 2 * RANK, width), BF16),
        right_in_total=pltpu.VMEM((4,) + unit, F32),
        late_rows=pltpu.VMEM(unit, F32),
        load_sem=pltpu.SemaphoreType.DMA((16,)),
        pair_send=pltpu.SemaphoreType.DMA((13,)),
        pair_recv=pltpu.SemaphoreType.DMA((13,)),
        stage_send=pltpu.SemaphoreType.DMA((6,)),
        stage_recv=pltpu.SemaphoreType.DMA((6,)),
    )
    made = OUTPUTS + BASES
    made_shapes = out_shapes + [((RANK, size), F32) for size in (width, width, width, wide)]
    names = INPUTS + made + tuple(scratch)
    in_hbm = pl.BlockSpec(memory_space=pltpu.HBM)
    in_vmem = pl.BlockSpec(memory_space=pltpu.VMEM)
    results = pl.pallas_call(
        functools.partial(layer_kernel, chips, groups, images, half, names),
        out_shape=[pltpu.VMEM(shape, dtype) for shape, dtype in made_shapes],
        in_specs=[in_hbm] * len(INPUTS),
        out_specs=[in_vmem] * len(made),
        scratch_shapes=list(scratch.values()),
        compiler_params=pltpu.CompilerParams(
            collective_id=0, has_side_effects=True, vmem_limit_bytes=40 << 20
        ),
        name="layer",
    )(*args[:20], *[jnp.transpose(factor) for factor in args[20:]])
    final_shapes = [
        jax.ShapeDtypeStruct((1,) + shape if 14 <= index < 18 else shape, dtype)
        for index, (shape, dtype) in enumerate(out_shapes)
    ]
    updated = {
        "next_" + kind + which: shape
        for index, kind in enumerate(KINDS)
        for which, shape in zip(MATRICES, weight_shapes)
    }
    stored = list(
        pl.pallas_call(
            functools.partial(
                store_kernel,
                made + tuple("hbm_" + name for name in OUTPUTS) + tuple(updated) + ("sem",),
                OUTPUTS,
            ),
            out_shape=final_shapes,
            in_specs=[in_vmem] * len(made),
            out_specs=[in_hbm] * len(OUTPUTS),
            scratch_shapes=[pltpu.VMEM(shape, F32) for shape in updated.values()]
            + [pltpu.SemaphoreType.DMA((len(OUTPUTS),))],
            compiler_params=pltpu.CompilerParams(vmem_limit_bytes=24 << 20),
            name="store",
        )(*results)
    )
    for index in (0, 2):
        stored[index] = jnp.transpose(stored[index], (1, 0, 2))
    return (*stored[:18], *[jnp.transpose(factor) for factor in stored[18:]])


def solution(mesh):
    images_over = ("node", "group")
    rows_spec = P(images_over, "seq", None)
    special_spec = P(images_over, None, None)
    worker_spec = P(("seq", "node", "group"), None, None)
    whole = P()
    placed = (
        (rows_spec, special_spec) * 2
        + (P(images_over, "seq"), P(images_over))
        + (whole,) * 10
        + (worker_spec,) * 4
        + (whole,) * 4
    )
    groups = mesh.shape["group"]
    chips = mesh.shape["node"] * groups
    return jax.shard_map(
        functools.partial(body, chips, groups),
        mesh=mesh,
        in_specs=placed,
        out_specs=(rows_spec, special_spec) * 2
        + (whole,) * 10
        + (worker_spec,) * 4
        + (whole,) * 4,
        check_vma=False,
    )
```

```python
import functools
import math

import jax
import jax.numpy as jnp
from jax import lax
from jax.experimental import pallas as pl
from jax.experimental.pallas import tpu as pltpu
from jax.sharding import PartitionSpec as P

HEADS = 6
HEAD_DIM = 64
EPSILON = 1e-06
RATE = 0.1
DECAY = 0.9
RANK = 8
MESH = pl.DeviceIdType.MESH
F32 = jnp.float32
BF16 = jnp.bfloat16
INPUTS = (
    "patch_tokens",
    "special_tokens",
    "patch_upstream",
    "special_upstream",
    "patch_rank",
    "keep_count",
    "project_in",
    "project_out",
    "expand_weight",
    "reduce_weight",
    "small_params",
    "project_in_momentum",
    "project_out_momentum",
    "expand_momentum",
    "reduce_momentum",
    "small_momentum",
    "project_in_error",
    "project_out_error",
    "expand_error",
    "reduce_error",
    "project_in_factor",
    "project_out_factor",
    "expand_factor",
    "reduce_factor",
)
OUTPUTS = (
    "out_patch",
    "out_special",
    "grad_patch",
    "grad_special",
    "new_in",
    "new_out",
    "new_exp",
    "new_red",
    "new_small",
    "mom_in",
    "mom_out",
    "mom_exp",
    "mom_red",
    "mom_small",
    "err_in",
    "err_out",
    "err_exp",
    "err_red",
    "new_f_in",
    "new_f_out",
    "new_f_exp",
    "new_f_red",
)
BASES = ("basis_in", "basis_out", "basis_exp", "basis_red")
KINDS = ("new_", "mom_", "err_")
MATRICES = ("in", "out", "exp", "red")
KEYS = 128


def round_up(value, unit):
    return -(-value // unit) * unit


def mm(left_side, right_side):
    return jnp.dot(left_side, right_side, preferred_element_type=F32)


def mm_nt(left_side, right_side):
    return lax.dot_general(
        left_side, right_side, (((1,), (1,)), ((), ())), preferred_element_type=F32
    )


def mm_tn(left_side, right_side):
    return lax.dot_general(
        left_side, right_side, (((0,), (0,)), ((), ())), preferred_element_type=F32
    )


def split(value):
    high = value.astype(BF16)
    return high, (value - high.astype(F32)).astype(BF16)


def orthonormal(rows):
    row_ids = lax.broadcasted_iota(jnp.int32, (RANK, 1), 0)
    for step in range(RANK):
        own = rows[step : step + 1, :]
        dots = jnp.sum(rows * own, axis=1, keepdims=True)
        scale = lax.rsqrt(dots[step : step + 1, :] + EPSILON)
        unit = own * scale
        later = jnp.where(row_ids > step, dots * scale, 0.0)
        rows = jnp.where(row_ids == step, unit, rows - later * unit)
    return rows


def outer_product(basis, right):
    basis_high, basis_low = split(basis)
    right_high, right_low = split(right)
    left_stack = jnp.concatenate(
        [basis_high.astype(F32), basis_low.astype(F32)] * 2, axis=0
    ).astype(BF16)
    right_stack = jnp.concatenate(
        [right_high.astype(F32)] * 2 + [right_low.astype(F32)] * 2, axis=0
    ).astype(BF16)
    return left_stack, right_stack


class Names:
    pass


def layer_kernel(chips, groups, images, half, names, *all_refs):
    refs = Names()
    for name, ref in zip(names, all_refs):
        setattr(refs, name, ref)
    r = refs
    r.grad_middle, r.grad_query = r.tokens, r.middle
    width = HEADS * HEAD_DIM
    special = round_up(half, 8)
    block = round_up(special + 2, 16)
    rows_all = images * block
    workers = 2 * chips
    seq = lax.axis_index("seq")
    node = lax.axis_index("node")
    group = lax.axis_index("group")
    chip = node * groups + group
    partner = 1 - seq

    loads = {}
    free_sems = list(range(r.load_sem.shape[0]))

    class Load:
        def __init__(self, source, target):
            self.sem_id = free_sems.pop(0)
            self.copy = pltpu.make_async_copy(source, target, r.load_sem.at[self.sem_id])
            self.copy.start()

        def wait(self):
            self.copy.wait()
            free_sems.append(self.sem_id)

    def load(name, source, target):
        loads[name] = Load(source, target)

    load("tokens", r.patch_tokens, r.raw_patch)
    load("special", r.special_tokens, r.raw_special)
    load("rank", r.patch_rank, r.rank)
    load("count", r.keep_count, r.count)
    load("small", r.small_params, r.new_small)
    load("w_in", r.project_in, r.new_in)

    load("f_in", r.project_in_factor, r.new_f_in)
    load("f_out", r.project_out_factor, r.new_f_out)
    load("f_exp", r.expand_factor, r.new_f_exp)
    load("f_red", r.reduce_factor, r.new_f_red)
    load("upstream", r.patch_upstream, r.raw_up)
    load("special_up", r.special_upstream, r.raw_special_up)
    load("e_in", r.project_in_error.at[0], r.err_in)
    load("e_exp", r.expand_error.at[0], r.err_exp)
    load("e_red", r.reduce_error.at[0], r.err_red)
    load("e_out", r.project_out_error.at[0], r.err_out)

    def load_third():
        load("w_out", r.project_out, r.new_out)
        load("w_exp", r.expand_weight, r.new_exp)
        load("w_red", r.reduce_weight, r.new_red)

    def load_last():
        load("m_small", r.small_momentum, r.mom_small)
        load("m_out", r.project_out_momentum, r.mom_out)
        load("m_exp", r.expand_momentum, r.mom_exp)
        load("m_red", r.reduce_momentum, r.mom_red)
        load("m_in", r.project_in_momentum, r.mom_in)

    barrier = pltpu.get_barrier_semaphore()
    pl.semaphore_signal(barrier, inc=1, device_id={"seq": partner}, device_id_type=MESH)

    nodes = chips // groups

    def each_chip(act):
        def row(step, first):
            for ahead in range(first, groups):
                act({"node": lax.rem(node + step, nodes), "group": lax.rem(group + ahead, groups)})

        def others(step, carry):
            row(step, 0)
            return carry

        lax.fori_loop(1, nodes, others, 0)
        row(0, 1)

    def greet(device):
        pl.semaphore_signal(barrier, inc=1, device_id=device, device_id_type=MESH)

    each_chip(greet)

    def to_partner(source, target, sem_id):
        return pltpu.make_async_remote_copy(
            src_ref=source,
            dst_ref=target,
            send_sem=r.pair_send.at[sem_id],
            recv_sem=r.pair_recv.at[sem_id],
            device_id={"seq": partner},
            device_id_type=MESH,
        )

    def remote(source, target, sem_id, device):
        return pltpu.make_async_remote_copy(
            src_ref=source,
            dst_ref=target,
            send_sem=r.stage_send.at[sem_id],
            recv_sem=r.stage_recv.at[sem_id],
            device_id=device,
            device_id_type=MESH,
        )

    def stage_finish(count, slots, sem_id):
        several = slots.at[pl.ds(0, count - 1)]
        whole = remote(several, several, sem_id, {"seq": partner})
        whole.wait_recv()
        whole.wait_send()
        if count <= 32:
            total = slots[0].astype(F32)
            for index in range(1, count):
                total = total + slots[index].astype(F32)
            return total

        def add(index, total):
            return total + slots[index].astype(F32)

        return lax.fori_loop(1, count, add, slots[0].astype(F32))

    def chips_start(source, slots, sem_id):
        slots[chip] = source[...]
        each_chip(lambda device: remote(source, slots.at[chip], sem_id, device).start())

    def chips_finish(slots, sem_id):
        return stage_finish(chips, slots, sem_id)

    def axis_start(axis, source, slots, sem_id):
        size, place = lax.axis_size(axis), lax.axis_index(axis)
        slots[place] = source[...]
        for step in range(1, size):
            device = {axis: lax.rem(place + step, size)}
            remote(source, slots.at[place], sem_id, device).start()

    def axis_finish(axis, slots, sem_id):
        return stage_finish(lax.axis_size(axis), slots, sem_id)

    loads["rank"].wait()
    loads["count"].wait()
    r.flags[...] = jnp.zeros_like(r.flags)
    for i in range(images):
        r.flags[i : i + 1, 0:half] = jnp.where(
            r.rank[i : i + 1, :] < r.count[i], 1.0, 0.0
        ).astype(F32)
    lane_ids = lax.broadcasted_iota(jnp.int32, (1, KEYS), 1)
    special_lanes = jnp.where((lane_ids >= special) & (lane_ids < special + 2), 1.0, 0.0)
    own_columns = jnp.transpose(r.flags[...] + special_lanes)
    for i in range(images):
        r.mask_columns[i, 0:KEYS, :] = own_columns[:, i : i + 1]

    small = r.new_small
    loads["small"].wait()

    def small_row(index):
        return small[index : index + 1, :]

    loads["tokens"].wait()
    loads["special"].wait()
    r.mixed[...] = r.raw_patch[...].astype(F32)
    for i in range(images):
        base = i * block
        r.tokens[base + special - 8 : base + block, :] = jnp.zeros(
            (block - special + 8, width), F32
        )
        r.tokens[base : base + half, :] = (
            r.mixed[:, i, :] * r.mask_columns[i, 0:half, :]
        )
        r.tokens[base + special : base + special + 2, :] = r.raw_special[i].astype(F32)

    def normalise(source, i, gain, shift, xhat_ref, scale_ref, hidden_ref):
        at = pl.ds(pl.multiple_of(i * block, 16), block)
        values = source[at, :]
        center = values - jnp.mean(values, axis=1, keepdims=True)
        spread = jnp.mean(center * center, axis=1, keepdims=True)
        scale = lax.rsqrt(spread + EPSILON)
        xhat = center * scale
        xhat_ref[at, :] = xhat
        scale_ref[at, :] = scale
        hidden_ref[at, :] = (xhat * gain + shift).astype(BF16)

    @pl.loop(0, images)
    def _(i):
        normalise(r.tokens, i, small_row(0), small_row(1), r.xhat_one, r.scale_one, r.hidden_one)

    loads["w_in"].wait()
    r.low_in[0:width, :] = r.new_in[...].astype(BF16)
    for i in range(images):
        r.keys[0, i, block:KEYS, :] = jnp.zeros((KEYS - block, 2 * width), BF16)
    product = mm(r.hidden_one[...], r.low_in[0:width, width : 3 * width])
    for i in range(images):
        at = slice(i * block, (i + 1) * block)
        r.keys[0, i, 0:block, 0:width] = product[at, 0:width].astype(BF16)
        r.keys[0, i, 0:block, width : 2 * width] = (
            product[at, width : 2 * width] + small_row(3)
        ).astype(BF16)
    pl.semaphore_wait(barrier, chips)
    key_copy = to_partner(r.keys.at[0], r.keys.at[1], 0)
    flag_copy = to_partner(r.flags, r.other_flags, 1)
    key_copy.start()
    flag_copy.start()
    product = mm(r.hidden_one[...], r.low_in[0:width, 0:width])
    query = (product + small_row(2)).astype(BF16).astype(F32) * (1.0 / math.sqrt(HEAD_DIM))
    r.query[...] = query.astype(BF16)

    def error_left(error_ref, factor_ref, row_start, row_count):
        return mm_nt(
            factor_ref[...].astype(BF16), error_ref[row_start : row_start + row_count, :].astype(BF16)
        )

    loads["upstream"].wait()
    loads["special_up"].wait()
    r.mixed[...] = r.raw_up[...].astype(F32)
    for i in range(images):
        base = i * block
        r.middle[base + special - 8 : base + block, :] = jnp.zeros(
            (block - special + 8, width), F32
        )
        r.middle[base : base + half, :] = r.mixed[:, i, :]
        r.middle[base + special : base + special + 2, :] = 0.5 * r.raw_special_up[i].astype(F32)
    r.lefts[6, 3:4, :] = jnp.sum(r.middle[...], axis=0, keepdims=True)
    r.upstream[...] = r.middle[...].astype(BF16)
    loads["f_in"].wait()
    loads["f_out"].wait()
    loads["f_exp"].wait()
    loads["f_red"].wait()

    def with_factor(low_ref, factor_ref):
        factor = factor_ref[...]
        low_ref[width : width + 2 * RANK, :] = jnp.concatenate(
            [factor, jnp.zeros_like(factor)], axis=0
        ).astype(BF16)

    with_factor(r.low_in, r.new_f_in)
    with_factor(r.low_out, r.new_f_out)
    with_factor(r.low_exp, r.new_f_exp)
    folded_red = mm_nt(r.new_f_red[...].astype(BF16), r.upstream[...])
    r.folded_red[...] = folded_red.astype(BF16)
    loads["e_in"].wait()
    r.left_in[...] = error_left(r.err_in, r.new_f_in, 0, width)
    loads["e_exp"].wait()
    r.lefts[4] = error_left(r.err_exp, r.new_f_exp, 0, width)
    load_third()
    loads["e_red"].wait()
    for part in range(4):
        r.lefts[part] = error_left(r.err_red, r.new_f_red, part * width, width)
    loads["e_out"].wait()
    r.lefts[5] = error_left(r.err_out, r.new_f_out, 0, width)

    key_copy.wait()
    flag_copy.wait()
    other_columns = jnp.transpose(r.other_flags[...])
    for i in range(images):
        r.mask_columns[i, KEYS : 2 * KEYS, :] = other_columns[:, i : i + 1]

    pair_width = 2 * HEAD_DIM
    pairs = HEADS // 2
    low_lanes = lax.broadcasted_iota(jnp.int32, (1, pair_width), 1) < HEAD_DIM

    def stacked(value):
        zero = jnp.zeros_like(value)
        return jnp.concatenate(
            [jnp.where(low_lanes, value, zero), jnp.where(low_lanes, zero, value)], axis=0
        )

    def unstacked(value):
        return jnp.where(low_lanes, value[0:block], value[block : 2 * block])

    def of_both(i, lanes):
        return jnp.concatenate([r.keys[0, i, :, lanes], r.keys[1, i, :, lanes]], axis=0)

    together = 2

    def lanes_of(pair, first=0):
        return slice(first + pair * pair_width, first + (pair + 1) * pair_width)

    def image_rows(i):
        return pl.ds(pl.multiple_of(i * block, 16), block)

    tasks = [(ahead, pair) for ahead in range(together) for pair in range(pairs)]

    @pl.loop(0, images // together)
    def _(step):
        for ahead, pair in tasks:
            i = step * together + ahead
            queries = stacked(r.query[image_rows(i), lanes_of(pair)])
            scores = mm_nt(of_both(i, lanes_of(pair)), queries)
            r.probs[i * pairs + pair] = jnp.where(r.mask_columns[i] > 0.5, scores, -1e30)
        for task, (ahead, pair) in enumerate(tasks):
            i = step * together + ahead
            scores = r.probs[i * pairs + pair]
            top = jnp.max(scores, axis=0, keepdims=True)
            weights = jnp.exp(scores - top)
            probs = weights * (1.0 / jnp.sum(weights, axis=0, keepdims=True))
            r.probs[i * pairs + pair] = probs
            r.low_probs[task] = probs.astype(BF16)
        for task, (ahead, pair) in enumerate(tasks):
            i = step * together + ahead
            mixed = mm_tn(r.low_probs[task], of_both(i, lanes_of(pair, width)))
            r.attended[image_rows(i), lanes_of(pair)] = unstacked(mixed).astype(BF16)

    loads["w_out"].wait()
    load_last()
    r.low_out[0:width, :] = r.new_out[...].astype(BF16)
    r.middle[...] = r.tokens[...] + mm(r.attended[...], r.low_out[0:width, :]) + small_row(4)

    @pl.loop(0, images)
    def _(i):
        normalise(r.middle, i, small_row(5), small_row(6), r.xhat_two, r.scale_two, r.hidden_two)

    strip = 64
    chunk = 2 * width
    hidden_lanes = r.low_exp.shape[1]
    loads["w_exp"].wait()
    r.low_exp[0:width, :] = r.new_exp[...].astype(BF16)
    loads["w_red"].wait()
    r.low_red[...] = r.new_red[...].astype(BF16)
    bias_rows = chunk // width
    part_lanes = r.wide.shape[2]
    parts = hidden_lanes // part_lanes
    bias_one = jnp.concatenate([small_row(8 + index) for index in range(hidden_lanes // width)], axis=1)
    r.total[...] = r.middle[...] + small_row(7)

    def lanes_at(part, count=1):
        return slice(part * part_lanes, (part + count) * part_lanes)

    def expand(part):
        r.wide[part % 2] = mm(r.hidden_two[...], r.low_exp[0:width, lanes_at(part)])

    def activate(part):
        for index in range(rows_all // strip):
            at = slice(index * strip, (index + 1) * strip)
            pre = r.wide[part % 2, at, :] + bias_one[:, lanes_at(part)]
            normal = 0.5 + 0.5 * lax.erf(pre * (1.0 / math.sqrt(2.0)))
            density = jnp.exp(-0.5 * pre * pre) * (1.0 / math.sqrt(2.0 * math.pi))
            r.activated[at, lanes_at(part)] = (pre * normal).astype(BF16)
            r.slope[at, lanes_at(part)] = normal + pre * density

    def contract(part):
        lanes = lanes_at(part, 2)
        r.total[...] += mm(r.activated[:, lanes], r.low_red[lanes, :])

    expand(0)
    for part in range(parts):
        if part + 1 < parts:
            expand(part + 1)
        activate(part)
        if part >= 2 and part % 2 == 0:
            contract(part - 2)
    contract(parts - 2)
    for i in range(images):
        base = i * block
        r.mixed[:, i, :] = r.total[base : base + half, :]
        r.out_special[i] = r.total[base + special : base + special + 2, :].astype(BF16)

    r.out_patch[...] = r.mixed[...].astype(BF16)

    def units_pair_start(units, arrived, sem_id):
        copy = to_partner(units, arrived, sem_id)
        copy.start()
        return copy

    def units_group_start(copy, units, arrived, outgoing, slots, sem_id):
        copy.wait()
        for index in range(2):
            first = seq * 4 + 2 * index
            outgoing[0, index] = jnp.concatenate(
                [units[first] + arrived[first], units[first + 1] + arrived[first + 1]], axis=0
            ).astype(BF16)
        axis_start("group", outgoing.at[0], slots, sem_id)

    def units_node_start(outgoing, group_slots, node_slots, sem_id):
        total = axis_finish("group", group_slots, sem_id)
        outgoing[1] = total.astype(BF16)
        axis_start("node", outgoing.at[1], node_slots, sem_id + 1)

    def units_share(node_slots, result, sem_id, pair_id):
        total = axis_finish("node", node_slots, sem_id)
        for index in range(2):
            first = seq * 4 + 2 * index
            result[first] = total[index, 0:RANK]
            result[first + 1] = total[index, RANK : 2 * RANK]
        half_units = result.at[pl.ds(seq * 4, 4)]
        copy = to_partner(half_units, half_units, pair_id)
        copy.start()
        return copy

    for part in range(4):
        lanes = slice(part * width, (part + 1) * width)
        r.lefts[part] += mm(r.folded_red[...], r.activated[:, lanes])
    for part in range(hidden_lanes // chunk):
        lanes = slice(part * chunk, (part + 1) * chunk)
        grad_act = mm_nt(r.upstream[...], r.low_red[lanes, :]).astype(BF16).astype(F32)
        grad_pre = grad_act * r.slope[:, lanes]
        r.grad_pre[:, lanes] = grad_pre.astype(BF16)
        row = jnp.sum(grad_pre, axis=0, keepdims=True)
        for index in range(bias_rows):
            first = 4 + part * bias_rows + index
            r.lefts[6, first : first + 1, :] = row[:, index * width : (index + 1) * width]
        back = mm_nt(r.grad_pre[:, lanes], r.low_exp[:, lanes])
        if part == 0:
            r.total[...] = back[:, 0:width]
            r.folded[...] = back[:, width : width + 2 * RANK]
        else:
            r.total[...] += back[:, 0:width]
            r.folded[...] += back[:, width : width + 2 * RANK]

    def left_of(hidden_ref):
        return mm_tn(r.folded[...].astype(BF16), hidden_ref[...])[0:RANK]

    r.lefts[4] += left_of(r.hidden_two)

    def normalise_back(i, gain, xhat_ref, scale_ref, gain_ref, shift_ref):
        at = pl.ds(pl.multiple_of(i * block, 16), block)
        grad = r.total[at, :]
        xhat = xhat_ref[at, :]
        gained = grad * gain
        first = jnp.mean(gained, axis=1, keepdims=True)
        second = jnp.mean(gained * xhat, axis=1, keepdims=True)
        gain_ref[...] += jnp.sum(grad * xhat, axis=0, keepdims=True)
        shift_ref[...] += jnp.sum(grad, axis=0, keepdims=True)
        return scale_ref[at, :] * (gained - first - xhat * second)

    r.gain_sum[...] = jnp.zeros_like(r.gain_sum)
    r.shift_sum[...] = jnp.zeros_like(r.shift_sum)
    r.branch_sum[...] = jnp.zeros_like(r.branch_sum)

    @pl.loop(0, images)
    def _(i):
        at = pl.ds(pl.multiple_of(i * block, 16), block)
        back = normalise_back(i, small_row(5), r.xhat_two, r.scale_two, r.gain_sum, r.shift_sum)
        grad = r.upstream[at, :].astype(F32) + back
        r.grad_middle[at, :] = grad
        low = grad.astype(BF16)
        r.grad_branch[at, :] = low
        r.branch_sum[...] += jnp.sum(low.astype(F32), axis=0, keepdims=True)

    r.lefts[6, 1:2, :] = r.gain_sum[...]
    r.lefts[6, 2:3, :] = r.shift_sum[...]
    r.lefts[6, 0:1, :] = r.branch_sum[...]
    r.lefts[7] = jnp.zeros((RANK, width), F32)
    back = mm_nt(r.grad_branch[...], r.low_out[...])
    r.grad_attended[...] = back[:, 0:width].astype(BF16)
    r.folded[...] = back[:, width : width + 2 * RANK]
    r.lefts[5] += left_of(r.attended)

    left_copy = units_pair_start(r.lefts, r.lefts_arrived, 2)

    def grad_copy(i):
        return to_partner(r.grad_sent.at[i], r.grad_arrived.at[i], 8 + i)

    def scratch_at(task):
        return slice(0, 2 * KEYS), slice(task * 2 * KEYS, task * 2 * KEYS + 2 * block)

    def special_rows(i):
        return pl.ds(pl.multiple_of(i * block + special, 8), 2)

    def reduce_gradient(part):
        lanes = slice(part * chunk, (part + 1) * chunk)
        r.err_red[lanes, :] += mm_tn(r.activated[:, lanes], r.upstream[...])

    def expand_gradient(part):
        lanes = slice(part * chunk, (part + 1) * chunk)
        r.err_exp[:, lanes] += mm_tn(r.hidden_two[...], r.grad_pre[:, lanes])

    r.err_out[...] += mm_tn(r.attended[...], r.grad_branch[...])
    reduce_gradient(0)
    units_group_start(left_copy, r.lefts, r.lefts_arrived, r.lefts_out, r.lefts_group, 0)

    @pl.loop(0, images // together)
    def _(step):
        for task, (ahead, pair) in enumerate(tasks):
            i = step * together + ahead
            grad_mixed = stacked(r.grad_attended[image_rows(i), lanes_of(pair)])
            r.slope[scratch_at(task)] = mm_nt(of_both(i, lanes_of(pair, width)), grad_mixed)
        for task, (ahead, pair) in enumerate(tasks):
            i = step * together + ahead
            probs = r.probs[i * pairs + pair]
            weighted = probs * r.slope[scratch_at(task)]
            delta = jnp.sum(weighted, axis=0, keepdims=True)
            r.low_probs[task] = (weighted - probs * delta).astype(BF16)
        for ahead in range(together):
            i = step * together + ahead
            at = image_rows(i)
            for pair in range(pairs):
                grad_scores = r.low_probs[ahead * pairs + pair]
                r.grad_query[at, lanes_of(pair)] = unstacked(
                    mm_tn(grad_scores, of_both(i, lanes_of(pair)))
                ) * (1.0 / math.sqrt(HEAD_DIM))
                grad_keys = mm(grad_scores, stacked(r.query[at, lanes_of(pair)]))
                r.grad_own[i, :, lanes_of(pair)] = grad_keys[0:KEYS]
                r.grad_sent[i, :, lanes_of(pair)] = grad_keys[KEYS : 2 * KEYS]
            for pair in range(pairs):
                grad_mixed = stacked(r.grad_attended[at, lanes_of(pair)])
                grad_values = mm(r.probs[i * pairs + pair].astype(BF16), grad_mixed)
                r.grad_own[i, :, lanes_of(pair, width)] = grad_values[0:KEYS]
                r.grad_sent[i, :, lanes_of(pair, width)] = grad_values[KEYS : 2 * KEYS]
            r.grad_sent[i, special : special + 2, :] = r.grad_own[i, special : special + 2, :]
            r.grad_sent[i, block : block + 2, 0:width] = r.grad_query[special_rows(i), :]
            grad_copy(i).start()

    row_ids = lax.broadcasted_iota(jnp.int32, (block, 1), 0)
    halved = jnp.where((row_ids >= special) & (row_ids < special + 2), 0.5, 1.0)
    r.late_rows[...] = jnp.zeros_like(r.late_rows)
    for part in range(1, hidden_lanes // chunk):
        reduce_gradient(part)
    expand_gradient(0)

    @pl.loop(0, images)
    def _(i):
        grad_copy(i).wait()
        base = pl.multiple_of(i * block, 16)
        at = pl.ds(base, block)
        specials = pl.ds(pl.multiple_of(base + special, 8), 2)
        r.grad_query[specials, :] += r.grad_arrived[i, block : block + 2, 0:width]
        query_part = r.grad_query[at, :].astype(BF16).astype(F32) * halved
        r.grad_qkv[at, 0:width] = query_part.astype(BF16)
        r.late_rows[2:3, :] += jnp.sum(query_part, axis=0, keepdims=True)
        rest = (r.grad_own[i, 0:block, :] + r.grad_arrived[i, 0:block, :]).astype(BF16)
        rest = rest.astype(F32) * halved
        r.late_rows[3:4, :] += jnp.sum(rest[:, width : 2 * width], axis=0, keepdims=True)
        r.grad_qkv[at, width : 3 * width] = rest.astype(BF16)

    units_node_start(r.lefts_out, r.lefts_group, r.lefts_node, 0)

    r.folded[...] = mm_nt(r.grad_qkv[...], r.low_in[width : width + 2 * RANK, :])
    r.left_in[...] += left_of(r.hidden_one)
    left_in_copy = to_partner(r.left_in, r.left_in_arrived, 4)
    left_in_copy.start()
    r.total[...] = mm_nt(r.grad_qkv[...], r.low_in[0:width, :])
    left_in_copy.wait()
    pair_sum = r.left_in[...] + r.left_in_arrived[...]
    r.left_in_out[...] = jnp.concatenate(
        [pair_sum[:, 0:256], jnp.concatenate([pair_sum[:, 256:384], jnp.zeros((RANK, 128), F32)], axis=1)],
        axis=0,
    ).astype(BF16)
    chips_start(r.left_in_out, r.left_in_slots, 5)

    for part in range(1, hidden_lanes // chunk):
        expand_gradient(part)
    r.gain_sum[...] = jnp.zeros_like(r.gain_sum)
    r.shift_sum[...] = jnp.zeros_like(r.shift_sum)

    @pl.loop(0, images)
    def _(i):
        at = pl.ds(pl.multiple_of(i * block, 16), block)
        back = normalise_back(i, small_row(0), r.xhat_one, r.scale_one, r.gain_sum, r.shift_sum)
        r.total[at, :] = (back + r.grad_middle[at, :]) * jnp.where(halved < 1.0, 2.0, 1.0)

    r.late_rows[0:1, :] = r.gain_sum[...]
    r.late_rows[1:2, :] = r.shift_sum[...]
    left_share = units_share(r.lefts_node, r.lefts_total, 1, 3)
    for part in range(3):
        lanes = slice(part * width, (part + 1) * width)
        r.err_in[:, lanes] += mm_tn(r.hidden_one[...], r.grad_qkv[:, lanes])
    own_lanes = r.cross_arrived.shape[1]
    apart = 3 * width - own_lanes
    cross_sent = r.low_exp.at[pl.ds(0, width), pl.ds(0, own_lanes)]
    cross_own = r.low_exp.at[pl.ds(0, width), pl.ds(own_lanes, own_lanes)]
    cross_sent[...] = r.err_in[:, pl.ds(pl.multiple_of(partner * apart, 128), own_lanes)].astype(
        BF16
    )
    cross_copy = to_partner(cross_sent, r.cross_arrived, 6)
    cross_copy.start()
    left_share.wait()
    inverse = 1.0 / workers
    basis_red = orthonormal(
        jnp.concatenate([r.lefts_total[part] for part in range(4)], axis=1) * inverse
    )
    basis_exp = orthonormal(r.lefts_total[4] * inverse)
    basis_out = orthonormal(r.lefts_total[5] * inverse)
    r.basis_red[...] = basis_red
    r.basis_exp[...] = basis_exp
    r.basis_out[...] = basis_out

    def right_of(basis, merged):
        both = jnp.concatenate([basis, basis - basis.astype(BF16).astype(F32)], axis=0).astype(BF16)
        product = mm(both, merged.astype(BF16))
        return product[0:RANK] + product[RANK : 2 * RANK]

    for part in range(4):
        lanes = slice(part * width, (part + 1) * width)
        r.rights[part] = right_of(basis_exp, r.err_exp[:, lanes])
    r.rights[4] = right_of(basis_red, r.err_red[...])
    r.rights[5] = right_of(basis_out, r.err_out[...])
    r.rights[6] = r.late_rows[...]
    r.rights[7] = jnp.zeros((RANK, width), F32)
    right_copy = units_pair_start(r.rights, r.rights_arrived, 5)
    units_group_start(right_copy, r.rights, r.rights_arrived, r.rights_out, r.rights_group, 2)
    cross_own[...] = r.err_in[:, pl.ds(pl.multiple_of(seq * apart, 128), own_lanes)].astype(BF16)

    total = chips_finish(r.left_in_slots, 5)
    basis_in = orthonormal(
        jnp.concatenate([total[0:RANK], total[RANK : 2 * RANK, 0:128]], axis=1) * inverse
    )
    r.basis_in[...] = basis_in
    cross_copy.wait()
    part = right_of(basis_in, cross_own[...]) + right_of(basis_in, r.cross_arrived[...])
    rest = jnp.concatenate(
        [part[:, width:own_lanes], jnp.zeros((RANK, 2 * width - own_lanes), F32)], axis=1
    )
    r.right_in_out[...] = jnp.concatenate([part[:, 0:width], rest], axis=0).astype(BF16)
    chips_start(r.right_in_out, r.right_in_slots, 4)
    units_node_start(r.rights_out, r.rights_group, r.rights_node, 2)
    for i in range(images):
        base = i * block
        r.mixed[:, i, :] = r.total[base : base + half, :] * r.mask_columns[i, 0:half, :]
        r.grad_special[i] = r.total[base + special : base + special + 2, :].astype(BF16)
    r.grad_patch[...] = r.mixed[...].astype(BF16)

    for name in ("m_small", "m_in", "m_out", "m_exp", "m_red"):
        loads[name].wait()
    right_share = units_share(r.rights_node, r.rights_total, 3, 12)
    right_share.wait()
    for part in range(4):
        r.new_f_exp[:, part * width : (part + 1) * width] = r.rights_total[part] * inverse
    r.new_f_red[...] = r.rights_total[4] * inverse
    r.new_f_out[...] = r.rights_total[5] * inverse

    def small_update(at, grad):
        momentum = DECAY * r.mom_small[at, :] + grad * inverse
        r.mom_small[at, :] = momentum
        r.new_small[at, :] = r.new_small[at, :] - RATE * momentum

    small_update(slice(0, 4), r.rights_total[6][0:4])
    small_update(slice(4, 12), r.lefts_total[6])

    total = chips_finish(r.right_in_slots, 4)
    r.right_in_total[seq] = jnp.concatenate(
        [total[0:RANK], total[RANK : 2 * RANK, 0 : own_lanes - width]], axis=1
    )
    share = to_partner(r.right_in_total.at[seq], r.right_in_total.at[seq], 7)
    share.start()
    share.wait()
    r.new_f_in[:, 0:own_lanes] = r.right_in_total[0] * inverse
    r.new_f_in[:, own_lanes : 3 * width] = (
        r.right_in_total[1][:, 2 * own_lanes - 3 * width : own_lanes] * inverse
    )


def store_kernel(names, targets, *all_refs):
    refs = Names()
    for name, ref in zip(names, all_refs):
        setattr(refs, name, ref)
    waits = []

    def send(name, at=None):
        source, target = getattr(refs, "next_" + name, None), getattr(refs, "hbm_" + name)
        if source is None:
            source = getattr(refs, name)
        if len(target.shape) > len(source.shape):
            target = target.at[0]
        sem = refs.sem.at[targets.index(name)]
        if at is None or at.start == 0:
            waits.append(pltpu.make_async_copy(source, target, sem))
        if at is not None:
            at = pl.ds(at.start, at.stop - at.start)
            source, target = source.at[at], target.at[at]
        pltpu.make_async_copy(source, target, sem).start()

    updated = {kind + which for kind in KINDS for which in MATRICES}
    for name in targets:
        if name not in updated:
            send(name)
    for which, rows in (("exp", 128), ("red", 384), ("out", 384), ("in", 128)):
        weight, momentum, error = (getattr(refs, kind + which) for kind in KINDS)
        new_weight, new_momentum, new_error = (getattr(refs, "next_" + kind + which) for kind in KINDS)
        left_stack, right_stack = outer_product(
            getattr(refs, "basis_" + which)[...], getattr(refs, "new_f_" + which)[...]
        )
        for strip in range(weight.shape[0] // rows):
            at = slice(strip * rows, (strip + 1) * rows)
            approx = mm_tn(left_stack[:, at], right_stack)
            new_error[at, :] = error[at, :] - approx
            send("err_" + which, at)
            next_momentum = DECAY * momentum[at, :] + approx
            new_momentum[at, :] = next_momentum
            send("mom_" + which, at)
            new_weight[at, :] = weight[at, :] - RATE * next_momentum
            send("new_" + which, at)
    for copy in waits:
        copy.wait()


def body(chips, groups, *args):
    args = list(args)
    for index in (0, 2):
        args[index] = jnp.transpose(args[index], (1, 0, 2))
    half, images, width = args[0].shape
    wide = args[8].shape[1]
    special = round_up(half, 8)
    block = round_up(special + 2, 16)
    rows = images * block
    out_shapes = [((half, images, width), BF16), ((images, 2, width), BF16)] * 2
    weight_shapes = [(width, 3 * width), (width, width), (width, wide), (wide, width)]
    small_shape = (args[10].shape, F32)
    out_shapes += [(shape, F32) for shape in weight_shapes] + [small_shape]
    out_shapes += [(shape, F32) for shape in weight_shapes] + [small_shape]
    out_shapes += [(shape, F32) for shape in weight_shapes]
    out_shapes += [((RANK, size), F32) for size in (3 * width, width, wide, width)]
    unit = (RANK, width)
    own_lanes = round_up(3 * width // 2, 128)
    scratch = dict(
        raw_patch=pltpu.VMEM((half, images, width), BF16),
        raw_special=pltpu.VMEM((images, 2, width), BF16),
        raw_up=pltpu.VMEM((half, images, width), BF16),
        raw_special_up=pltpu.VMEM((images, 2, width), BF16),
        mixed=pltpu.VMEM((half, images, width), F32),
        rank=pltpu.VMEM((images, half), jnp.int32),
        count=pltpu.SMEM((images,), jnp.int32),
        folded=pltpu.VMEM((rows, 2 * RANK), F32),
        folded_red=pltpu.VMEM((RANK, rows), BF16),
        low_probs=pltpu.VMEM((HEADS, 2 * KEYS, 2 * block), BF16),
        branch_sum=pltpu.VMEM((1, width), F32),
        flags=pltpu.VMEM((8, KEYS), F32),
        other_flags=pltpu.VMEM((8, KEYS), F32),
        mask_columns=pltpu.VMEM((images, 2 * KEYS, 1), F32),
        tokens=pltpu.VMEM((rows, width), F32),
        xhat_one=pltpu.VMEM((rows, width), F32),
        xhat_two=pltpu.VMEM((rows, width), F32),
        scale_one=pltpu.VMEM((rows, 1), F32),
        scale_two=pltpu.VMEM((rows, 1), F32),
        hidden_one=pltpu.VMEM((rows, width), BF16),
        hidden_two=pltpu.VMEM((rows, width), BF16),
        low_in=pltpu.VMEM((width + 2 * RANK, 3 * width), BF16),
        low_out=pltpu.VMEM((width + 2 * RANK, width), BF16),
        low_exp=pltpu.VMEM((width + 2 * RANK, wide), BF16),
        low_red=pltpu.VMEM((wide, width), BF16),
        query=pltpu.VMEM((rows, width), BF16),
        keys=pltpu.VMEM((2, images, KEYS, 2 * width), BF16),
        upstream=pltpu.VMEM((rows, width), BF16),
        probs=pltpu.VMEM((images * HEADS // 2, 2 * KEYS, 2 * block), F32),
        attended=pltpu.VMEM((rows, width), BF16),
        middle=pltpu.VMEM((rows, width), F32),
        wide=pltpu.VMEM((2, rows, 256), F32),
        activated=pltpu.VMEM((rows, wide), BF16),
        slope=pltpu.VMEM((rows, wide), F32),
        grad_pre=pltpu.VMEM((rows, wide), BF16),
        total=pltpu.VMEM((rows, width), F32),
        gain_sum=pltpu.VMEM((1, width), F32),
        shift_sum=pltpu.VMEM((1, width), F32),
        grad_branch=pltpu.VMEM((rows, width), BF16),
        grad_attended=pltpu.VMEM((rows, width), BF16),
        grad_own=pltpu.VMEM((images, KEYS, 2 * width), F32),
        grad_sent=pltpu.VMEM((images, KEYS, 2 * width), F32),
        grad_arrived=pltpu.VMEM((images, KEYS, 2 * width), F32),
        grad_qkv=pltpu.VMEM((rows, 3 * width), BF16),
        lefts=pltpu.VMEM((8,) + unit, F32),
        lefts_arrived=pltpu.VMEM((8,) + unit, F32),
        lefts_out=pltpu.VMEM((2, 2, 2 * RANK, width), BF16),
        lefts_group=pltpu.VMEM((groups, 2, 2 * RANK, width), BF16),
        lefts_node=pltpu.VMEM((chips // groups, 2, 2 * RANK, width), BF16),
        lefts_total=pltpu.VMEM((8,) + unit, F32),
        rights=pltpu.VMEM((8,) + unit, F32),
        rights_arrived=pltpu.VMEM((8,) + unit, F32),
        rights_out=pltpu.VMEM((2, 2, 2 * RANK, width), BF16),
        rights_group=pltpu.VMEM((groups, 2, 2 * RANK, width), BF16),
        rights_node=pltpu.VMEM((chips // groups, 2, 2 * RANK, width), BF16),
        rights_total=pltpu.VMEM((8,) + unit, F32),
        left_in=pltpu.VMEM(unit, F32),
        left_in_arrived=pltpu.VMEM(unit, F32),
        left_in_out=pltpu.VMEM((2 * RANK, 256), BF16),
        left_in_slots=pltpu.VMEM((chips, 2 * RANK, 256), BF16),
        cross_arrived=pltpu.VMEM((width, own_lanes), BF16),
        right_in_out=pltpu.VMEM((2 * RANK, width), BF16),
        right_in_slots=pltpu.VMEM((chips, 2 * RANK, width), BF16),
        right_in_total=pltpu.VMEM((2, RANK, own_lanes), F32),
        late_rows=pltpu.VMEM(unit, F32),
        load_sem=pltpu.SemaphoreType.DMA((16,)),
        pair_send=pltpu.SemaphoreType.DMA((15,)),
        pair_recv=pltpu.SemaphoreType.DMA((15,)),
        stage_send=pltpu.SemaphoreType.DMA((6,)),
        stage_recv=pltpu.SemaphoreType.DMA((6,)),
    )
    made = OUTPUTS + BASES
    made_shapes = out_shapes + [((RANK, size), F32) for size in (width, width, width, wide)]
    names = INPUTS + made + tuple(scratch)
    in_hbm = pl.BlockSpec(memory_space=pltpu.HBM)
    in_vmem = pl.BlockSpec(memory_space=pltpu.VMEM)
    results = pl.pallas_call(
        functools.partial(layer_kernel, chips, groups, images, half, names),
        out_shape=[pltpu.VMEM(shape, dtype) for shape, dtype in made_shapes],
        in_specs=[in_hbm] * len(INPUTS),
        out_specs=[in_vmem] * len(made),
        scratch_shapes=list(scratch.values()),
        compiler_params=pltpu.CompilerParams(
            collective_id=0, has_side_effects=True, vmem_limit_bytes=40 << 20
        ),
        name="layer",
    )(*args[:20], *[jnp.transpose(factor) for factor in args[20:]])
    final_shapes = [
        jax.ShapeDtypeStruct((1,) + shape if 14 <= index < 18 else shape, dtype)
        for index, (shape, dtype) in enumerate(out_shapes)
    ]
    updated = {
        "next_" + kind + which: shape
        for index, kind in enumerate(KINDS)
        for which, shape in zip(MATRICES, weight_shapes)
    }
    stored = list(
        pl.pallas_call(
            functools.partial(
                store_kernel,
                made + tuple("hbm_" + name for name in OUTPUTS) + tuple(updated) + ("sem",),
                OUTPUTS,
            ),
            out_shape=final_shapes,
            in_specs=[in_vmem] * len(made),
            out_specs=[in_hbm] * len(OUTPUTS),
            scratch_shapes=[pltpu.VMEM(shape, F32) for shape in updated.values()]
            + [pltpu.SemaphoreType.DMA((len(OUTPUTS),))],
            compiler_params=pltpu.CompilerParams(vmem_limit_bytes=24 << 20),
            name="store",
        )(*results)
    )
    for index in (0, 2):
        stored[index] = jnp.transpose(stored[index], (1, 0, 2))
    return (*stored[:18], *[jnp.transpose(factor) for factor in stored[18:]])


def solution(mesh):
    images_over = ("node", "group")
    rows_spec = P(images_over, "seq", None)
    special_spec = P(images_over, None, None)
    worker_spec = P(("seq", "node", "group"), None, None)
    whole = P()
    placed = (
        (rows_spec, special_spec) * 2
        + (P(images_over, "seq"), P(images_over))
        + (whole,) * 10
        + (worker_spec,) * 4
        + (whole,) * 4
    )
    groups = mesh.shape["group"]
    chips = mesh.shape["node"] * groups
    return jax.shard_map(
        functools.partial(body, chips, groups),
        mesh=mesh,
        in_specs=placed,
        out_specs=(rows_spec, special_spec) * 2
        + (whole,) * 10
        + (worker_spec,) * 4
        + (whole,) * 4,
        check_vma=False,
    )
```

```python
import functools
import math

import jax
import jax.numpy as jnp
from jax import lax
from jax.experimental import pallas as pl
from jax.experimental.pallas import tpu as pltpu
from jax.sharding import PartitionSpec as P

HEADS = 6
HEAD_DIM = 64
EPSILON = 1e-06
RATE = 0.1
DECAY = 0.9
RANK = 8
MESH = pl.DeviceIdType.MESH
F32 = jnp.float32
BF16 = jnp.bfloat16
INPUTS = (
    "patch_tokens",
    "special_tokens",
    "patch_upstream",
    "special_upstream",
    "patch_rank",
    "keep_count",
    "project_in",
    "project_out",
    "expand_weight",
    "reduce_weight",
    "small_params",
    "project_in_momentum",
    "project_out_momentum",
    "expand_momentum",
    "reduce_momentum",
    "small_momentum",
    "project_in_error",
    "project_out_error",
    "expand_error",
    "reduce_error",
    "project_in_factor",
    "project_out_factor",
    "expand_factor",
    "reduce_factor",
)
OUTPUTS = (
    "out_patch",
    "out_special",
    "grad_patch",
    "grad_special",
    "new_in",
    "new_out",
    "new_exp",
    "new_red",
    "new_small",
    "mom_in",
    "mom_out",
    "mom_exp",
    "mom_red",
    "mom_small",
    "err_in",
    "err_out",
    "err_exp",
    "err_red",
    "new_f_in",
    "new_f_out",
    "new_f_exp",
    "new_f_red",
)
BASES = ("basis_in", "basis_out", "basis_exp", "basis_red")
KINDS = ("new_", "mom_", "err_")
MATRICES = ("in", "out", "exp", "red")
KEYS = 128


def round_up(value, unit):
    return -(-value // unit) * unit


def mm(left_side, right_side):
    return jnp.dot(left_side, right_side, preferred_element_type=F32)


def mm_nt(left_side, right_side):
    return lax.dot_general(
        left_side, right_side, (((1,), (1,)), ((), ())), preferred_element_type=F32
    )


def mm_tn(left_side, right_side):
    return lax.dot_general(
        left_side, right_side, (((0,), (0,)), ((), ())), preferred_element_type=F32
    )


def split(value):
    high = value.astype(BF16)
    return high, (value - high.astype(F32)).astype(BF16)


def orthonormal(rows):
    row_ids = lax.broadcasted_iota(jnp.int32, (RANK, 1), 0)
    for step in range(RANK):
        own = rows[step : step + 1, :]
        dots = jnp.sum(rows * own, axis=1, keepdims=True)
        scale = lax.rsqrt(dots[step : step + 1, :] + EPSILON)
        unit = own * scale
        later = jnp.where(row_ids > step, dots * scale, 0.0)
        rows = jnp.where(row_ids == step, unit, rows - later * unit)
    return rows


def outer_product(basis, right):
    basis_high, basis_low = split(basis)
    right_high, right_low = split(right)
    left_stack = jnp.concatenate(
        [basis_high.astype(F32), basis_low.astype(F32)] * 2, axis=0
    ).astype(BF16)
    right_stack = jnp.concatenate(
        [right_high.astype(F32)] * 2 + [right_low.astype(F32)] * 2, axis=0
    ).astype(BF16)
    return left_stack, right_stack


class Names:
    pass


def layer_kernel(chips, groups, images, half, names, *all_refs):
    refs = Names()
    for name, ref in zip(names, all_refs):
        setattr(refs, name, ref)
    r = refs
    r.grad_middle, r.grad_query = r.tokens, r.middle
    width = HEADS * HEAD_DIM
    special = round_up(half, 8)
    block = round_up(special + 2, 16)
    rows_all = images * block
    workers = 2 * chips
    seq = lax.axis_index("seq")
    node = lax.axis_index("node")
    group = lax.axis_index("group")
    chip = node * groups + group
    partner = 1 - seq

    loads = {}
    free_sems = list(range(r.load_sem.shape[0]))

    class Load:
        def __init__(self, source, target):
            self.sem_id = free_sems.pop(0)
            self.copy = pltpu.make_async_copy(source, target, r.load_sem.at[self.sem_id])
            self.copy.start()

        def wait(self):
            self.copy.wait()
            free_sems.append(self.sem_id)

    def load(name, source, target):
        loads[name] = Load(source, target)

    load("tokens", r.patch_tokens, r.raw_patch)
    load("special", r.special_tokens, r.raw_special)
    load("rank", r.patch_rank, r.rank)
    load("count", r.keep_count, r.count)
    load("small", r.small_params, r.new_small)
    for name, lanes in (("w_keys", pl.ds(width, 2 * width)), ("w_query", pl.ds(0, width))):
        load(name, r.project_in.at[:, lanes], r.new_in.at[:, lanes])

    load("f_in", r.project_in_factor, r.new_f_in)
    load("f_out", r.project_out_factor, r.new_f_out)
    load("f_exp", r.expand_factor, r.new_f_exp)
    load("f_red", r.reduce_factor, r.new_f_red)
    load("upstream", r.patch_upstream, r.raw_up)
    load("special_up", r.special_upstream, r.raw_special_up)
    load("e_in", r.project_in_error.at[0], r.err_in)
    load("e_exp", r.expand_error.at[0], r.err_exp)
    load("e_red", r.reduce_error.at[0], r.err_red)
    load("e_out", r.project_out_error.at[0], r.err_out)

    def load_third():
        load("w_out", r.project_out, r.new_out)
        load("w_exp", r.expand_weight, r.new_exp)
        load("w_red", r.reduce_weight, r.new_red)

    def load_last():
        load("m_small", r.small_momentum, r.mom_small)
        load("m_out", r.project_out_momentum, r.mom_out)
        load("m_exp", r.expand_momentum, r.mom_exp)
        load("m_red", r.reduce_momentum, r.mom_red)
        load("m_in", r.project_in_momentum, r.mom_in)

    barrier = pltpu.get_barrier_semaphore()
    pl.semaphore_signal(barrier, inc=1, device_id={"seq": partner}, device_id_type=MESH)

    nodes = chips // groups

    def each_chip(act):
        def row(step, first):
            for ahead in range(first, groups):
                act({"node": lax.rem(node + step, nodes), "group": lax.rem(group + ahead, groups)})

        def others(step, carry):
            row(step, 0)
            return carry

        lax.fori_loop(1, nodes, others, 0)
        row(0, 1)

    def greet(device):
        pl.semaphore_signal(barrier, inc=1, device_id=device, device_id_type=MESH)

    each_chip(greet)

    def to_partner(source, target, sem_id):
        return pltpu.make_async_remote_copy(
            src_ref=source,
            dst_ref=target,
            send_sem=r.pair_send.at[sem_id],
            recv_sem=r.pair_recv.at[sem_id],
            device_id={"seq": partner},
            device_id_type=MESH,
        )

    def remote(source, target, sem_id, device):
        return pltpu.make_async_remote_copy(
            src_ref=source,
            dst_ref=target,
            send_sem=r.stage_send.at[sem_id],
            recv_sem=r.stage_recv.at[sem_id],
            device_id=device,
            device_id_type=MESH,
        )

    def stage_finish(count, slots, sem_id):
        several = slots.at[pl.ds(0, count - 1)]
        whole = remote(several, several, sem_id, {"seq": partner})
        whole.wait_recv()
        whole.wait_send()
        if count <= 32:
            total = slots[0].astype(F32)
            for index in range(1, count):
                total = total + slots[index].astype(F32)
            return total

        def add(index, total):
            return total + slots[index].astype(F32)

        return lax.fori_loop(1, count, add, slots[0].astype(F32))

    def chips_start(source, slots, sem_id):
        slots[chip] = source[...]
        each_chip(lambda device: remote(source, slots.at[chip], sem_id, device).start())

    def chips_finish(slots, sem_id):
        return stage_finish(chips, slots, sem_id)

    def axis_start(axis, source, slots, sem_id):
        size, place = lax.axis_size(axis), lax.axis_index(axis)
        slots[place] = source[...]
        for step in range(1, size):
            device = {axis: lax.rem(place + step, size)}
            remote(source, slots.at[place], sem_id, device).start()

    def axis_finish(axis, slots, sem_id):
        return stage_finish(lax.axis_size(axis), slots, sem_id)

    loads["rank"].wait()
    loads["count"].wait()
    r.flags[...] = jnp.zeros_like(r.flags)
    for i in range(images):
        r.flags[i : i + 1, 0:half] = jnp.where(
            r.rank[i : i + 1, :] < r.count[i], 1.0, 0.0
        ).astype(F32)
    lane_ids = lax.broadcasted_iota(jnp.int32, (1, KEYS), 1)
    special_lanes = jnp.where((lane_ids >= special) & (lane_ids < special + 2), 1.0, 0.0)
    own_columns = jnp.transpose(r.flags[...] + special_lanes)
    for i in range(images):
        r.mask_columns[i, 0:KEYS, :] = own_columns[:, i : i + 1]

    small = r.new_small
    loads["small"].wait()

    def small_row(index):
        return small[index : index + 1, :]

    loads["tokens"].wait()
    loads["special"].wait()
    r.mixed[...] = r.raw_patch[...].astype(F32)
    for i in range(images):
        base = i * block
        r.tokens[base + special - 8 : base + block, :] = jnp.zeros(
            (block - special + 8, width), F32
        )
        r.tokens[base : base + half, :] = (
            r.mixed[:, i, :] * r.mask_columns[i, 0:half, :]
        )
        r.tokens[base + special : base + special + 2, :] = r.raw_special[i].astype(F32)

    def normalise(source, i, gain, shift, xhat_ref, scale_ref, hidden_ref):
        at = pl.ds(pl.multiple_of(i * block, 16), block)
        values = source[at, :]
        center = values - jnp.mean(values, axis=1, keepdims=True)
        spread = jnp.mean(center * center, axis=1, keepdims=True)
        scale = lax.rsqrt(spread + EPSILON)
        xhat = center * scale
        xhat_ref[at, :] = xhat
        scale_ref[at, :] = scale
        hidden_ref[at, :] = (xhat * gain + shift).astype(BF16)

    @pl.loop(0, images)
    def _(i):
        normalise(r.tokens, i, small_row(0), small_row(1), r.xhat_one, r.scale_one, r.hidden_one)

    loads["w_keys"].wait()
    r.low_in[0:width, width : 3 * width] = r.new_in[:, width : 3 * width].astype(BF16)
    for i in range(images):
        r.keys[0, i, block:KEYS, :] = jnp.zeros((KEYS - block, 2 * width), BF16)
    product = mm(r.hidden_one[...], r.low_in[0:width, width : 3 * width])
    for i in range(images):
        at = slice(i * block, (i + 1) * block)
        r.keys[0, i, 0:block, 0:width] = product[at, 0:width].astype(BF16)
        r.keys[0, i, 0:block, width : 2 * width] = (
            product[at, width : 2 * width] + small_row(3)
        ).astype(BF16)
    pl.semaphore_wait(barrier, chips)
    key_copy = to_partner(r.keys.at[0], r.keys.at[1], 0)
    flag_copy = to_partner(r.flags, r.other_flags, 1)
    key_copy.start()
    flag_copy.start()
    loads["w_query"].wait()
    r.low_in[0:width, 0:width] = r.new_in[:, 0:width].astype(BF16)
    product = mm(r.hidden_one[...], r.low_in[0:width, 0:width])
    query = (product + small_row(2)).astype(BF16).astype(F32) * (1.0 / math.sqrt(HEAD_DIM))
    r.query[...] = query.astype(BF16)

    def error_left(error_ref, factor_ref, row_start, row_count):
        return mm_nt(
            factor_ref[...].astype(BF16), error_ref[row_start : row_start + row_count, :].astype(BF16)
        )

    loads["upstream"].wait()
    loads["special_up"].wait()
    r.mixed[...] = r.raw_up[...].astype(F32)
    for i in range(images):
        base = i * block
        r.middle[base + special - 8 : base + block, :] = jnp.zeros(
            (block - special + 8, width), F32
        )
        r.middle[base : base + half, :] = r.mixed[:, i, :]
        r.middle[base + special : base + special + 2, :] = 0.5 * r.raw_special_up[i].astype(F32)
    r.lefts[6, 3:4, :] = jnp.sum(r.middle[...], axis=0, keepdims=True)
    r.upstream[...] = r.middle[...].astype(BF16)
    loads["f_in"].wait()
    loads["f_out"].wait()
    loads["f_exp"].wait()
    loads["f_red"].wait()

    def with_factor(low_ref, factor_ref):
        factor = factor_ref[...]
        low_ref[width : width + 2 * RANK, :] = jnp.concatenate(
            [factor, jnp.zeros_like(factor)], axis=0
        ).astype(BF16)

    with_factor(r.low_in, r.new_f_in)
    with_factor(r.low_out, r.new_f_out)
    with_factor(r.low_exp, r.new_f_exp)
    folded_red = mm_nt(r.new_f_red[...].astype(BF16), r.upstream[...])
    r.folded_red[...] = folded_red.astype(BF16)
    loads["e_in"].wait()
    r.left_in[...] = error_left(r.err_in, r.new_f_in, 0, width)
    loads["e_exp"].wait()
    r.lefts[4] = error_left(r.err_exp, r.new_f_exp, 0, width)
    load_third()
    loads["e_red"].wait()
    for part in range(4):
        r.lefts[part] = error_left(r.err_red, r.new_f_red, part * width, width)
    loads["e_out"].wait()
    r.lefts[5] = error_left(r.err_out, r.new_f_out, 0, width)

    key_copy.wait()
    flag_copy.wait()
    other_columns = jnp.transpose(r.other_flags[...])
    for i in range(images):
        r.mask_columns[i, KEYS : 2 * KEYS, :] = other_columns[:, i : i + 1]

    pair_width = 2 * HEAD_DIM
    pairs = HEADS // 2
    low_lanes = lax.broadcasted_iota(jnp.int32, (1, pair_width), 1) < HEAD_DIM

    def stacked(value):
        zero = jnp.zeros_like(value)
        return jnp.concatenate(
            [jnp.where(low_lanes, value, zero), jnp.where(low_lanes, zero, value)], axis=0
        )

    def unstacked(value):
        return jnp.where(low_lanes, value[0:block], value[block : 2 * block])

    def of_both(i, lanes):
        return jnp.concatenate([r.keys[0, i, :, lanes], r.keys[1, i, :, lanes]], axis=0)

    together = 2

    def lanes_of(pair, first=0):
        return slice(first + pair * pair_width, first + (pair + 1) * pair_width)

    def image_rows(i):
        return pl.ds(pl.multiple_of(i * block, 16), block)

    tasks = [(ahead, pair) for ahead in range(together) for pair in range(pairs)]

    @pl.loop(0, images // together)
    def _(step):
        for ahead, pair in tasks:
            i = step * together + ahead
            queries = stacked(r.query[image_rows(i), lanes_of(pair)])
            scores = mm_nt(of_both(i, lanes_of(pair)), queries)
            r.probs[i * pairs + pair] = jnp.where(r.mask_columns[i] > 0.5, scores, -1e30)
        for task, (ahead, pair) in enumerate(tasks):
            i = step * together + ahead
            scores = r.probs[i * pairs + pair]
            top = jnp.max(scores, axis=0, keepdims=True)
            weights = jnp.exp(scores - top)
            probs = weights * (1.0 / jnp.sum(weights, axis=0, keepdims=True))
            r.probs[i * pairs + pair] = probs
            r.low_probs[task] = probs.astype(BF16)
        for task, (ahead, pair) in enumerate(tasks):
            i = step * together + ahead
            mixed = mm_tn(r.low_probs[task], of_both(i, lanes_of(pair, width)))
            r.attended[image_rows(i), lanes_of(pair)] = unstacked(mixed).astype(BF16)

    loads["w_out"].wait()
    load_last()
    r.low_out[0:width, :] = r.new_out[...].astype(BF16)
    r.middle[...] = r.tokens[...] + mm(r.attended[...], r.low_out[0:width, :]) + small_row(4)

    @pl.loop(0, images)
    def _(i):
        normalise(r.middle, i, small_row(5), small_row(6), r.xhat_two, r.scale_two, r.hidden_two)

    strip = 64
    chunk = 2 * width
    hidden_lanes = r.low_exp.shape[1]
    loads["w_exp"].wait()
    r.low_exp[0:width, :] = r.new_exp[...].astype(BF16)
    loads["w_red"].wait()
    r.low_red[...] = r.new_red[...].astype(BF16)
    bias_rows = chunk // width
    part_lanes = r.wide.shape[2]
    parts = hidden_lanes // part_lanes
    bias_one = jnp.concatenate([small_row(8 + index) for index in range(hidden_lanes // width)], axis=1)
    r.total[...] = r.middle[...] + small_row(7)

    def lanes_at(part, count=1):
        return slice(part * part_lanes, (part + count) * part_lanes)

    def expand(part):
        r.wide[part % 2] = mm(r.hidden_two[...], r.low_exp[0:width, lanes_at(part)])

    def activate(part):
        for index in range(rows_all // strip):
            at = slice(index * strip, (index + 1) * strip)
            pre = r.wide[part % 2, at, :] + bias_one[:, lanes_at(part)]
            normal = 0.5 + 0.5 * lax.erf(pre * (1.0 / math.sqrt(2.0)))
            density = jnp.exp(-0.5 * pre * pre) * (1.0 / math.sqrt(2.0 * math.pi))
            r.activated[at, lanes_at(part)] = (pre * normal).astype(BF16)
            r.slope[at, lanes_at(part)] = normal + pre * density

    def contract(part):
        lanes = lanes_at(part, 2)
        r.total[...] += mm(r.activated[:, lanes], r.low_red[lanes, :])

    expand(0)
    for part in range(parts):
        if part + 1 < parts:
            expand(part + 1)
        activate(part)
        if part >= 2 and part % 2 == 0:
            contract(part - 2)
    contract(parts - 2)
    for i in range(images):
        base = i * block
        r.mixed[:, i, :] = r.total[base : base + half, :]
        r.out_special[i] = r.total[base + special : base + special + 2, :].astype(BF16)

    r.out_patch[...] = r.mixed[...].astype(BF16)

    def units_pair_start(units, arrived, sem_id):
        copy = to_partner(units, arrived, sem_id)
        copy.start()
        return copy

    def units_group_start(copy, units, arrived, outgoing, slots, sem_id):
        copy.wait()
        for index in range(2):
            first = seq * 4 + 2 * index
            outgoing[0, index] = jnp.concatenate(
                [units[first] + arrived[first], units[first + 1] + arrived[first + 1]], axis=0
            ).astype(BF16)
        axis_start("group", outgoing.at[0], slots, sem_id)

    def units_node_start(outgoing, group_slots, node_slots, sem_id):
        total = axis_finish("group", group_slots, sem_id)
        outgoing[1] = total.astype(BF16)
        axis_start("node", outgoing.at[1], node_slots, sem_id + 1)

    def units_share(node_slots, result, sem_id, pair_id):
        total = axis_finish("node", node_slots, sem_id)
        for index in range(2):
            first = seq * 4 + 2 * index
            result[first] = total[index, 0:RANK]
            result[first + 1] = total[index, RANK : 2 * RANK]
        half_units = result.at[pl.ds(seq * 4, 4)]
        copy = to_partner(half_units, half_units, pair_id)
        copy.start()
        return copy

    for part in range(4):
        lanes = slice(part * width, (part + 1) * width)
        r.lefts[part] += mm(r.folded_red[...], r.activated[:, lanes])
    for part in range(hidden_lanes // chunk):
        lanes = slice(part * chunk, (part + 1) * chunk)
        grad_act = mm_nt(r.upstream[...], r.low_red[lanes, :]).astype(BF16).astype(F32)
        grad_pre = grad_act * r.slope[:, lanes]
        r.grad_pre[:, lanes] = grad_pre.astype(BF16)
        row = jnp.sum(grad_pre, axis=0, keepdims=True)
        for index in range(bias_rows):
            first = 4 + part * bias_rows + index
            r.lefts[6, first : first + 1, :] = row[:, index * width : (index + 1) * width]
        back = mm_nt(r.grad_pre[:, lanes], r.low_exp[:, lanes])
        if part == 0:
            r.total[...] = back[:, 0:width]
            r.folded[...] = back[:, width : width + 2 * RANK]
        else:
            r.total[...] += back[:, 0:width]
            r.folded[...] += back[:, width : width + 2 * RANK]

    def left_of(hidden_ref):
        return mm_tn(r.folded[...].astype(BF16), hidden_ref[...])[0:RANK]

    r.lefts[4] += left_of(r.hidden_two)

    def normalise_back(i, gain, xhat_ref, scale_ref, gain_ref, shift_ref):
        at = pl.ds(pl.multiple_of(i * block, 16), block)
        grad = r.total[at, :]
        xhat = xhat_ref[at, :]
        gained = grad * gain
        first = jnp.mean(gained, axis=1, keepdims=True)
        second = jnp.mean(gained * xhat, axis=1, keepdims=True)
        gain_ref[...] += jnp.sum(grad * xhat, axis=0, keepdims=True)
        shift_ref[...] += jnp.sum(grad, axis=0, keepdims=True)
        return scale_ref[at, :] * (gained - first - xhat * second)

    r.gain_sum[...] = jnp.zeros_like(r.gain_sum)
    r.shift_sum[...] = jnp.zeros_like(r.shift_sum)
    r.branch_sum[...] = jnp.zeros_like(r.branch_sum)

    @pl.loop(0, images)
    def _(i):
        at = pl.ds(pl.multiple_of(i * block, 16), block)
        back = normalise_back(i, small_row(5), r.xhat_two, r.scale_two, r.gain_sum, r.shift_sum)
        grad = r.upstream[at, :].astype(F32) + back
        r.grad_middle[at, :] = grad
        low = grad.astype(BF16)
        r.grad_branch[at, :] = low
        r.branch_sum[...] += jnp.sum(low.astype(F32), axis=0, keepdims=True)

    r.lefts[6, 1:2, :] = r.gain_sum[...]
    r.lefts[6, 2:3, :] = r.shift_sum[...]
    r.lefts[6, 0:1, :] = r.branch_sum[...]
    r.lefts[7] = jnp.zeros((RANK, width), F32)
    back = mm_nt(r.grad_branch[...], r.low_out[...])
    r.grad_attended[...] = back[:, 0:width].astype(BF16)
    r.folded[...] = back[:, width : width + 2 * RANK]
    r.lefts[5] += left_of(r.attended)

    left_copy = units_pair_start(r.lefts, r.lefts_arrived, 2)

    def grad_copy(i):
        return to_partner(r.grad_sent.at[i], r.grad_arrived.at[i], 8 + i)

    def scratch_at(task):
        return slice(0, 2 * KEYS), slice(task * 2 * KEYS, task * 2 * KEYS + 2 * block)

    def special_rows(i):
        return pl.ds(pl.multiple_of(i * block + special, 8), 2)

    def reduce_gradient(part):
        lanes = slice(part * chunk, (part + 1) * chunk)
        r.err_red[lanes, :] += mm_tn(r.activated[:, lanes], r.upstream[...])

    def expand_gradient(part):
        lanes = slice(part * chunk, (part + 1) * chunk)
        r.err_exp[:, lanes] += mm_tn(r.hidden_two[...], r.grad_pre[:, lanes])

    r.err_out[...] += mm_tn(r.attended[...], r.grad_branch[...])
    reduce_gradient(0)
    units_group_start(left_copy, r.lefts, r.lefts_arrived, r.lefts_out, r.lefts_group, 0)

    @pl.loop(0, images // together)
    def _(step):
        for task, (ahead, pair) in enumerate(tasks):
            i = step * together + ahead
            grad_mixed = stacked(r.grad_attended[image_rows(i), lanes_of(pair)])
            r.slope[scratch_at(task)] = mm_nt(of_both(i, lanes_of(pair, width)), grad_mixed)
        for task, (ahead, pair) in enumerate(tasks):
            i = step * together + ahead
            probs = r.probs[i * pairs + pair]
            weighted = probs * r.slope[scratch_at(task)]
            delta = jnp.sum(weighted, axis=0, keepdims=True)
            r.low_probs[task] = (weighted - probs * delta).astype(BF16)
        for ahead in range(together):
            i = step * together + ahead
            at = image_rows(i)
            for pair in range(pairs):
                grad_scores = r.low_probs[ahead * pairs + pair]
                r.grad_query[at, lanes_of(pair)] = unstacked(
                    mm_tn(grad_scores, of_both(i, lanes_of(pair)))
                ) * (1.0 / math.sqrt(HEAD_DIM))
                grad_keys = mm(grad_scores, stacked(r.query[at, lanes_of(pair)]))
                r.grad_own[i, :, lanes_of(pair)] = grad_keys[0:KEYS]
                r.grad_sent[i, :, lanes_of(pair)] = grad_keys[KEYS : 2 * KEYS]
            for pair in range(pairs):
                grad_mixed = stacked(r.grad_attended[at, lanes_of(pair)])
                grad_values = mm(r.probs[i * pairs + pair].astype(BF16), grad_mixed)
                r.grad_own[i, :, lanes_of(pair, width)] = grad_values[0:KEYS]
                r.grad_sent[i, :, lanes_of(pair, width)] = grad_values[KEYS : 2 * KEYS]
            r.grad_sent[i, special : special + 2, :] = r.grad_own[i, special : special + 2, :]
            r.grad_sent[i, block : block + 2, 0:width] = r.grad_query[special_rows(i), :]
            grad_copy(i).start()

    row_ids = lax.broadcasted_iota(jnp.int32, (block, 1), 0)
    halved = jnp.where((row_ids >= special) & (row_ids < special + 2), 0.5, 1.0)
    r.late_rows[...] = jnp.zeros_like(r.late_rows)
    for part in range(1, hidden_lanes // chunk):
        reduce_gradient(part)
    expand_gradient(0)

    @pl.loop(0, images)
    def _(i):
        grad_copy(i).wait()
        base = pl.multiple_of(i * block, 16)
        at = pl.ds(base, block)
        specials = pl.ds(pl.multiple_of(base + special, 8), 2)
        r.grad_query[specials, :] += r.grad_arrived[i, block : block + 2, 0:width]
        query_part = r.grad_query[at, :].astype(BF16).astype(F32) * halved
        r.grad_qkv[at, 0:width] = query_part.astype(BF16)
        r.late_rows[2:3, :] += jnp.sum(query_part, axis=0, keepdims=True)
        rest = (r.grad_own[i, 0:block, :] + r.grad_arrived[i, 0:block, :]).astype(BF16)
        rest = rest.astype(F32) * halved
        r.late_rows[3:4, :] += jnp.sum(rest[:, width : 2 * width], axis=0, keepdims=True)
        r.grad_qkv[at, width : 3 * width] = rest.astype(BF16)

    units_node_start(r.lefts_out, r.lefts_group, r.lefts_node, 0)

    r.folded[...] = mm_nt(r.grad_qkv[...], r.low_in[width : width + 2 * RANK, :])
    r.left_in[...] += left_of(r.hidden_one)
    left_in_copy = to_partner(r.left_in, r.left_in_arrived, 4)
    left_in_copy.start()
    r.total[...] = mm_nt(r.grad_qkv[...], r.low_in[0:width, :])
    left_in_copy.wait()
    pair_sum = r.left_in[...] + r.left_in_arrived[...]
    r.left_in_out[...] = jnp.concatenate(
        [pair_sum[:, 0:256], jnp.concatenate([pair_sum[:, 256:384], jnp.zeros((RANK, 128), F32)], axis=1)],
        axis=0,
    ).astype(BF16)
    chips_start(r.left_in_out, r.left_in_slots, 5)

    for part in range(1, hidden_lanes // chunk):
        expand_gradient(part)
    r.gain_sum[...] = jnp.zeros_like(r.gain_sum)
    r.shift_sum[...] = jnp.zeros_like(r.shift_sum)

    @pl.loop(0, images)
    def _(i):
        at = pl.ds(pl.multiple_of(i * block, 16), block)
        back = normalise_back(i, small_row(0), r.xhat_one, r.scale_one, r.gain_sum, r.shift_sum)
        r.total[at, :] = (back + r.grad_middle[at, :]) * jnp.where(halved < 1.0, 2.0, 1.0)

    r.late_rows[0:1, :] = r.gain_sum[...]
    r.late_rows[1:2, :] = r.shift_sum[...]
    left_share = units_share(r.lefts_node, r.lefts_total, 1, 3)
    for part in range(3):
        lanes = slice(part * width, (part + 1) * width)
        r.err_in[:, lanes] += mm_tn(r.hidden_one[...], r.grad_qkv[:, lanes])
    own_lanes = r.cross_arrived.shape[1]
    apart = 3 * width - own_lanes
    cross_sent = r.low_exp.at[pl.ds(0, width), pl.ds(0, own_lanes)]
    cross_own = r.low_exp.at[pl.ds(0, width), pl.ds(own_lanes, own_lanes)]
    cross_sent[...] = r.err_in[:, pl.ds(pl.multiple_of(partner * apart, 128), own_lanes)].astype(
        BF16
    )
    cross_copy = to_partner(cross_sent, r.cross_arrived, 6)
    cross_copy.start()
    left_share.wait()
    inverse = 1.0 / workers
    basis_red = orthonormal(
        jnp.concatenate([r.lefts_total[part] for part in range(4)], axis=1) * inverse
    )
    basis_exp = orthonormal(r.lefts_total[4] * inverse)
    basis_out = orthonormal(r.lefts_total[5] * inverse)
    r.basis_red[...] = basis_red
    r.basis_exp[...] = basis_exp
    r.basis_out[...] = basis_out

    def right_of(basis, merged):
        both = jnp.concatenate([basis, basis - basis.astype(BF16).astype(F32)], axis=0).astype(BF16)
        product = mm(both, merged.astype(BF16))
        return product[0:RANK] + product[RANK : 2 * RANK]

    for part in range(4):
        lanes = slice(part * width, (part + 1) * width)
        r.rights[part] = right_of(basis_exp, r.err_exp[:, lanes])
    r.rights[4] = right_of(basis_red, r.err_red[...])
    r.rights[5] = right_of(basis_out, r.err_out[...])
    r.rights[6] = r.late_rows[...]
    r.rights[7] = jnp.zeros((RANK, width), F32)
    right_copy = units_pair_start(r.rights, r.rights_arrived, 5)
    units_group_start(right_copy, r.rights, r.rights_arrived, r.rights_out, r.rights_group, 2)
    cross_own[...] = r.err_in[:, pl.ds(pl.multiple_of(seq * apart, 128), own_lanes)].astype(BF16)

    total = chips_finish(r.left_in_slots, 5)
    basis_in = orthonormal(
        jnp.concatenate([total[0:RANK], total[RANK : 2 * RANK, 0:128]], axis=1) * inverse
    )
    r.basis_in[...] = basis_in
    cross_copy.wait()
    part = right_of(basis_in, cross_own[...]) + right_of(basis_in, r.cross_arrived[...])
    rest = jnp.concatenate(
        [part[:, width:own_lanes], jnp.zeros((RANK, 2 * width - own_lanes), F32)], axis=1
    )
    r.right_in_out[...] = jnp.concatenate([part[:, 0:width], rest], axis=0).astype(BF16)
    chips_start(r.right_in_out, r.right_in_slots, 4)
    units_node_start(r.rights_out, r.rights_group, r.rights_node, 2)
    for i in range(images):
        base = i * block
        r.mixed[:, i, :] = r.total[base : base + half, :] * r.mask_columns[i, 0:half, :]
        r.grad_special[i] = r.total[base + special : base + special + 2, :].astype(BF16)
    r.grad_patch[...] = r.mixed[...].astype(BF16)

    for name in ("m_small", "m_in", "m_out", "m_exp", "m_red"):
        loads[name].wait()
    total = chips_finish(r.right_in_slots, 4)
    r.right_in_total[seq] = jnp.concatenate(
        [total[0:RANK], total[RANK : 2 * RANK, 0 : own_lanes - width]], axis=1
    )
    share = to_partner(r.right_in_total.at[seq], r.right_in_total.at[seq], 7)
    share.start()
    right_share = units_share(r.rights_node, r.rights_total, 3, 12)

    def small_update(at, grad):
        momentum = DECAY * r.mom_small[at, :] + grad * inverse
        r.mom_small[at, :] = momentum
        r.new_small[at, :] = r.new_small[at, :] - RATE * momentum

    small_update(slice(4, 12), r.lefts_total[6])
    share.wait()
    r.new_f_in[:, 0:own_lanes] = r.right_in_total[0] * inverse
    r.new_f_in[:, own_lanes : 3 * width] = (
        r.right_in_total[1][:, 2 * own_lanes - 3 * width : own_lanes] * inverse
    )
    right_share.wait()
    for part in range(4):
        r.new_f_exp[:, part * width : (part + 1) * width] = r.rights_total[part] * inverse
    r.new_f_red[...] = r.rights_total[4] * inverse
    r.new_f_out[...] = r.rights_total[5] * inverse
    small_update(slice(0, 4), r.rights_total[6][0:4])


def store_kernel(names, targets, *all_refs):
    refs = Names()
    for name, ref in zip(names, all_refs):
        setattr(refs, name, ref)
    waits = []

    def send(name, at=None):
        source, target = getattr(refs, "next_" + name, None), getattr(refs, "hbm_" + name)
        if source is None:
            source = getattr(refs, name)
        if len(target.shape) > len(source.shape):
            target = target.at[0]
        sem = refs.sem.at[targets.index(name)]
        if at is None or at.start == 0:
            waits.append(pltpu.make_async_copy(source, target, sem))
        if at is not None:
            at = pl.ds(at.start, at.stop - at.start)
            source, target = source.at[at], target.at[at]
        pltpu.make_async_copy(source, target, sem).start()

    updated = {kind + which for kind in KINDS for which in MATRICES}
    for name in targets:
        if name not in updated:
            send(name)
    for which, rows in (("exp", 128), ("red", 384), ("out", 384), ("in", 128)):
        weight, momentum, error = (getattr(refs, kind + which) for kind in KINDS)
        new_weight, new_momentum, new_error = (getattr(refs, "next_" + kind + which) for kind in KINDS)
        left_stack, right_stack = outer_product(
            getattr(refs, "basis_" + which)[...], getattr(refs, "new_f_" + which)[...]
        )
        for strip in range(weight.shape[0] // rows):
            at = slice(strip * rows, (strip + 1) * rows)
            approx = mm_tn(left_stack[:, at], right_stack)
            new_error[at, :] = error[at, :] - approx
            send("err_" + which, at)
            next_momentum = DECAY * momentum[at, :] + approx
            new_momentum[at, :] = next_momentum
            send("mom_" + which, at)
            new_weight[at, :] = weight[at, :] - RATE * next_momentum
            send("new_" + which, at)
    for copy in waits:
        copy.wait()


def body(chips, groups, *args):
    args = list(args)
    for index in (0, 2):
        args[index] = jnp.transpose(args[index], (1, 0, 2))
    half, images, width = args[0].shape
    wide = args[8].shape[1]
    special = round_up(half, 8)
    block = round_up(special + 2, 16)
    rows = images * block
    out_shapes = [((half, images, width), BF16), ((images, 2, width), BF16)] * 2
    weight_shapes = [(width, 3 * width), (width, width), (width, wide), (wide, width)]
    small_shape = (args[10].shape, F32)
    out_shapes += [(shape, F32) for shape in weight_shapes] + [small_shape]
    out_shapes += [(shape, F32) for shape in weight_shapes] + [small_shape]
    out_shapes += [(shape, F32) for shape in weight_shapes]
    out_shapes += [((RANK, size), F32) for size in (3 * width, width, wide, width)]
    unit = (RANK, width)
    own_lanes = round_up(3 * width // 2, 128)
    scratch = dict(
        raw_patch=pltpu.VMEM((half, images, width), BF16),
        raw_special=pltpu.VMEM((images, 2, width), BF16),
        raw_up=pltpu.VMEM((half, images, width), BF16),
        raw_special_up=pltpu.VMEM((images, 2, width), BF16),
        mixed=pltpu.VMEM((half, images, width), F32),
        rank=pltpu.VMEM((images, half), jnp.int32),
        count=pltpu.SMEM((images,), jnp.int32),
        folded=pltpu.VMEM((rows, 2 * RANK), F32),
        folded_red=pltpu.VMEM((RANK, rows), BF16),
        low_probs=pltpu.VMEM((HEADS, 2 * KEYS, 2 * block), BF16),
        branch_sum=pltpu.VMEM((1, width), F32),
        flags=pltpu.VMEM((8, KEYS), F32),
        other_flags=pltpu.VMEM((8, KEYS), F32),
        mask_columns=pltpu.VMEM((images, 2 * KEYS, 1), F32),
        tokens=pltpu.VMEM((rows, width), F32),
        xhat_one=pltpu.VMEM((rows, width), F32),
        xhat_two=pltpu.VMEM((rows, width), F32),
        scale_one=pltpu.VMEM((rows, 1), F32),
        scale_two=pltpu.VMEM((rows, 1), F32),
        hidden_one=pltpu.VMEM((rows, width), BF16),
        hidden_two=pltpu.VMEM((rows, width), BF16),
        low_in=pltpu.VMEM((width + 2 * RANK, 3 * width), BF16),
        low_out=pltpu.VMEM((width + 2 * RANK, width), BF16),
        low_exp=pltpu.VMEM((width + 2 * RANK, wide), BF16),
        low_red=pltpu.VMEM((wide, width), BF16),
        query=pltpu.VMEM((rows, width), BF16),
        keys=pltpu.VMEM((2, images, KEYS, 2 * width), BF16),
        upstream=pltpu.VMEM((rows, width), BF16),
        probs=pltpu.VMEM((images * HEADS // 2, 2 * KEYS, 2 * block), F32),
        attended=pltpu.VMEM((rows, width), BF16),
        middle=pltpu.VMEM((rows, width), F32),
        wide=pltpu.VMEM((2, rows, 256), F32),
        activated=pltpu.VMEM((rows, wide), BF16),
        slope=pltpu.VMEM((rows, wide), F32),
        grad_pre=pltpu.VMEM((rows, wide), BF16),
        total=pltpu.VMEM((rows, width), F32),
        gain_sum=pltpu.VMEM((1, width), F32),
        shift_sum=pltpu.VMEM((1, width), F32),
        grad_branch=pltpu.VMEM((rows, width), BF16),
        grad_attended=pltpu.VMEM((rows, width), BF16),
        grad_own=pltpu.VMEM((images, KEYS, 2 * width), F32),
        grad_sent=pltpu.VMEM((images, KEYS, 2 * width), F32),
        grad_arrived=pltpu.VMEM((images, KEYS, 2 * width), F32),
        grad_qkv=pltpu.VMEM((rows, 3 * width), BF16),
        lefts=pltpu.VMEM((8,) + unit, F32),
        lefts_arrived=pltpu.VMEM((8,) + unit, F32),
        lefts_out=pltpu.VMEM((2, 2, 2 * RANK, width), BF16),
        lefts_group=pltpu.VMEM((groups, 2, 2 * RANK, width), BF16),
        lefts_node=pltpu.VMEM((chips // groups, 2, 2 * RANK, width), BF16),
        lefts_total=pltpu.VMEM((8,) + unit, F32),
        rights=pltpu.VMEM((8,) + unit, F32),
        rights_arrived=pltpu.VMEM((8,) + unit, F32),
        rights_out=pltpu.VMEM((2, 2, 2 * RANK, width), BF16),
        rights_group=pltpu.VMEM((groups, 2, 2 * RANK, width), BF16),
        rights_node=pltpu.VMEM((chips // groups, 2, 2 * RANK, width), BF16),
        rights_total=pltpu.VMEM((8,) + unit, F32),
        left_in=pltpu.VMEM(unit, F32),
        left_in_arrived=pltpu.VMEM(unit, F32),
        left_in_out=pltpu.VMEM((2 * RANK, 256), BF16),
        left_in_slots=pltpu.VMEM((chips, 2 * RANK, 256), BF16),
        cross_arrived=pltpu.VMEM((width, own_lanes), BF16),
        right_in_out=pltpu.VMEM((2 * RANK, width), BF16),
        right_in_slots=pltpu.VMEM((chips, 2 * RANK, width), BF16),
        right_in_total=pltpu.VMEM((2, RANK, own_lanes), F32),
        late_rows=pltpu.VMEM(unit, F32),
        load_sem=pltpu.SemaphoreType.DMA((17,)),
        pair_send=pltpu.SemaphoreType.DMA((15,)),
        pair_recv=pltpu.SemaphoreType.DMA((15,)),
        stage_send=pltpu.SemaphoreType.DMA((6,)),
        stage_recv=pltpu.SemaphoreType.DMA((6,)),
    )
    made = OUTPUTS + BASES
    made_shapes = out_shapes + [((RANK, size), F32) for size in (width, width, width, wide)]
    names = INPUTS + made + tuple(scratch)
    in_hbm = pl.BlockSpec(memory_space=pltpu.HBM)
    in_vmem = pl.BlockSpec(memory_space=pltpu.VMEM)
    results = pl.pallas_call(
        functools.partial(layer_kernel, chips, groups, images, half, names),
        out_shape=[pltpu.VMEM(shape, dtype) for shape, dtype in made_shapes],
        in_specs=[in_hbm] * len(INPUTS),
        out_specs=[in_vmem] * len(made),
        scratch_shapes=list(scratch.values()),
        compiler_params=pltpu.CompilerParams(
            collective_id=0, has_side_effects=True, vmem_limit_bytes=40 << 20
        ),
        name="layer",
    )(*args[:20], *[jnp.transpose(factor) for factor in args[20:]])
    final_shapes = [
        jax.ShapeDtypeStruct((1,) + shape if 14 <= index < 18 else shape, dtype)
        for index, (shape, dtype) in enumerate(out_shapes)
    ]
    updated = {
        "next_" + kind + which: shape
        for index, kind in enumerate(KINDS)
        for which, shape in zip(MATRICES, weight_shapes)
    }
    stored = list(
        pl.pallas_call(
            functools.partial(
                store_kernel,
                made + tuple("hbm_" + name for name in OUTPUTS) + tuple(updated) + ("sem",),
                OUTPUTS,
            ),
            out_shape=final_shapes,
            in_specs=[in_vmem] * len(made),
            out_specs=[in_hbm] * len(OUTPUTS),
            scratch_shapes=[pltpu.VMEM(shape, F32) for shape in updated.values()]
            + [pltpu.SemaphoreType.DMA((len(OUTPUTS),))],
            compiler_params=pltpu.CompilerParams(vmem_limit_bytes=24 << 20),
            name="store",
        )(*results)
    )
    for index in (0, 2):
        stored[index] = jnp.transpose(stored[index], (1, 0, 2))
    return (*stored[:18], *[jnp.transpose(factor) for factor in stored[18:]])


def solution(mesh):
    images_over = ("node", "group")
    rows_spec = P(images_over, "seq", None)
    special_spec = P(images_over, None, None)
    worker_spec = P(("seq", "node", "group"), None, None)
    whole = P()
    placed = (
        (rows_spec, special_spec) * 2
        + (P(images_over, "seq"), P(images_over))
        + (whole,) * 10
        + (worker_spec,) * 4
        + (whole,) * 4
    )
    groups = mesh.shape["group"]
    chips = mesh.shape["node"] * groups
    return jax.shard_map(
        functools.partial(body, chips, groups),
        mesh=mesh,
        in_specs=placed,
        out_specs=(rows_spec, special_spec) * 2
        + (whole,) * 10
        + (worker_spec,) * 4
        + (whole,) * 4,
        check_vma=False,
    )
```

```python
import functools
import math

import jax
import jax.numpy as jnp
from jax import lax
from jax.experimental import pallas as pl
from jax.experimental.pallas import tpu as pltpu
from jax.sharding import PartitionSpec as P

HEADS = 6
HEAD_DIM = 64
EPSILON = 1e-06
RATE = 0.1
DECAY = 0.9
RANK = 8
MESH = pl.DeviceIdType.MESH
F32 = jnp.float32
BF16 = jnp.bfloat16
INPUTS = (
    "patch_tokens",
    "special_tokens",
    "patch_upstream",
    "special_upstream",
    "patch_rank",
    "keep_count",
    "project_in",
    "project_out",
    "expand_weight",
    "reduce_weight",
    "small_params",
    "project_in_momentum",
    "project_out_momentum",
    "expand_momentum",
    "reduce_momentum",
    "small_momentum",
    "project_in_error",
    "project_out_error",
    "expand_error",
    "reduce_error",
    "project_in_factor",
    "project_out_factor",
    "expand_factor",
    "reduce_factor",
)
OUTPUTS = (
    "out_patch",
    "out_special",
    "grad_patch",
    "grad_special",
    "new_in",
    "new_out",
    "new_exp",
    "new_red",
    "new_small",
    "mom_in",
    "mom_out",
    "mom_exp",
    "mom_red",
    "mom_small",
    "err_in",
    "err_out",
    "err_exp",
    "err_red",
    "new_f_in",
    "new_f_out",
    "new_f_exp",
    "new_f_red",
)
BASES = ("basis_in", "basis_out", "basis_exp", "basis_red")
KINDS = ("new_", "mom_", "err_")
MATRICES = ("in", "out", "exp", "red")
KEYS = 128


def round_up(value, unit):
    return -(-value // unit) * unit


def mm(left_side, right_side):
    return jnp.dot(left_side, right_side, preferred_element_type=F32)


def mm_nt(left_side, right_side):
    return lax.dot_general(
        left_side, right_side, (((1,), (1,)), ((), ())), preferred_element_type=F32
    )


def mm_tn(left_side, right_side):
    return lax.dot_general(
        left_side, right_side, (((0,), (0,)), ((), ())), preferred_element_type=F32
    )


def split(value):
    high = value.astype(BF16)
    return high, (value - high.astype(F32)).astype(BF16)


def orthonormal(rows):
    row_ids = lax.broadcasted_iota(jnp.int32, (RANK, 1), 0)
    for step in range(RANK):
        own = rows[step : step + 1, :]
        dots = jnp.sum(rows * own, axis=1, keepdims=True)
        scale = lax.rsqrt(dots[step : step + 1, :] + EPSILON)
        unit = own * scale
        later = jnp.where(row_ids > step, dots * scale, 0.0)
        rows = jnp.where(row_ids == step, unit, rows - later * unit)
    return rows


def outer_product(basis, right):
    basis_high, basis_low = split(basis)
    right_high, right_low = split(right)
    left_stack = jnp.concatenate(
        [basis_high.astype(F32), basis_low.astype(F32)] * 2, axis=0
    ).astype(BF16)
    right_stack = jnp.concatenate(
        [right_high.astype(F32)] * 2 + [right_low.astype(F32)] * 2, axis=0
    ).astype(BF16)
    return left_stack, right_stack


class Names:
    pass


def layer_kernel(chips, groups, images, half, names, *all_refs):
    refs = Names()
    for name, ref in zip(names, all_refs):
        setattr(refs, name, ref)
    r = refs
    r.grad_middle, r.grad_query = r.tokens, r.middle
    width = HEADS * HEAD_DIM
    special = round_up(half, 8)
    block = round_up(special + 2, 16)
    rows_all = images * block
    workers = 2 * chips
    seq = lax.axis_index("seq")
    node = lax.axis_index("node")
    group = lax.axis_index("group")
    chip = node * groups + group
    partner = 1 - seq

    loads = {}
    free_sems = list(range(r.load_sem.shape[0]))

    class Load:
        def __init__(self, source, target):
            self.sem_id = free_sems.pop(0)
            self.copy = pltpu.make_async_copy(source, target, r.load_sem.at[self.sem_id])
            self.copy.start()

        def wait(self):
            self.copy.wait()
            free_sems.append(self.sem_id)

    def load(name, source, target):
        loads[name] = Load(source, target)

    load("tokens", r.patch_tokens, r.raw_patch)
    load("special", r.special_tokens, r.raw_special)
    load("rank", r.patch_rank, r.rank)
    load("count", r.keep_count, r.count)
    load("small", r.small_params, r.new_small)
    for name, lanes in (("w_keys", pl.ds(width, 2 * width)), ("w_query", pl.ds(0, width))):
        load(name, r.project_in.at[:, lanes], r.new_in.at[:, lanes])

    load("f_in", r.project_in_factor, r.new_f_in)
    load("f_out", r.project_out_factor, r.new_f_out)
    load("f_exp", r.expand_factor, r.new_f_exp)
    load("f_red", r.reduce_factor, r.new_f_red)
    load("upstream", r.patch_upstream, r.raw_up)
    load("special_up", r.special_upstream, r.raw_special_up)
    load("e_in", r.project_in_error.at[0], r.err_in)
    load("e_exp", r.expand_error.at[0], r.err_exp)
    load("e_red", r.reduce_error.at[0], r.err_red)
    load("e_out", r.project_out_error.at[0], r.err_out)

    def load_third():
        load("w_out", r.project_out, r.new_out)
        load("w_exp", r.expand_weight, r.new_exp)
        load("w_red", r.reduce_weight, r.new_red)

    def load_last():
        load("m_small", r.small_momentum, r.mom_small)
        load("m_out", r.project_out_momentum, r.mom_out)
        load("m_exp", r.expand_momentum, r.mom_exp)
        load("m_red", r.reduce_momentum, r.mom_red)
        load("m_in", r.project_in_momentum, r.mom_in)

    barrier = pltpu.get_barrier_semaphore()
    pl.semaphore_signal(barrier, inc=1, device_id={"seq": partner}, device_id_type=MESH)

    nodes = chips // groups

    def each_chip(act):
        def row(step, first):
            for ahead in range(first, groups):
                act({"node": lax.rem(node + step, nodes), "group": lax.rem(group + ahead, groups)})

        def others(step, carry):
            row(step, 0)
            return carry

        lax.fori_loop(1, nodes, others, 0)
        row(0, 1)

    def greet(device):
        pl.semaphore_signal(barrier, inc=1, device_id=device, device_id_type=MESH)

    each_chip(greet)

    def to_partner(source, target, sem_id):
        return pltpu.make_async_remote_copy(
            src_ref=source,
            dst_ref=target,
            send_sem=r.pair_send.at[sem_id],
            recv_sem=r.pair_recv.at[sem_id],
            device_id={"seq": partner},
            device_id_type=MESH,
        )

    def remote(source, target, sem_id, device):
        return pltpu.make_async_remote_copy(
            src_ref=source,
            dst_ref=target,
            send_sem=r.stage_send.at[sem_id],
            recv_sem=r.stage_recv.at[sem_id],
            device_id=device,
            device_id_type=MESH,
        )

    def stage_finish(count, slots, sem_id):
        several = slots.at[pl.ds(0, count - 1)]
        whole = remote(several, several, sem_id, {"seq": partner})
        whole.wait_recv()
        whole.wait_send()
        if count <= 32:
            total = slots[0].astype(F32)
            for index in range(1, count):
                total = total + slots[index].astype(F32)
            return total

        def add(index, total):
            return total + slots[index].astype(F32)

        return lax.fori_loop(1, count, add, slots[0].astype(F32))

    def chips_start(source, slots, sem_id):
        slots[chip] = source[...]
        each_chip(lambda device: remote(source, slots.at[chip], sem_id, device).start())

    def chips_finish(slots, sem_id):
        return stage_finish(chips, slots, sem_id)

    def axis_start(axis, source, slots, sem_id):
        size, place = lax.axis_size(axis), lax.axis_index(axis)
        slots[place] = source[...]
        for step in range(1, size):
            device = {axis: lax.rem(place + step, size)}
            remote(source, slots.at[place], sem_id, device).start()

    def axis_finish(axis, slots, sem_id):
        return stage_finish(lax.axis_size(axis), slots, sem_id)

    loads["rank"].wait()
    loads["count"].wait()
    r.flags[...] = jnp.zeros_like(r.flags)
    for i in range(images):
        r.flags[i : i + 1, 0:half] = jnp.where(
            r.rank[i : i + 1, :] < r.count[i], 1.0, 0.0
        ).astype(F32)
    lane_ids = lax.broadcasted_iota(jnp.int32, (1, KEYS), 1)
    special_lanes = jnp.where((lane_ids >= special) & (lane_ids < special + 2), 1.0, 0.0)
    own_columns = jnp.transpose(r.flags[...] + special_lanes)
    for i in range(images):
        r.mask_columns[i, 0:KEYS, :] = own_columns[:, i : i + 1]

    small = r.new_small
    loads["small"].wait()

    def small_row(index):
        return small[index : index + 1, :]

    loads["tokens"].wait()
    loads["special"].wait()
    r.mixed[...] = r.raw_patch[...].astype(F32)
    for i in range(images):
        base = i * block
        r.tokens[base + special - 8 : base + block, :] = jnp.zeros(
            (block - special + 8, width), F32
        )
        r.tokens[base : base + half, :] = (
            r.mixed[:, i, :] * r.mask_columns[i, 0:half, :]
        )
        r.tokens[base + special : base + special + 2, :] = r.raw_special[i].astype(F32)

    def normalise(source, i, gain, shift, xhat_ref, scale_ref, hidden_ref):
        at = pl.ds(pl.multiple_of(i * block, 16), block)
        values = source[at, :]
        center = values - jnp.mean(values, axis=1, keepdims=True)
        spread = jnp.mean(center * center, axis=1, keepdims=True)
        scale = lax.rsqrt(spread + EPSILON)
        xhat = center * scale
        xhat_ref[at, :] = xhat
        scale_ref[at, :] = scale
        hidden_ref[at, :] = (xhat * gain + shift).astype(BF16)

    @pl.loop(0, images)
    def _(i):
        normalise(r.tokens, i, small_row(0), small_row(1), r.xhat_one, r.scale_one, r.hidden_one)

    loads["w_keys"].wait()
    r.low_in[0:width, width : 3 * width] = r.new_in[:, width : 3 * width].astype(BF16)
    for i in range(images):
        r.keys[0, i, block:KEYS, :] = jnp.zeros((KEYS - block, 2 * width), BF16)
    product = mm(r.hidden_one[...], r.low_in[0:width, width : 3 * width])
    for i in range(images):
        at = slice(i * block, (i + 1) * block)
        r.keys[0, i, 0:block, 0:width] = product[at, 0:width].astype(BF16)
        r.keys[0, i, 0:block, width : 2 * width] = (
            product[at, width : 2 * width] + small_row(3)
        ).astype(BF16)
    pl.semaphore_wait(barrier, chips)
    key_copy = to_partner(r.keys.at[0], r.keys.at[1], 0)
    flag_copy = to_partner(r.flags, r.other_flags, 1)
    key_copy.start()
    flag_copy.start()
    loads["w_query"].wait()
    r.low_in[0:width, 0:width] = r.new_in[:, 0:width].astype(BF16)
    product = mm(r.hidden_one[...], r.low_in[0:width, 0:width])
    query = (product + small_row(2)).astype(BF16).astype(F32) * (1.0 / math.sqrt(HEAD_DIM))
    r.query[...] = query.astype(BF16)

    def error_left(error_ref, factor_ref, row_start, row_count):
        return mm_nt(
            factor_ref[...].astype(BF16), error_ref[row_start : row_start + row_count, :].astype(BF16)
        )

    loads["upstream"].wait()
    loads["special_up"].wait()
    r.mixed[...] = r.raw_up[...].astype(F32)
    for i in range(images):
        base = i * block
        r.middle[base + special - 8 : base + block, :] = jnp.zeros(
            (block - special + 8, width), F32
        )
        r.middle[base : base + half, :] = r.mixed[:, i, :]
        r.middle[base + special : base + special + 2, :] = 0.5 * r.raw_special_up[i].astype(F32)
    r.lefts[6, 3:4, :] = jnp.sum(r.middle[...], axis=0, keepdims=True)
    r.upstream[...] = r.middle[...].astype(BF16)
    loads["f_in"].wait()
    loads["f_out"].wait()
    loads["f_exp"].wait()
    loads["f_red"].wait()

    def with_factor(low_ref, factor_ref):
        factor = factor_ref[...]
        low_ref[width : width + 2 * RANK, :] = jnp.concatenate(
            [factor, jnp.zeros_like(factor)], axis=0
        ).astype(BF16)

    with_factor(r.low_in, r.new_f_in)
    with_factor(r.low_out, r.new_f_out)
    with_factor(r.low_exp, r.new_f_exp)
    folded_red = mm_nt(r.new_f_red[...].astype(BF16), r.upstream[...])
    r.folded_red[...] = folded_red.astype(BF16)
    loads["e_in"].wait()
    r.left_in[...] = error_left(r.err_in, r.new_f_in, 0, width)
    loads["e_exp"].wait()
    r.lefts[4] = error_left(r.err_exp, r.new_f_exp, 0, width)
    load_third()
    loads["e_red"].wait()
    for part in range(4):
        r.lefts[part] = error_left(r.err_red, r.new_f_red, part * width, width)
    loads["e_out"].wait()
    r.lefts[5] = error_left(r.err_out, r.new_f_out, 0, width)

    key_copy.wait()
    flag_copy.wait()
    other_columns = jnp.transpose(r.other_flags[...])
    for i in range(images):
        r.mask_columns[i, KEYS : 2 * KEYS, :] = other_columns[:, i : i + 1]

    pair_width = 2 * HEAD_DIM
    pairs = HEADS // 2
    low_lanes = lax.broadcasted_iota(jnp.int32, (1, pair_width), 1) < HEAD_DIM

    def stacked(value):
        zero = jnp.zeros_like(value)
        return jnp.concatenate(
            [jnp.where(low_lanes, value, zero), jnp.where(low_lanes, zero, value)], axis=0
        )

    def unstacked(value):
        return jnp.where(low_lanes, value[0:block], value[block : 2 * block])

    def of_both(i, lanes):
        return jnp.concatenate([r.keys[0, i, :, lanes], r.keys[1, i, :, lanes]], axis=0)

    together = 2

    def lanes_of(pair, first=0):
        return slice(first + pair * pair_width, first + (pair + 1) * pair_width)

    def image_rows(i):
        return pl.ds(pl.multiple_of(i * block, 16), block)

    tasks = [(ahead, pair) for ahead in range(together) for pair in range(pairs)]

    @pl.loop(0, images // together)
    def _(step):
        for ahead, pair in tasks:
            i = step * together + ahead
            queries = stacked(r.query[image_rows(i), lanes_of(pair)])
            scores = mm_nt(of_both(i, lanes_of(pair)), queries)
            r.probs[i * pairs + pair] = jnp.where(r.mask_columns[i] > 0.5, scores, -1e30)
        for task, (ahead, pair) in enumerate(tasks):
            i = step * together + ahead
            scores = r.probs[i * pairs + pair]
            top = jnp.max(scores, axis=0, keepdims=True)
            weights = jnp.exp(scores - top)
            probs = weights * (1.0 / jnp.sum(weights, axis=0, keepdims=True))
            r.probs[i * pairs + pair] = probs
            r.low_probs[task] = probs.astype(BF16)
        for task, (ahead, pair) in enumerate(tasks):
            i = step * together + ahead
            mixed = mm_tn(r.low_probs[task], of_both(i, lanes_of(pair, width)))
            r.attended[image_rows(i), lanes_of(pair)] = unstacked(mixed).astype(BF16)

    loads["w_out"].wait()
    load_last()
    r.low_out[0:width, :] = r.new_out[...].astype(BF16)
    r.middle[...] = r.tokens[...] + mm(r.attended[...], r.low_out[0:width, :]) + small_row(4)

    @pl.loop(0, images)
    def _(i):
        normalise(r.middle, i, small_row(5), small_row(6), r.xhat_two, r.scale_two, r.hidden_two)

    strip = 64
    chunk = 2 * width
    hidden_lanes = r.low_exp.shape[1]
    loads["w_exp"].wait()
    r.low_exp[0:width, :] = r.new_exp[...].astype(BF16)
    loads["w_red"].wait()
    r.low_red[...] = r.new_red[...].astype(BF16)
    bias_rows = chunk // width
    part_lanes = r.wide.shape[2]
    parts = hidden_lanes // part_lanes
    bias_one = jnp.concatenate([small_row(8 + index) for index in range(hidden_lanes // width)], axis=1)
    r.total[...] = r.middle[...] + small_row(7)

    def lanes_at(part, count=1):
        return slice(part * part_lanes, (part + count) * part_lanes)

    def expand(part):
        r.wide[part % 2] = mm(r.hidden_two[...], r.low_exp[0:width, lanes_at(part)])

    def activate(part):
        for index in range(rows_all // strip):
            at = slice(index * strip, (index + 1) * strip)
            pre = r.wide[part % 2, at, :] + bias_one[:, lanes_at(part)]
            normal = 0.5 + 0.5 * lax.erf(pre * (1.0 / math.sqrt(2.0)))
            density = jnp.exp(-0.5 * pre * pre) * (1.0 / math.sqrt(2.0 * math.pi))
            r.activated[at, lanes_at(part)] = (pre * normal).astype(BF16)
            r.slope[at, lanes_at(part)] = normal + pre * density

    def contract(part):
        lanes = lanes_at(part, 2)
        r.total[...] += mm(r.activated[:, lanes], r.low_red[lanes, :])

    expand(0)
    for part in range(parts):
        if part + 1 < parts:
            expand(part + 1)
        activate(part)
        if part >= 2 and part % 2 == 0:
            contract(part - 2)
    contract(parts - 2)
    for i in range(images):
        base = i * block
        r.mixed[:, i, :] = r.total[base : base + half, :]
        r.out_special[i] = r.total[base + special : base + special + 2, :].astype(BF16)

    r.out_patch[...] = r.mixed[...].astype(BF16)

    def units_pair_start(units, arrived, sem_id):
        copy = to_partner(units, arrived, sem_id)
        copy.start()
        return copy

    def units_group_start(copy, units, arrived, outgoing, slots, sem_id):
        copy.wait()
        for index in range(2):
            first = seq * 4 + 2 * index
            outgoing[0, index] = jnp.concatenate(
                [units[first] + arrived[first], units[first + 1] + arrived[first + 1]], axis=0
            ).astype(BF16)
        axis_start("group", outgoing.at[0], slots, sem_id)

    def units_node_start(outgoing, group_slots, node_slots, sem_id):
        total = axis_finish("group", group_slots, sem_id)
        outgoing[1] = total.astype(BF16)
        axis_start("node", outgoing.at[1], node_slots, sem_id + 1)

    def units_share(node_slots, result, sem_id, pair_id):
        total = axis_finish("node", node_slots, sem_id)
        for index in range(2):
            first = seq * 4 + 2 * index
            result[first] = total[index, 0:RANK]
            result[first + 1] = total[index, RANK : 2 * RANK]
        half_units = result.at[pl.ds(seq * 4, 4)]
        copy = to_partner(half_units, half_units, pair_id)
        copy.start()
        return copy

    for part in range(4):
        lanes = slice(part * width, (part + 1) * width)
        r.lefts[part] += mm(r.folded_red[...], r.activated[:, lanes])
    for part in range(hidden_lanes // chunk):
        lanes = slice(part * chunk, (part + 1) * chunk)
        grad_act = mm_nt(r.upstream[...], r.low_red[lanes, :]).astype(BF16).astype(F32)
        grad_pre = grad_act * r.slope[:, lanes]
        r.grad_pre[:, lanes] = grad_pre.astype(BF16)
        row = jnp.sum(grad_pre, axis=0, keepdims=True)
        for index in range(bias_rows):
            first = 4 + part * bias_rows + index
            r.lefts[6, first : first + 1, :] = row[:, index * width : (index + 1) * width]
        back = mm_nt(r.grad_pre[:, lanes], r.low_exp[:, lanes])
        if part == 0:
            r.total[...] = back[:, 0:width]
            r.folded[...] = back[:, width : width + 2 * RANK]
        else:
            r.total[...] += back[:, 0:width]
            r.folded[...] += back[:, width : width + 2 * RANK]

    def left_of(hidden_ref):
        return mm_tn(r.folded[...].astype(BF16), hidden_ref[...])[0:RANK]

    r.lefts[4] += left_of(r.hidden_two)

    def normalise_back(i, gain, xhat_ref, scale_ref, gain_ref, shift_ref):
        at = pl.ds(pl.multiple_of(i * block, 16), block)
        grad = r.total[at, :]
        xhat = xhat_ref[at, :]
        gained = grad * gain
        first = jnp.mean(gained, axis=1, keepdims=True)
        second = jnp.mean(gained * xhat, axis=1, keepdims=True)
        gain_ref[...] += jnp.sum(grad * xhat, axis=0, keepdims=True)
        shift_ref[...] += jnp.sum(grad, axis=0, keepdims=True)
        return scale_ref[at, :] * (gained - first - xhat * second)

    r.gain_sum[...] = jnp.zeros_like(r.gain_sum)
    r.shift_sum[...] = jnp.zeros_like(r.shift_sum)
    r.branch_sum[...] = jnp.zeros_like(r.branch_sum)

    @pl.loop(0, images)
    def _(i):
        at = pl.ds(pl.multiple_of(i * block, 16), block)
        back = normalise_back(i, small_row(5), r.xhat_two, r.scale_two, r.gain_sum, r.shift_sum)
        grad = r.upstream[at, :].astype(F32) + back
        r.grad_middle[at, :] = grad
        low = grad.astype(BF16)
        r.grad_branch[at, :] = low
        r.branch_sum[...] += jnp.sum(low.astype(F32), axis=0, keepdims=True)

    r.lefts[6, 1:2, :] = r.gain_sum[...]
    r.lefts[6, 2:3, :] = r.shift_sum[...]
    r.lefts[6, 0:1, :] = r.branch_sum[...]
    r.lefts[7] = jnp.zeros((RANK, width), F32)
    back = mm_nt(r.grad_branch[...], r.low_out[...])
    r.grad_attended[...] = back[:, 0:width].astype(BF16)
    r.folded[...] = back[:, width : width + 2 * RANK]
    r.lefts[5] += left_of(r.attended)

    left_copy = units_pair_start(r.lefts, r.lefts_arrived, 2)

    def grad_copy(i):
        return to_partner(r.grad_sent.at[i], r.grad_arrived.at[i], 8 + i)

    def scratch_at(task):
        return slice(0, 2 * KEYS), slice(task * 2 * KEYS, task * 2 * KEYS + 2 * block)

    def special_rows(i):
        return pl.ds(pl.multiple_of(i * block + special, 8), 2)

    def reduce_gradient(part):
        lanes = slice(part * chunk, (part + 1) * chunk)
        r.err_red[lanes, :] += mm_tn(r.activated[:, lanes], r.upstream[...])

    def expand_gradient(part):
        lanes = slice(part * chunk, (part + 1) * chunk)
        r.err_exp[:, lanes] += mm_tn(r.hidden_two[...], r.grad_pre[:, lanes])

    r.err_out[...] += mm_tn(r.attended[...], r.grad_branch[...])
    reduce_gradient(0)
    units_group_start(left_copy, r.lefts, r.lefts_arrived, r.lefts_out, r.lefts_group, 0)

    @pl.loop(0, images // together)
    def _(step):
        for task, (ahead, pair) in enumerate(tasks):
            i = step * together + ahead
            grad_mixed = stacked(r.grad_attended[image_rows(i), lanes_of(pair)])
            r.slope[scratch_at(task)] = mm_nt(of_both(i, lanes_of(pair, width)), grad_mixed)
        for task, (ahead, pair) in enumerate(tasks):
            i = step * together + ahead
            probs = r.probs[i * pairs + pair]
            weighted = probs * r.slope[scratch_at(task)]
            delta = jnp.sum(weighted, axis=0, keepdims=True)
            r.low_probs[task] = (weighted - probs * delta).astype(BF16)
        for ahead in range(together):
            i = step * together + ahead
            at = image_rows(i)
            for pair in range(pairs):
                grad_scores = r.low_probs[ahead * pairs + pair]
                r.grad_query[at, lanes_of(pair)] = unstacked(
                    mm_tn(grad_scores, of_both(i, lanes_of(pair)))
                ) * (1.0 / math.sqrt(HEAD_DIM))
                grad_keys = mm(grad_scores, stacked(r.query[at, lanes_of(pair)]))
                r.grad_own[i, :, lanes_of(pair)] = grad_keys[0:KEYS]
                r.grad_sent[i, :, lanes_of(pair)] = grad_keys[KEYS : 2 * KEYS]
            for pair in range(pairs):
                grad_mixed = stacked(r.grad_attended[at, lanes_of(pair)])
                grad_values = mm(r.probs[i * pairs + pair].astype(BF16), grad_mixed)
                r.grad_own[i, :, lanes_of(pair, width)] = grad_values[0:KEYS]
                r.grad_sent[i, :, lanes_of(pair, width)] = grad_values[KEYS : 2 * KEYS]
            r.grad_sent[i, special : special + 2, :] = r.grad_own[i, special : special + 2, :]
            r.grad_sent[i, block : block + 2, 0:width] = r.grad_query[special_rows(i), :]
            grad_copy(i).start()

    row_ids = lax.broadcasted_iota(jnp.int32, (block, 1), 0)
    halved = jnp.where((row_ids >= special) & (row_ids < special + 2), 0.5, 1.0)
    r.late_rows[...] = jnp.zeros_like(r.late_rows)
    for part in range(1, hidden_lanes // chunk):
        reduce_gradient(part)
    expand_gradient(0)

    @pl.loop(0, images)
    def _(i):
        grad_copy(i).wait()
        base = pl.multiple_of(i * block, 16)
        at = pl.ds(base, block)
        specials = pl.ds(pl.multiple_of(base + special, 8), 2)
        r.grad_query[specials, :] += r.grad_arrived[i, block : block + 2, 0:width]
        query_part = r.grad_query[at, :].astype(BF16).astype(F32) * halved
        r.grad_qkv[at, 0:width] = query_part.astype(BF16)
        r.late_rows[2:3, :] += jnp.sum(query_part, axis=0, keepdims=True)
        rest = (r.grad_own[i, 0:block, :] + r.grad_arrived[i, 0:block, :]).astype(BF16)
        rest = rest.astype(F32) * halved
        r.late_rows[3:4, :] += jnp.sum(rest[:, width : 2 * width], axis=0, keepdims=True)
        r.grad_qkv[at, width : 3 * width] = rest.astype(BF16)

    units_node_start(r.lefts_out, r.lefts_group, r.lefts_node, 0)

    r.folded[...] = mm_nt(r.grad_qkv[...], r.low_in[width : width + 2 * RANK, :])
    r.left_in[...] += left_of(r.hidden_one)
    left_in_copy = to_partner(r.left_in, r.left_in_arrived, 4)
    left_in_copy.start()
    r.total[...] = mm_nt(r.grad_qkv[...], r.low_in[0:width, :])
    left_in_copy.wait()
    pair_sum = r.left_in[...] + r.left_in_arrived[...]
    r.left_in_out[...] = jnp.concatenate(
        [pair_sum[:, 0:256], jnp.concatenate([pair_sum[:, 256:384], jnp.zeros((RANK, 128), F32)], axis=1)],
        axis=0,
    ).astype(BF16)
    chips_start(r.left_in_out, r.left_in_slots, 5)

    for part in range(1, hidden_lanes // chunk):
        expand_gradient(part)
    r.gain_sum[...] = jnp.zeros_like(r.gain_sum)
    r.shift_sum[...] = jnp.zeros_like(r.shift_sum)

    @pl.loop(0, images)
    def _(i):
        at = pl.ds(pl.multiple_of(i * block, 16), block)
        back = normalise_back(i, small_row(0), r.xhat_one, r.scale_one, r.gain_sum, r.shift_sum)
        r.total[at, :] = (back + r.grad_middle[at, :]) * jnp.where(halved < 1.0, 2.0, 1.0)

    r.late_rows[0:1, :] = r.gain_sum[...]
    r.late_rows[1:2, :] = r.shift_sum[...]
    left_share = units_share(r.lefts_node, r.lefts_total, 1, 3)
    for part in range(3):
        lanes = slice(part * width, (part + 1) * width)
        r.err_in[:, lanes] += mm_tn(r.hidden_one[...], r.grad_qkv[:, lanes])
    own_lanes = r.cross_arrived.shape[1]
    apart = 3 * width - own_lanes
    cross_sent = r.low_exp.at[pl.ds(0, width), pl.ds(0, own_lanes)]
    cross_own = r.low_exp.at[pl.ds(0, width), pl.ds(own_lanes, own_lanes)]
    cross_sent[...] = r.err_in[:, pl.ds(pl.multiple_of(partner * apart, 128), own_lanes)].astype(
        BF16
    )
    cross_copy = to_partner(cross_sent, r.cross_arrived, 6)
    cross_copy.start()
    left_share.wait()
    inverse = 1.0 / workers
    basis_red = orthonormal(
        jnp.concatenate([r.lefts_total[part] for part in range(4)], axis=1) * inverse
    )
    basis_exp = orthonormal(r.lefts_total[4] * inverse)
    basis_out = orthonormal(r.lefts_total[5] * inverse)
    r.basis_red[...] = basis_red
    r.basis_exp[...] = basis_exp
    r.basis_out[...] = basis_out

    def right_of(basis, merged):
        both = jnp.concatenate([basis, basis - basis.astype(BF16).astype(F32)], axis=0).astype(BF16)
        product = mm(both, merged.astype(BF16))
        return product[0:RANK] + product[RANK : 2 * RANK]

    for part in range(4):
        lanes = slice(part * width, (part + 1) * width)
        r.rights[part] = right_of(basis_exp, r.err_exp[:, lanes])
    r.rights[4] = right_of(basis_red, r.err_red[...])
    r.rights[5] = right_of(basis_out, r.err_out[...])
    r.rights[6] = r.late_rows[...]
    r.rights[7] = jnp.zeros((RANK, width), F32)
    right_copy = units_pair_start(r.rights, r.rights_arrived, 5)
    units_group_start(right_copy, r.rights, r.rights_arrived, r.rights_out, r.rights_group, 2)
    cross_own[...] = r.err_in[:, pl.ds(pl.multiple_of(seq * apart, 128), own_lanes)].astype(BF16)

    total = chips_finish(r.left_in_slots, 5)
    basis_in = orthonormal(
        jnp.concatenate([total[0:RANK], total[RANK : 2 * RANK, 0:128]], axis=1) * inverse
    )
    r.basis_in[...] = basis_in
    cross_copy.wait()
    part = right_of(basis_in, cross_own[...]) + right_of(basis_in, r.cross_arrived[...])
    rest = jnp.concatenate(
        [part[:, width:own_lanes], jnp.zeros((RANK, 2 * width - own_lanes), F32)], axis=1
    )
    r.right_in_out[...] = jnp.concatenate([part[:, 0:width], rest], axis=0).astype(BF16)
    chips_start(r.right_in_out, r.right_in_slots, 4)
    units_node_start(r.rights_out, r.rights_group, r.rights_node, 2)
    for i in range(images):
        base = i * block
        r.mixed[:, i, :] = r.total[base : base + half, :] * r.mask_columns[i, 0:half, :]
        r.grad_special[i] = r.total[base + special : base + special + 2, :].astype(BF16)
    r.grad_patch[...] = r.mixed[...].astype(BF16)

    for name in ("m_small", "m_in", "m_out", "m_exp", "m_red"):
        loads[name].wait()
    total = chips_finish(r.right_in_slots, 4)
    r.right_in_total[seq] = jnp.concatenate(
        [total[0:RANK], total[RANK : 2 * RANK, 0 : own_lanes - width]], axis=1
    )
    share = to_partner(r.right_in_total.at[seq], r.right_in_total.at[seq], 7)
    share.start()
    right_share = units_share(r.rights_node, r.rights_total, 3, 12)

    def small_update(at, grad):
        momentum = DECAY * r.mom_small[at, :] + grad * inverse
        r.mom_small[at, :] = momentum
        r.new_small[at, :] = r.new_small[at, :] - RATE * momentum

    small_update(slice(4, 12), r.lefts_total[6])
    share.wait()
    r.new_f_in[:, 0:own_lanes] = r.right_in_total[0] * inverse
    r.new_f_in[:, own_lanes : 3 * width] = (
        r.right_in_total[1][:, 2 * own_lanes - 3 * width : own_lanes] * inverse
    )
    right_share.wait()
    for part in range(4):
        r.new_f_exp[:, part * width : (part + 1) * width] = r.rights_total[part] * inverse
    r.new_f_red[...] = r.rights_total[4] * inverse
    r.new_f_out[...] = r.rights_total[5] * inverse
    small_update(slice(0, 4), r.rights_total[6][0:4])


def store_kernel(names, targets, *all_refs):
    refs = Names()
    for name, ref in zip(names, all_refs):
        setattr(refs, name, ref)
    waits = []

    def send(name, at=None):
        source, target = getattr(refs, "next_" + name, None), getattr(refs, "hbm_" + name)
        if source is None:
            source = getattr(refs, name)
        if len(target.shape) > len(source.shape):
            target = target.at[0]
        sem = refs.sem.at[targets.index(name)]
        if at is None or at.start == 0:
            waits.append(pltpu.make_async_copy(source, target, sem))
        if at is not None:
            at = pl.ds(at.start, at.stop - at.start)
            source, target = source.at[at], target.at[at]
        pltpu.make_async_copy(source, target, sem).start()

    updated = {kind + which for kind in KINDS for which in MATRICES}
    for name in targets:
        if name not in updated:
            send(name)
    for which, rows in (("exp", 64), ("in", 64), ("red", 256), ("out", 192)):
        weight, momentum, error = (getattr(refs, kind + which) for kind in KINDS)
        new_weight, new_momentum, new_error = (getattr(refs, "next_" + kind + which) for kind in KINDS)
        left_stack, right_stack = outer_product(
            getattr(refs, "basis_" + which)[...], getattr(refs, "new_f_" + which)[...]
        )
        for strip in range(weight.shape[0] // rows):
            at = slice(strip * rows, (strip + 1) * rows)
            approx = mm_tn(left_stack[:, at], right_stack)
            new_error[at, :] = error[at, :] - approx
            send("err_" + which, at)
            next_momentum = DECAY * momentum[at, :] + approx
            new_momentum[at, :] = next_momentum
            send("mom_" + which, at)
            new_weight[at, :] = weight[at, :] - RATE * next_momentum
            send("new_" + which, at)
    for copy in waits:
        copy.wait()


def body(chips, groups, *args):
    args = list(args)
    for index in (0, 2):
        args[index] = jnp.transpose(args[index], (1, 0, 2))
    half, images, width = args[0].shape
    wide = args[8].shape[1]
    special = round_up(half, 8)
    block = round_up(special + 2, 16)
    rows = images * block
    out_shapes = [((half, images, width), BF16), ((images, 2, width), BF16)] * 2
    weight_shapes = [(width, 3 * width), (width, width), (width, wide), (wide, width)]
    small_shape = (args[10].shape, F32)
    out_shapes += [(shape, F32) for shape in weight_shapes] + [small_shape]
    out_shapes += [(shape, F32) for shape in weight_shapes] + [small_shape]
    out_shapes += [(shape, F32) for shape in weight_shapes]
    out_shapes += [((RANK, size), F32) for size in (3 * width, width, wide, width)]
    unit = (RANK, width)
    own_lanes = round_up(3 * width // 2, 128)
    scratch = dict(
        raw_patch=pltpu.VMEM((half, images, width), BF16),
        raw_special=pltpu.VMEM((images, 2, width), BF16),
        raw_up=pltpu.VMEM((half, images, width), BF16),
        raw_special_up=pltpu.VMEM((images, 2, width), BF16),
        mixed=pltpu.VMEM((half, images, width), F32),
        rank=pltpu.VMEM((images, half), jnp.int32),
        count=pltpu.SMEM((images,), jnp.int32),
        folded=pltpu.VMEM((rows, 2 * RANK), F32),
        folded_red=pltpu.VMEM((RANK, rows), BF16),
        low_probs=pltpu.VMEM((HEADS, 2 * KEYS, 2 * block), BF16),
        branch_sum=pltpu.VMEM((1, width), F32),
        flags=pltpu.VMEM((8, KEYS), F32),
        other_flags=pltpu.VMEM((8, KEYS), F32),
        mask_columns=pltpu.VMEM((images, 2 * KEYS, 1), F32),
        tokens=pltpu.VMEM((rows, width), F32),
        xhat_one=pltpu.VMEM((rows, width), F32),
        xhat_two=pltpu.VMEM((rows, width), F32),
        scale_one=pltpu.VMEM((rows, 1), F32),
        scale_two=pltpu.VMEM((rows, 1), F32),
        hidden_one=pltpu.VMEM((rows, width), BF16),
        hidden_two=pltpu.VMEM((rows, width), BF16),
        low_in=pltpu.VMEM((width + 2 * RANK, 3 * width), BF16),
        low_out=pltpu.VMEM((width + 2 * RANK, width), BF16),
        low_exp=pltpu.VMEM((width + 2 * RANK, wide), BF16),
        low_red=pltpu.VMEM((wide, width), BF16),
        query=pltpu.VMEM((rows, width), BF16),
        keys=pltpu.VMEM((2, images, KEYS, 2 * width), BF16),
        upstream=pltpu.VMEM((rows, width), BF16),
        probs=pltpu.VMEM((images * HEADS // 2, 2 * KEYS, 2 * block), F32),
        attended=pltpu.VMEM((rows, width), BF16),
        middle=pltpu.VMEM((rows, width), F32),
        wide=pltpu.VMEM((2, rows, 256), F32),
        activated=pltpu.VMEM((rows, wide), BF16),
        slope=pltpu.VMEM((rows, wide), F32),
        grad_pre=pltpu.VMEM((rows, wide), BF16),
        total=pltpu.VMEM((rows, width), F32),
        gain_sum=pltpu.VMEM((1, width), F32),
        shift_sum=pltpu.VMEM((1, width), F32),
        grad_branch=pltpu.VMEM((rows, width), BF16),
        grad_attended=pltpu.VMEM((rows, width), BF16),
        grad_own=pltpu.VMEM((images, KEYS, 2 * width), F32),
        grad_sent=pltpu.VMEM((images, KEYS, 2 * width), F32),
        grad_arrived=pltpu.VMEM((images, KEYS, 2 * width), F32),
        grad_qkv=pltpu.VMEM((rows, 3 * width), BF16),
        lefts=pltpu.VMEM((8,) + unit, F32),
        lefts_arrived=pltpu.VMEM((8,) + unit, F32),
        lefts_out=pltpu.VMEM((2, 2, 2 * RANK, width), BF16),
        lefts_group=pltpu.VMEM((groups, 2, 2 * RANK, width), BF16),
        lefts_node=pltpu.VMEM((chips // groups, 2, 2 * RANK, width), BF16),
        lefts_total=pltpu.VMEM((8,) + unit, F32),
        rights=pltpu.VMEM((8,) + unit, F32),
        rights_arrived=pltpu.VMEM((8,) + unit, F32),
        rights_out=pltpu.VMEM((2, 2, 2 * RANK, width), BF16),
        rights_group=pltpu.VMEM((groups, 2, 2 * RANK, width), BF16),
        rights_node=pltpu.VMEM((chips // groups, 2, 2 * RANK, width), BF16),
        rights_total=pltpu.VMEM((8,) + unit, F32),
        left_in=pltpu.VMEM(unit, F32),
        left_in_arrived=pltpu.VMEM(unit, F32),
        left_in_out=pltpu.VMEM((2 * RANK, 256), BF16),
        left_in_slots=pltpu.VMEM((chips, 2 * RANK, 256), BF16),
        cross_arrived=pltpu.VMEM((width, own_lanes), BF16),
        right_in_out=pltpu.VMEM((2 * RANK, width), BF16),
        right_in_slots=pltpu.VMEM((chips, 2 * RANK, width), BF16),
        right_in_total=pltpu.VMEM((2, RANK, own_lanes), F32),
        late_rows=pltpu.VMEM(unit, F32),
        load_sem=pltpu.SemaphoreType.DMA((17,)),
        pair_send=pltpu.SemaphoreType.DMA((13,)),
        pair_recv=pltpu.SemaphoreType.DMA((13,)),
        stage_send=pltpu.SemaphoreType.DMA((6,)),
        stage_recv=pltpu.SemaphoreType.DMA((6,)),
    )
    made = OUTPUTS + BASES
    made_shapes = out_shapes + [((RANK, size), F32) for size in (width, width, width, wide)]
    names = INPUTS + made + tuple(scratch)
    in_hbm = pl.BlockSpec(memory_space=pltpu.HBM)
    in_vmem = pl.BlockSpec(memory_space=pltpu.VMEM)
    results = pl.pallas_call(
        functools.partial(layer_kernel, chips, groups, images, half, names),
        out_shape=[pltpu.VMEM(shape, dtype) for shape, dtype in made_shapes],
        in_specs=[in_hbm] * len(INPUTS),
        out_specs=[in_vmem] * len(made),
        scratch_shapes=list(scratch.values()),
        compiler_params=pltpu.CompilerParams(
            collective_id=0, has_side_effects=True, vmem_limit_bytes=40 << 20
        ),
        name="layer",
    )(*args[:20], *[jnp.transpose(factor) for factor in args[20:]])
    final_shapes = [
        jax.ShapeDtypeStruct((1,) + shape if 14 <= index < 18 else shape, dtype)
        for index, (shape, dtype) in enumerate(out_shapes)
    ]
    updated = {
        "next_" + kind + which: shape
        for index, kind in enumerate(KINDS)
        for which, shape in zip(MATRICES, weight_shapes)
    }
    stored = list(
        pl.pallas_call(
            functools.partial(
                store_kernel,
                made + tuple("hbm_" + name for name in OUTPUTS) + tuple(updated) + ("sem",),
                OUTPUTS,
            ),
            out_shape=final_shapes,
            in_specs=[in_vmem] * len(made),
            out_specs=[in_hbm] * len(OUTPUTS),
            scratch_shapes=[pltpu.VMEM(shape, F32) for shape in updated.values()]
            + [pltpu.SemaphoreType.DMA((len(OUTPUTS),))],
            compiler_params=pltpu.CompilerParams(vmem_limit_bytes=24 << 20),
            name="store",
        )(*results)
    )
    for index in (0, 2):
        stored[index] = jnp.transpose(stored[index], (1, 0, 2))
    return (*stored[:18], *[jnp.transpose(factor) for factor in stored[18:]])


def solution(mesh):
    images_over = ("node", "group")
    rows_spec = P(images_over, "seq", None)
    special_spec = P(images_over, None, None)
    worker_spec = P(("seq", "node", "group"), None, None)
    whole = P()
    placed = (
        (rows_spec, special_spec) * 2
        + (P(images_over, "seq"), P(images_over))
        + (whole,) * 10
        + (worker_spec,) * 4
        + (whole,) * 4
    )
    groups = mesh.shape["group"]
    chips = mesh.shape["node"] * groups
    return jax.shard_map(
        functools.partial(body, chips, groups),
        mesh=mesh,
        in_specs=placed,
        out_specs=(rows_spec, special_spec) * 2
        + (whole,) * 10
        + (worker_spec,) * 4
        + (whole,) * 4,
        check_vma=False,
    )
```
